32 devices in a mesh: groups: 2 (over y), seq: 4 (over z), head: 2 (over x), dp: 2 (over core).
Axes of the slice: x: 2, y: 2, z: 4, core: 2. Of those that a mesh axis runs over, the one named last changes fastest.
Arguments:
- queries: bfloat16 [4, 2048, 512], P(('groups', 'dp'), 'seq', 'head'), parts along dimension 0, may hold values from -6 to 6
- key_rows: bfloat16 [4, 2048, 512], P(('groups', 'dp'), 'seq', 'head'), parts along dimension 0, may hold values from -6 to 6
- value_rows: bfloat16 [4, 2048, 512], P(('groups', 'dp'), 'seq', 'head'), parts along dimension 0, may hold values from -6 to 6
- layout: int32 [4, 8, 4], P('head'), may hold values from 0 to 7
- out_weight: bfloat16 [4096, 512], P(None, 'head'), may hold values from -0.25 to 0.25
- out_grad: bfloat16 [4, 2048, 4096], P(('groups', 'dp'), 'seq', 'head'), parts along dimension 0, may hold values from -6 to 6
Outputs:
- attn: bfloat16 [4, 2048, 512], P(('groups', 'dp'), 'seq', 'head'), parts along dimension 0
- query_grad: bfloat16 [4, 2048, 512], P(('groups', 'dp'), 'seq', 'head'), parts along dimension 0
- key_grad: bfloat16 [4, 2048, 512], P(('groups', 'dp'), 'seq', 'head'), parts along dimension 0
- value_grad: bfloat16 [4, 2048, 512], P(('groups', 'dp'), 'seq', 'head'), parts along dimension 0
- weight_grad: float32 [8192, 512], P(('groups', 'seq', 'dp'), 'head'), parts along dimension 0
The draws below stay inside these ranges and needn't reach their ends.
There are 2 independent parts, one for each index of `groups`. The reference program is written for one: setup_inputs(seed, part) draws one part's arguments, and reference() takes and returns one part's arrays. A program takes and returns all parts, laid end to end along the dimension named above; an argument that names none is the same for every part. Nothing has to cross between parts.
Inputs may be any that keep to these rules, and one draw needn't show every extreme that they name: layout[h, i, j] names a key-value block of the same sequence that query block i of head h reads; entries may repeat and may name any block.
All inputs are finite; a program needn't handle non-finite values.
Results may differ from the reference program's by a relative error of at most 0.018.
Values may be sent and summed in bfloat16 or wider, within the bound.
No kernel may reach another device: no remote copies, remote signals or barrier semaphores. Data moves between devices by JAX's collectives and lax.ppermute only.
A program may use at most 64 MiB of HBM per device.

```python
import math
import jax
import jax.numpy as jnp
import numpy as np
from jax import lax

D = 4096
DH = 128
BLK = 256
NSEL = 4
HEADS = 4
SEQS = 2
L = 2048
NB = 8


def place_ends(drawn, key, least, high):
    longest = drawn.shape.index(max(drawn.shape))
    spots = []
    for shift in (0, 1):
        where = [jax.random.randint(jax.random.fold_in(key, axis), (), 0, length) for axis, length in enumerate(drawn.shape)]
        where[longest] = (where[longest] + shift) % drawn.shape[longest]
        spots.append(tuple(where))
    return drawn.at[spots[0]].set(least).at[spots[1]].set(high)


def with_spikes(entries, own_key, source, target, blocks, factor):
    def block_of(axis_at):
        return (jnp.arange(entries.shape[axis_at]) // (entries.shape[axis_at] // blocks)).reshape((-1,) + (1,) * (entries.ndim - 1 - axis_at))

    one_side = jax.random.permutation(own_key, blocks)[block_of(target)]
    second = (block_of(target) + blocks // 2) % blocks
    return jnp.where((block_of(source) == one_side) | (block_of(source) == second), factor * entries, entries)


def block_scale(own_key, dims, split, smallest, top_value):
    def one(axis_at, parts):
        draws = jax.random.uniform(jax.random.fold_in(jax.random.fold_in(own_key, 6), axis_at), (parts,), jnp.float32, smallest / len(split), top_value / len(split))
        return jnp.repeat(jnp.exp(draws), dims[axis_at] // parts).reshape((-1,) + (1,) * (len(dims) - axis_at - 1))

    level = one(*split[0])
    for cut in split[1:]:
        level = level * one(*cut)
    return level


def cumulative_ranks(count, slope):
    weights = [(1 << 20) // math.isqrt(grade ** slope) + 1 for grade in range(1, count + 1)]
    width = 1 + sum(weights) // (1 << 30)
    return np.cumsum(np.array([max(1, weight // width) for weight in weights]))


def ranked_ids(stream_key, extent, amount, lean):
    table = cumulative_ranks(amount, lean)
    pick = jax.random.randint(jax.random.fold_in(stream_key, 1), extent, 0, int(table[amount - 1]))
    rank = jnp.searchsorted(jnp.asarray(table, jnp.int32), pick, side="right")
    return jax.random.permutation(jax.random.fold_in(stream_key, 2), amount)[rank].astype(jnp.int32)


def noise(stream_key, shape, deviation, bound, split=(), kind=jnp.bfloat16):
    array = deviation * jax.random.normal(stream_key, shape, jnp.float32)
    if split:
        array = array * block_scale(stream_key, shape, split, -0.22, 0.18)
    return jnp.clip(array, -bound, bound).astype(kind)


def bell_draw_with(rng, dims, deviation, most, shards, heavy, held_as=jnp.bfloat16):
    drawn = deviation * jax.random.normal(rng, dims, jnp.float32)
    if shards:
        drawn = drawn * block_scale(rng, dims, shards, -0.22, 0.18)
    return jnp.clip(with_spikes(drawn, jax.random.fold_in(rng, 3), *heavy), -most, most).astype(held_as)


def setup_inputs(seed: int = 0, part: int = 0) -> dict:
    keys = jax.random.split(jax.random.key(seed), 7)
    part_splits = jax.random.split(jax.random.fold_in(keys[6], part), 7)
    return {
        "queries": noise(part_splits[0], (SEQS, L, HEADS * DH), 1.0, 6.0, ((0, 2), (1, 4), (2, 2))),
        "key_rows": noise(part_splits[1], (SEQS, L, HEADS * DH), 1.0, 6.0, ((0, 2), (1, 4), (2, 2))),
        "value_rows": noise(part_splits[2], (SEQS, L, HEADS * DH), 1.0, 6.0, ((0, 2), (1, 4), (2, 2))),
        "layout": place_ends(ranked_ids(keys[3], (HEADS, NB, NSEL), NB, 2), jax.random.fold_in(keys[3], 3), 0, NB - 1).astype(jnp.int32),
        "out_weight": noise(keys[4], (D, HEADS * DH), (HEADS * DH) ** -0.5, 0.25, ((1, 2),)),
        "out_grad": bell_draw_with(part_splits[5], (SEQS, L, D), 1.0, 6.0, ((0, 2), (1, 4), (2, 2)), (1, 2, 4, 2.0)),
    }


epsilon = 1e-06

def feature_map(inputs):
    return jnp.where(inputs > 0, inputs + 1.0, jnp.exp(jnp.minimum(inputs, 0.0)))

def feature_slope(inputs):
    return jnp.where(inputs > 0, 1.0, jnp.exp(jnp.minimum(inputs, 0.0)))

def reference(queries, key_rows, value_rows, layout, out_weight, out_grad):
    highest = lax.Precision.HIGHEST
    counts = lax.optimization_barrier(jnp.sum((layout[..., None] == jnp.arange(NB, dtype=jnp.int32)).astype(jnp.float32), axis=2))
    causal = jnp.tril(jnp.ones((BLK, BLK), jnp.float32))
    attn_list = []
    query_list = []
    key_list = []
    value_list = []
    weight_total = jnp.zeros((D, HEADS * DH), jnp.float32)
    for sequence in range(SEQS):
        query_in = queries[sequence].astype(jnp.float32).reshape(NB, BLK, HEADS, DH)
        key_in = key_rows[sequence].astype(jnp.float32).reshape(NB, BLK, HEADS, DH)
        value_in = value_rows[sequence].astype(jnp.float32).reshape(NB, BLK, HEADS, DH)
        query_feat = feature_map(query_in).astype(jnp.bfloat16).astype(jnp.float32)
        key_feat = feature_map(key_in).astype(jnp.bfloat16).astype(jnp.float32)
        states = jnp.einsum('nthd,nthe->nhde', key_feat, value_in)
        carried = jnp.einsum('hqb,bhde->qhde', counts, states, precision=highest)
        carried_b = carried.astype(jnp.bfloat16).astype(jnp.float32)
        scores = jnp.einsum('nthd,nshd->nhts', query_feat, key_feat) * causal
        scores_b = scores.astype(jnp.bfloat16).astype(jnp.float32)
        numer = jnp.einsum('nthd,nhde->nthe', query_feat, carried_b) + jnp.einsum('nhts,nshe->nthe', scores_b, value_in)
        rinv = lax.rsqrt(lax.optimization_barrier(jnp.mean(numer * numer, axis=-1, keepdims=True)) + epsilon)
        attn_out = (numer * rinv).astype(jnp.bfloat16)
        d_attn = jnp.dot(out_grad[sequence], out_weight, preferred_element_type=jnp.float32).astype(jnp.bfloat16)
        grad_f = d_attn.astype(jnp.float32).reshape(NB, BLK, HEADS, DH)
        d_numer = rinv * grad_f - numer * rinv ** 3 * lax.optimization_barrier(jnp.mean(grad_f * numer, axis=-1, keepdims=True))
        d_numer = d_numer.astype(jnp.bfloat16).astype(jnp.float32)
        c_grad = jnp.einsum('nthd,nthe->nhde', query_feat, d_numer)
        s_grad = jnp.einsum('hqb,qhde->bhde', counts, c_grad, precision=highest)
        s_grad = s_grad.astype(jnp.bfloat16).astype(jnp.float32)
        p_grad = (jnp.einsum('nthe,nshe->nhts', d_numer, value_in) * causal).astype(jnp.bfloat16).astype(jnp.float32)
        dq_feat = jnp.einsum('nthe,nhde->nthd', d_numer, carried_b) + jnp.einsum('nhts,nshd->nthd', p_grad, key_feat)
        dk_feat = jnp.einsum('nshe,nhde->nshd', value_in, s_grad) + jnp.einsum('nhts,nthd->nshd', p_grad, query_feat)
        dv_full = jnp.einsum('nshd,nhde->nshe', key_feat, s_grad) + jnp.einsum('nhts,nthe->nshe', scores_b, d_numer)
        attn_flat = attn_out.reshape(L, HEADS * DH)
        attn_list.append(attn_flat)
        query_list.append((dq_feat * feature_slope(query_in)).astype(jnp.bfloat16).reshape(L, HEADS * DH))
        key_list.append((dk_feat * feature_slope(key_in)).astype(jnp.bfloat16).reshape(L, HEADS * DH))
        value_list.append(dv_full.astype(jnp.bfloat16).reshape(L, HEADS * DH))
        weight_total = weight_total + jnp.dot(out_grad[sequence].T, attn_flat, preferred_element_type=jnp.float32)
    return (jnp.stack(attn_list), jnp.stack(query_list), jnp.stack(key_list), jnp.stack(value_list), weight_total)
```

```python
import functools

import jax
import jax.numpy as jnp
from jax import lax
from jax.experimental import pallas as pl
from jax.experimental.pallas import tpu as pltpu
from jax.sharding import PartitionSpec as P

DH = 128
BLK = 256
EPS = 1e-06
F32 = jnp.float32
BF16 = jnp.bfloat16
VM = pl.BlockSpec(memory_space=pltpu.VMEM)
SM = pl.BlockSpec(memory_space=pltpu.SMEM)
TN = (((0,), (0,)), ((), ()))
NT = (((1,), (1,)), ((), ()))
NN = (((1,), (0,)), ((), ()))


def sds(shape, dtype):
    return jax.ShapeDtypeStruct(shape, dtype)


def mm(a, b, dims):
    return lax.dot_general(a, b, dims, preferred_element_type=F32)


def feature(x):
    return jnp.where(x > 0, x + 1.0, jnp.exp(jnp.minimum(x, 0.0)))


def slope(x):
    return jnp.where(x > 0, 1.0, jnp.exp(jnp.minimum(x, 0.0)))


def call(body, outs, ins, flops, name):
    read = sum(a.size * a.dtype.itemsize for a in ins)
    wrote = sum(s.size * s.dtype.itemsize for s in outs)
    return pl.pallas_call(
        body,
        out_shape=outs,
        in_specs=[SM if a.dtype == jnp.int32 else VM for a in ins],
        out_specs=[VM] * len(outs),
        name=name,
        cost_estimate=pl.CostEstimate(flops=flops, bytes_accessed=read + wrote, transcendentals=0),
    )(*ins)


def tiles(tokens, heads):
    for n in range(tokens // BLK):
        for h in range(heads):
            yield n * heads + h, slice(n * BLK, (n + 1) * BLK), slice(h * DH, (h + 1) * DH)


def mat(i):
    return slice(i * DH, (i + 1) * DH)


def states_body(k_ref, v_ref, kf_ref, st_ref):
    for i, r, c in tiles(k_ref.shape[0], k_ref.shape[1] // DH):
        kf = feature(k_ref[r, c].astype(F32)).astype(BF16)
        kf_ref[r, c] = kf
        st_ref[mat(i), :] = mm(kf, v_ref[r, c], TN).astype(BF16)


def causal():
    rows = lax.broadcasted_iota(jnp.int32, (BLK, BLK), 0)
    cols = lax.broadcasted_iota(jnp.int32, (BLK, BLK), 1)
    return rows >= cols


def scores_body(q_ref, kf_ref, v_ref, qf_ref, sc_ref, intra_ref):
    keep = causal()
    for i, r, c in tiles(q_ref.shape[0], q_ref.shape[1] // DH):
        qf = feature(q_ref[r, c].astype(F32)).astype(BF16)
        qf_ref[r, c] = qf
        sc = jnp.where(keep, mm(qf, kf_ref[r, c], NT), 0.0).astype(BF16)
        sc_ref[i * BLK : (i + 1) * BLK, :] = sc
        intra_ref[r, c] = mm(sc, v_ref[r, c], NN)


def count(lay_ref, nsel, nb_all, h, i, b):
    total = jnp.int32(0)
    base = (h * nb_all + i) * nsel
    for j in range(nsel):
        total = total + jnp.where(lay_ref[base + j] == b, 1, 0)
    return total.astype(F32)


def numer_body(dims, np_, *refs):
    nb, heads, nb_all, nsel = dims
    pos_ref, base_ref, lay_ref = refs[:3]
    parts = refs[3 : 3 + np_]
    qf_ref, intra_ref, carried_ref, num_ref, attn_ref = refs[3 + np_ :]
    for i, r, c in tiles(qf_ref.shape[0], heads):
        n, h = divmod(i, heads)
        query_block = pos_ref[0] * nb + n
        total = jnp.zeros((DH, DH), F32)
        for s, part in enumerate(parts):
            for b in range(part.shape[0] // (heads * DH)):
                times = count(lay_ref, nsel, nb_all, h, query_block, base_ref[s] + b)
                total = total + times * part[mat(b * heads + h), :].astype(F32)
        carried = total.astype(BF16)
        carried_ref[mat(i), :] = carried
        num = mm(qf_ref[r, c], carried, NN) + intra_ref[r, c]
        num_ref[r, c] = num
        rinv = lax.rsqrt(jnp.mean(num * num, axis=-1, keepdims=True) + EPS)
        attn_ref[r, c] = (num * rinv).astype(BF16)


def dnum_body(n_d, *refs):
    d_refs = refs[:n_d]
    num_ref, qf_ref, dnum_ref, cg_ref = refs[n_d:]
    for i, r, c in tiles(num_ref.shape[0], num_ref.shape[1] // DH):
        num = num_ref[r, c]
        grad = d_refs[0][r, c].astype(F32)
        for d in d_refs[1:]:
            grad = grad + d[r, c].astype(F32)
        grad = grad.astype(BF16).astype(F32)
        rinv = lax.rsqrt(jnp.mean(num * num, axis=-1, keepdims=True) + EPS)
        lean = jnp.mean(grad * num, axis=-1, keepdims=True)
        dnum = (rinv * grad - num * (rinv * rinv * rinv * lean)).astype(BF16)
        dnum_ref[r, c] = dnum
        cg_ref[mat(i), :] = mm(qf_ref[r, c], dnum, TN).astype(BF16)


def query_body(q_ref, qf_ref, kf_ref, v_ref, dnum_ref, carried_ref, sc_ref, dq_ref, dk_ref, dv_ref):
    keep = causal()
    for i, r, c in tiles(q_ref.shape[0], q_ref.shape[1] // DH):
        dnum = dnum_ref[r, c]
        pg = jnp.where(keep, mm(dnum, v_ref[r, c], NT), 0.0).astype(BF16)
        dq = mm(dnum, carried_ref[mat(i), :], NT) + mm(pg, kf_ref[r, c], NN)
        dq_ref[r, c] = (dq * slope(q_ref[r, c].astype(F32))).astype(BF16)
        dk_ref[r, c] = mm(pg, qf_ref[r, c], TN)
        dv_ref[r, c] = mm(sc_ref[i * BLK : (i + 1) * BLK, :], dnum, TN)


def key_body(dims, np_, *refs):
    nb, heads, nb_all, nsel = dims
    pos_ref, base_ref, lay_ref = refs[:3]
    parts = refs[3 : 3 + np_]
    k_ref, kf_ref, v_ref, dkp_ref, dvp_ref, dk_ref, dv_ref = refs[3 + np_ :]
    for i, r, c in tiles(k_ref.shape[0], heads):
        n, h = divmod(i, heads)
        key_block = pos_ref[0] * nb + n
        total = jnp.zeros((DH, DH), F32)
        for s, part in enumerate(parts):
            for b in range(part.shape[0] // (heads * DH)):
                times = count(lay_ref, nsel, nb_all, h, base_ref[s] + b, key_block)
                total = total + times * part[mat(b * heads + h), :].astype(F32)
        sg = total.astype(BF16)
        dk = mm(v_ref[r, c], sg, NT) + dkp_ref[r, c]
        dk_ref[r, c] = (dk * slope(k_ref[r, c].astype(F32))).astype(BF16)
        dv_ref[r, c] = (mm(kf_ref[r, c], sg, NN) + dvp_ref[r, c]).astype(BF16)


def own_body(at_ref, og_ref, w_ref, out_ref):
    part = mm(og_ref[...], w_ref[...], NN)

    @pl.when(pl.program_id(0) == 0)
    def _():
        out_ref[...] = part

    @pl.when(pl.program_id(0) > 0)
    def _():
        out_ref[...] += part


def own_partial(at, og, w, steps=4):
    tokens, width = og.shape
    cols = w.shape[1]
    bk = width // steps
    return pl.pallas_call(
        own_body,
        out_shape=sds((tokens, cols), F32),
        grid_spec=pltpu.PrefetchScalarGridSpec(
            num_scalar_prefetch=1,
            grid=(steps,),
            in_specs=[
                pl.BlockSpec((tokens, bk), lambda g, at: (0, g)),
                pl.BlockSpec((bk, cols), lambda g, at: (at[0] * steps + g, 0)),
            ],
            out_specs=pl.BlockSpec((tokens, cols), lambda g, at: (0, 0)),
        ),
        name="own_partial",
        cost_estimate=pl.CostEstimate(
            flops=2 * tokens * width * cols,
            bytes_accessed=2 * tokens * width + 2 * width * cols + 4 * tokens * cols,
            transcendentals=0,
        ),
    )(at, og, w)


def other_body(at_ref, og_ref, first_ref, second_ref, out_ref, acc_ref):
    @pl.when(pl.program_id(0) == 0)
    def _():
        acc_ref[...] = mm(og_ref[...], first_ref[...], NN)

    @pl.when(pl.program_id(0) == 1)
    def _():
        out_ref[...] = (acc_ref[...] + mm(og_ref[...], second_ref[...], NN)).astype(BF16)


def other_partial(at, og, first, second):
    tokens, width = og.shape
    half, cols = first.shape
    return pl.pallas_call(
        other_body,
        out_shape=sds((tokens, cols), BF16),
        grid_spec=pltpu.PrefetchScalarGridSpec(
            num_scalar_prefetch=1,
            grid=(2,),
            in_specs=[
                pl.BlockSpec((tokens, half), lambda g, at: (0, at[g])),
                pl.BlockSpec((half, cols), lambda g, at: (0, 0)),
                pl.BlockSpec((half, cols), lambda g, at: (0, 0)),
            ],
            out_specs=pl.BlockSpec((tokens, cols), lambda g, at: (0, 0)),
            scratch_shapes=[pltpu.VMEM((tokens, cols), F32)],
        ),
        name="other_partial",
        cost_estimate=pl.CostEstimate(
            flops=2 * tokens * width * cols,
            bytes_accessed=2 * tokens * width + 2 * width * cols + 2 * tokens * cols,
            transcendentals=0,
        ),
    )(at, og, first, second)


def wg_send_body(at_ref, attn_ref, og_ref, out_ref):
    out_ref[...] = mm(attn_ref[...], og_ref[...], TN).astype(BF16)


def wg_keep_body(at_ref, attn_ref, og_ref, got_ref, give_ref, keep_ref):
    total = mm(attn_ref[...], og_ref[...], TN) + got_ref[...].astype(F32)

    @pl.when(pl.program_id(0) == 0)
    def _():
        give_ref[...] = total.astype(BF16)

    @pl.when(pl.program_id(0) == 1)
    def _():
        keep_ref[...] = total


def weight_part(at, attn, og, got=None):
    tokens, cols = attn.shape
    rows = og.shape[1] // 4
    whole = pl.BlockSpec((cols, rows), lambda g, at: (0, 0))
    specs = [
        pl.BlockSpec((tokens, cols), lambda g, at: (0, 0)),
        pl.BlockSpec((tokens, rows), lambda g, at: (0, at[g])),
    ]
    if got is None:
        body, args = wg_send_body, (at, attn, og)
        outs = sds((2 * cols, rows), BF16)
        out_specs = pl.BlockSpec((cols, rows), lambda g, at: (g, 0))
    else:
        body, args = wg_keep_body, (at, attn, og, got)
        specs.append(pl.BlockSpec((cols, rows), lambda g, at: (g, 0)))
        outs = (sds((cols, rows), BF16), sds((cols, rows), F32))
        out_specs = (whole, whole)
    return pl.pallas_call(
        body,
        out_shape=outs,
        grid_spec=pltpu.PrefetchScalarGridSpec(
            num_scalar_prefetch=1, grid=(2,), in_specs=specs, out_specs=out_specs
        ),
        name="weight_send" if got is None else "weight_keep",
        cost_estimate=pl.CostEstimate(
            flops=4 * tokens * rows * cols,
            bytes_accessed=2 * tokens * (cols + 2 * rows) + 6 * cols * rows,
            transcendentals=0,
        ),
    )(*args)


def pair_body(keep_ref, got_ref, out_ref):
    out_ref[...] = (keep_ref[...] + got_ref[...].astype(F32)).astype(BF16)


def final_body(pos_ref, mine_ref, a_ref, b_ref, c_ref, out_ref):
    mine = jnp.where(pos_ref[1] > 0, mine_ref[...].astype(F32), 0.0)
    total = mine + a_ref[...].astype(F32) + b_ref[...].astype(F32) + c_ref[...].astype(F32)
    out_ref[...] = total.T


def swap(x, axis):
    return lax.ppermute(x, axis, [(0, 1), (1, 0)])


def gather_parts(x, size):
    if size > 4:
        return [lax.all_gather(x, "seq", axis=0, tiled=True)]
    parts = [x]
    for shift in range(1, size):
        pairs = [(i, (i + shift) % size) for i in range(size)]
        parts.append(lax.ppermute(x, "seq", pairs))
    return parts


def per_device(queries, key_rows, value_rows, layout, out_weight, out_grad):
    seq_size = lax.axis_size("seq")
    head_size = lax.axis_size("head")
    dp_size = lax.axis_size("dp")
    z = lax.axis_index("seq").astype(jnp.int32)
    x = lax.axis_index("head").astype(jnp.int32)
    core = lax.axis_index("dp").astype(jnp.int32)
    heads, nb_all, nsel = layout.shape
    q, k, v, og = queries[0], key_rows[0], value_rows[0], out_grad[0]
    tokens, cols = q.shape
    nb = tokens // BLK
    dims = (nb, heads, nb_all, nsel)
    paired = seq_size == 4 and head_size == 2 and dp_size == 2
    home = (z // 2 == x).astype(jnp.int32)
    pos = jnp.stack([z, home])
    lay = layout.reshape(-1)
    if seq_size > 4:
        bases = jnp.zeros((1,), jnp.int32)
    else:
        bases = ((z - jnp.arange(seq_size, dtype=jnp.int32)) % seq_size) * nb
    flat = sds((tokens, cols), F32)
    rows16 = sds((tokens, cols), BF16)
    mats = sds((nb * heads * DH, DH), BF16)
    unit = 2 * tokens * cols * DH

    if paired:
        width = og.shape[1]
        half = width // 2
        far = lax.dynamic_slice_in_dim(out_weight, (1 - x) * width + core * half, half, 0)
        w_first = swap(far, "head")
    kf, st = call(states_body, (rows16, mats), (k, v), unit, "states")
    parts = gather_parts(st, seq_size)
    qf, sc, intra = call(
        scores_body,
        (rows16, sds((nb * heads * BLK, BLK), BF16), flat),
        (q, kf, v),
        4 * unit,
        "scores",
    )
    if paired:
        d_own = own_partial(x[None], og, out_weight)
        w_second = swap(w_first, "dp")
        d_other = other_partial(jnp.stack([core, 1 - core]), og, w_first, w_second)
    else:
        og = lax.all_gather(og, "head", axis=1, tiled=True)
        d_own = jnp.dot(og, out_weight, preferred_element_type=F32)
    carried, num, attn = call(
        functools.partial(numer_body, dims, len(parts)),
        (mats, flat, rows16),
        (pos, bases, lay, *parts, qf, intra),
        unit,
        "numer",
    )
    if paired:
        attn_other = swap(attn, "head")
        d_parts = (d_own, swap(d_other, "head"))
    else:
        d_parts = (d_own,)
    dnum, cg = call(
        functools.partial(dnum_body, len(d_parts)),
        (rows16, mats),
        (*d_parts, num, qf),
        unit,
        "dnum",
    )
    cparts = gather_parts(cg, seq_size)
    dq, dkp, dvp = call(
        query_body,
        (rows16, flat, flat),
        (q, qf, kf, v, dnum, carried, sc),
        9 * unit,
        "query",
    )
    dk, dv = call(
        functools.partial(key_body, dims, len(cparts)),
        (rows16, rows16),
        (pos, bases, lay, *cparts, k, kf, v, dkp, dvp),
        2 * unit,
        "key",
    )
    if paired:
        parity = z % 2
        order = jnp.stack([1 - parity, parity])
        give_at = 2 * order + (1 - core)
        keep_at = 2 * order + core
        neighbours = [(0, 1), (1, 0), (2, 3), (3, 2)]
        sums = []
        for block in (attn, attn_other):
            got = swap(weight_part(give_at, block, og), "dp")
            give, keep = weight_part(keep_at, block, og, got)
            got = lax.ppermute(give, "seq", neighbours)
            sums.append(call(pair_body, (sds(keep.shape, BF16),), (keep, got), 0, "pair")[0])
        mine, cross = sums
        to_line, to_side, to_both = [], [], []
        for s in range(4):
            for h in range(2):
                if s // 2 == h:
                    to_side.append((s * 2 + h, s * 2 + 1 - h))
                else:
                    to_line.append((s * 2 + h, (s ^ 2) * 2 + h))
                    to_both.append((s * 2 + h, (s ^ 2) * 2 + 1 - h))
        axes = ("seq", "head")
        arrived = (
            lax.ppermute(mine, axes, to_line),
            lax.ppermute(cross, axes, to_both),
            lax.ppermute(cross, axes, to_side),
        )
        (weight_grad,) = call(
            final_body, (sds(mine.shape[::-1], F32),), (pos, mine, *arrived), 0, "final"
        )
    else:
        weight_grad = lax.psum_scatter(
            lax.dot_general(og, attn, TN, preferred_element_type=F32).astype(BF16),
            ("seq", "dp"),
            scatter_dimension=0,
            tiled=True,
        ).astype(F32)
    return attn[None], dq[None], dk[None], dv[None], weight_grad


def solution(mesh):
    rows = P(("groups", "dp"), "seq", "head")
    return jax.shard_map(
        per_device,
        mesh=mesh,
        in_specs=(rows, rows, rows, P("head", None, None), P(None, "head"), rows),
        out_specs=(rows, rows, rows, rows, P(("groups", "seq", "dp"), "head")),
        check_vma=False,
    )
```

```python
import functools

import jax
import jax.numpy as jnp
from jax import lax
from jax.experimental import pallas as pl
from jax.experimental.pallas import tpu as pltpu
from jax.sharding import PartitionSpec as P

DH = 128
BLK = 256
EPS = 1e-06
LIMIT = 16 << 20
F32 = jnp.float32
BF16 = jnp.bfloat16
VM = pl.BlockSpec(memory_space=pltpu.VMEM)
SM = pl.BlockSpec(memory_space=pltpu.SMEM)
TN = (((0,), (0,)), ((), ()))
NT = (((1,), (1,)), ((), ()))
NN = (((1,), (0,)), ((), ()))


def sds(shape, dtype):
    return jax.ShapeDtypeStruct(shape, dtype)


def mm(a, b, dims):
    return lax.dot_general(a, b, dims, preferred_element_type=F32)


def feature(x):
    return jnp.where(x > 0, x + 1.0, jnp.exp(jnp.minimum(x, 0.0)))


def slope(x):
    return jnp.where(x > 0, 1.0, jnp.exp(jnp.minimum(x, 0.0)))


def call(body, outs, ins, flops, name):
    read = sum(a.size * a.dtype.itemsize for a in ins)
    wrote = sum(s.size * s.dtype.itemsize for s in outs)
    return pl.pallas_call(
        body,
        out_shape=outs,
        in_specs=[SM if a.dtype == jnp.int32 else VM for a in ins],
        out_specs=[VM] * len(outs),
        name=name,
        compiler_params=pltpu.CompilerParams(vmem_limit_bytes=LIMIT),
        cost_estimate=pl.CostEstimate(flops=flops, bytes_accessed=read + wrote, transcendentals=0),
    )(*ins)


def tiles(tokens, heads):
    for n in range(tokens // BLK):
        for h in range(heads):
            yield n * heads + h, slice(n * BLK, (n + 1) * BLK), slice(h * DH, (h + 1) * DH)


def mat(i):
    return slice(i * DH, (i + 1) * DH)


def states_body(k_ref, v_ref, kf_ref, st_ref):
    for i, r, c in tiles(k_ref.shape[0], k_ref.shape[1] // DH):
        kf = feature(k_ref[r, c].astype(F32)).astype(BF16)
        kf_ref[r, c] = kf
        st_ref[mat(i), :] = mm(kf, v_ref[r, c], TN).astype(BF16)


def causal():
    rows = lax.broadcasted_iota(jnp.int32, (BLK, BLK), 0)
    cols = lax.broadcasted_iota(jnp.int32, (BLK, BLK), 1)
    return rows >= cols


def scores_body(q_ref, kf_ref, v_ref, qf_ref, sc_ref, intra_ref):
    keep = causal()
    for i, r, c in tiles(q_ref.shape[0], q_ref.shape[1] // DH):
        qf = feature(q_ref[r, c].astype(F32)).astype(BF16)
        qf_ref[r, c] = qf
        sc = jnp.where(keep, mm(qf, kf_ref[r, c], NT), 0.0).astype(BF16)
        sc_ref[i * BLK : (i + 1) * BLK, :] = sc
        intra_ref[r, c] = mm(sc, v_ref[r, c], NN)


def count(lay_ref, nsel, nb_all, h, i, b):
    total = jnp.int32(0)
    base = (h * nb_all + i) * nsel
    for j in range(nsel):
        total = total + jnp.where(lay_ref[base + j] == b, 1, 0)
    return total.astype(F32)


def numer_body(dims, np_, *refs):
    nb, heads, nb_all, nsel = dims
    pos_ref, base_ref, lay_ref = refs[:3]
    parts = refs[3 : 3 + np_]
    qf_ref, intra_ref, carried_ref, num_ref, attn_ref = refs[3 + np_ :]
    for i, r, c in tiles(qf_ref.shape[0], heads):
        n, h = divmod(i, heads)
        query_block = pos_ref[0] * nb + n
        total = jnp.zeros((DH, DH), F32)
        for s, part in enumerate(parts):
            for b in range(part.shape[0] // (heads * DH)):
                times = count(lay_ref, nsel, nb_all, h, query_block, base_ref[s] + b)
                total = total + times * part[mat(b * heads + h), :].astype(F32)
        carried = total.astype(BF16)
        carried_ref[mat(i), :] = carried
        num = mm(qf_ref[r, c], carried, NN) + intra_ref[r, c]
        num_ref[r, c] = num
        rinv = lax.rsqrt(jnp.mean(num * num, axis=-1, keepdims=True) + EPS)
        attn_ref[r, c] = (num * rinv).astype(BF16)


def dnum_body(n_d, *refs):
    d_refs = refs[:n_d]
    num_ref, qf_ref, dnum_ref, cg_ref = refs[n_d:]
    for i, r, c in tiles(num_ref.shape[0], num_ref.shape[1] // DH):
        num = num_ref[r, c]
        grad = d_refs[0][r, c].astype(F32)
        for d in d_refs[1:]:
            grad = grad + d[r, c].astype(F32)
        grad = grad.astype(BF16).astype(F32)
        rinv = lax.rsqrt(jnp.mean(num * num, axis=-1, keepdims=True) + EPS)
        lean = jnp.mean(grad * num, axis=-1, keepdims=True)
        dnum = (rinv * grad - num * (rinv * rinv * rinv * lean)).astype(BF16)
        dnum_ref[r, c] = dnum
        cg_ref[mat(i), :] = mm(qf_ref[r, c], dnum, TN).astype(BF16)


def query_body(q_ref, qf_ref, kf_ref, v_ref, dnum_ref, carried_ref, sc_ref, dq_ref, dk_ref, dv_ref):
    keep = causal()
    for i, r, c in tiles(q_ref.shape[0], q_ref.shape[1] // DH):
        dnum = dnum_ref[r, c]
        pg = jnp.where(keep, mm(dnum, v_ref[r, c], NT), 0.0).astype(BF16)
        dq = mm(dnum, carried_ref[mat(i), :], NT) + mm(pg, kf_ref[r, c], NN)
        dq_ref[r, c] = (dq * slope(q_ref[r, c].astype(F32))).astype(BF16)
        dk_ref[r, c] = mm(pg, qf_ref[r, c], TN)
        dv_ref[r, c] = mm(sc_ref[i * BLK : (i + 1) * BLK, :], dnum, TN)


def key_body(dims, np_, *refs):
    nb, heads, nb_all, nsel = dims
    pos_ref, base_ref, lay_ref = refs[:3]
    parts = refs[3 : 3 + np_]
    k_ref, kf_ref, v_ref, dkp_ref, dvp_ref, dk_ref, dv_ref = refs[3 + np_ :]
    for i, r, c in tiles(k_ref.shape[0], heads):
        n, h = divmod(i, heads)
        key_block = pos_ref[0] * nb + n
        total = jnp.zeros((DH, DH), F32)
        for s, part in enumerate(parts):
            for b in range(part.shape[0] // (heads * DH)):
                times = count(lay_ref, nsel, nb_all, h, base_ref[s] + b, key_block)
                total = total + times * part[mat(b * heads + h), :].astype(F32)
        sg = total.astype(BF16)
        dk = mm(v_ref[r, c], sg, NT) + dkp_ref[r, c]
        dk_ref[r, c] = (dk * slope(k_ref[r, c].astype(F32))).astype(BF16)
        dv_ref[r, c] = (mm(kf_ref[r, c], sg, NN) + dvp_ref[r, c]).astype(BF16)


def own_body(at_ref, og_ref, w_ref, out_ref):
    part = mm(og_ref[...], w_ref[...], NN)

    @pl.when(pl.program_id(0) == 0)
    def _():
        out_ref[...] = part

    @pl.when(pl.program_id(0) > 0)
    def _():
        out_ref[...] += part


def own_partial(at, og, w, steps=4):
    tokens, width = og.shape
    cols = w.shape[1]
    bk = width // steps
    return pl.pallas_call(
        own_body,
        out_shape=sds((tokens, cols), F32),
        grid_spec=pltpu.PrefetchScalarGridSpec(
            num_scalar_prefetch=1,
            grid=(steps,),
            in_specs=[
                pl.BlockSpec((tokens, bk), lambda g, at: (0, g)),
                pl.BlockSpec((bk, cols), lambda g, at: (at[0] * steps + g, 0)),
            ],
            out_specs=pl.BlockSpec((tokens, cols), lambda g, at: (0, 0)),
        ),
        name="own_partial",
        compiler_params=pltpu.CompilerParams(vmem_limit_bytes=LIMIT),
        cost_estimate=pl.CostEstimate(
            flops=2 * tokens * width * cols,
            bytes_accessed=2 * tokens * width + 2 * width * cols + 4 * tokens * cols,
            transcendentals=0,
        ),
    )(at, og, w)


def other_body(at_ref, og_ref, first_ref, second_ref, out_ref, acc_ref):
    @pl.when(pl.program_id(0) == 0)
    def _():
        acc_ref[...] = mm(og_ref[...], first_ref[...], NN)

    @pl.when(pl.program_id(0) == 1)
    def _():
        out_ref[...] = (acc_ref[...] + mm(og_ref[...], second_ref[...], NN)).astype(BF16)


def other_partial(at, og, first, second):
    tokens, width = og.shape
    half, cols = first.shape
    return pl.pallas_call(
        other_body,
        out_shape=sds((tokens, cols), BF16),
        grid_spec=pltpu.PrefetchScalarGridSpec(
            num_scalar_prefetch=1,
            grid=(2,),
            in_specs=[
                pl.BlockSpec((tokens, half), lambda g, at: (0, at[g])),
                pl.BlockSpec((half, cols), lambda g, at: (0, 0)),
                pl.BlockSpec((half, cols), lambda g, at: (0, 0)),
            ],
            out_specs=pl.BlockSpec((tokens, cols), lambda g, at: (0, 0)),
            scratch_shapes=[pltpu.VMEM((tokens, cols), F32)],
        ),
        name="other_partial",
        compiler_params=pltpu.CompilerParams(vmem_limit_bytes=LIMIT),
        cost_estimate=pl.CostEstimate(
            flops=2 * tokens * width * cols,
            bytes_accessed=2 * tokens * width + 2 * width * cols + 2 * tokens * cols,
            transcendentals=0,
        ),
    )(at, og, first, second)


def wg_send_body(at_ref, attn_ref, og_ref, out_ref):
    out_ref[...] = mm(attn_ref[...], og_ref[...], TN).astype(BF16)


def wg_keep_body(at_ref, attn_ref, og_ref, got_ref, give_ref, keep_ref):
    total = mm(attn_ref[...], og_ref[...], TN) + got_ref[...].astype(F32)

    @pl.when(pl.program_id(0) == 0)
    def _():
        give_ref[...] = total.astype(BF16)

    @pl.when(pl.program_id(0) == 1)
    def _():
        keep_ref[...] = total


def weight_part(at, attn, og, got=None):
    tokens, cols = attn.shape
    rows = og.shape[1] // 4
    whole = pl.BlockSpec((cols, rows), lambda g, at: (0, 0))
    specs = [
        pl.BlockSpec((tokens, cols), lambda g, at: (0, 0)),
        pl.BlockSpec((tokens, rows), lambda g, at: (0, at[g])),
    ]
    if got is None:
        body, args = wg_send_body, (at, attn, og)
        outs = sds((2 * cols, rows), BF16)
        out_specs = pl.BlockSpec((cols, rows), lambda g, at: (g, 0))
    else:
        body, args = wg_keep_body, (at, attn, og, got)
        specs.append(pl.BlockSpec((cols, rows), lambda g, at: (g, 0)))
        outs = (sds((cols, rows), BF16), sds((cols, rows), F32))
        out_specs = (whole, whole)
    return pl.pallas_call(
        body,
        out_shape=outs,
        grid_spec=pltpu.PrefetchScalarGridSpec(
            num_scalar_prefetch=1, grid=(2,), in_specs=specs, out_specs=out_specs
        ),
        name="weight_send" if got is None else "weight_keep",
        compiler_params=pltpu.CompilerParams(vmem_limit_bytes=LIMIT),
        cost_estimate=pl.CostEstimate(
            flops=4 * tokens * rows * cols,
            bytes_accessed=2 * tokens * (cols + 2 * rows) + 6 * cols * rows,
            transcendentals=0,
        ),
    )(*args)


def pair_body(keep_ref, got_ref, out_ref):
    out_ref[...] = (keep_ref[...] + got_ref[...].astype(F32)).astype(BF16)


def final_body(pos_ref, mine_ref, a_ref, b_ref, c_ref, out_ref):
    mine = jnp.where(pos_ref[1] > 0, mine_ref[...].astype(F32), 0.0)
    total = mine + a_ref[...].astype(F32) + b_ref[...].astype(F32) + c_ref[...].astype(F32)
    out_ref[...] = total.T


def swap(x, axis):
    return lax.ppermute(x, axis, [(0, 1), (1, 0)])


def gather_parts(x, size):
    if size > 4:
        return [lax.all_gather(x, "seq", axis=0, tiled=True)]
    parts = [x]
    for shift in range(1, size):
        pairs = [(i, (i + shift) % size) for i in range(size)]
        parts.append(lax.ppermute(x, "seq", pairs))
    return parts


def per_device(queries, key_rows, value_rows, layout, out_weight, out_grad):
    seq_size = lax.axis_size("seq")
    head_size = lax.axis_size("head")
    dp_size = lax.axis_size("dp")
    z = lax.axis_index("seq").astype(jnp.int32)
    x = lax.axis_index("head").astype(jnp.int32)
    core = lax.axis_index("dp").astype(jnp.int32)
    heads, nb_all, nsel = layout.shape
    q, k, v, og = queries[0], key_rows[0], value_rows[0], out_grad[0]
    tokens, cols = q.shape
    nb = tokens // BLK
    dims = (nb, heads, nb_all, nsel)
    paired = seq_size == 4 and head_size == 2 and dp_size == 2
    home = (z // 2 == x).astype(jnp.int32)
    pos = jnp.stack([z, home])
    lay = layout.reshape(-1)
    if seq_size > 4:
        bases = jnp.zeros((1,), jnp.int32)
    else:
        bases = ((z - jnp.arange(seq_size, dtype=jnp.int32)) % seq_size) * nb
    flat = sds((tokens, cols), F32)
    rows16 = sds((tokens, cols), BF16)
    mats = sds((nb * heads * DH, DH), BF16)
    unit = 2 * tokens * cols * DH

    if paired:
        width = og.shape[1]
        half = width // 2
        far = lax.dynamic_slice_in_dim(out_weight, (1 - x) * width + core * half, half, 0)
        w_first = swap(far, "head")
    kf, st = call(states_body, (rows16, mats), (k, v), unit, "states")
    parts = gather_parts(st, seq_size)
    qf, sc, intra = call(
        scores_body,
        (rows16, sds((nb * heads * BLK, BLK), BF16), flat),
        (q, kf, v),
        4 * unit,
        "scores",
    )
    if paired:
        d_own = own_partial(x[None], og, out_weight)
        w_second = swap(w_first, "dp")
        d_other = other_partial(jnp.stack([core, 1 - core]), og, w_first, w_second)
    else:
        og = lax.all_gather(og, "head", axis=1, tiled=True)
        d_own = jnp.dot(og, out_weight, preferred_element_type=F32)
    carried, num, attn = call(
        functools.partial(numer_body, dims, len(parts)),
        (mats, flat, rows16),
        (pos, bases, lay, *parts, qf, intra),
        unit,
        "numer",
    )
    if paired:
        attn_other = swap(attn, "head")
        d_parts = (d_own, swap(d_other, "head"))
    else:
        d_parts = (d_own,)
    dnum, cg = call(
        functools.partial(dnum_body, len(d_parts)),
        (rows16, mats),
        (*d_parts, num, qf),
        unit,
        "dnum",
    )
    cparts = gather_parts(cg, seq_size)
    dq, dkp, dvp = call(
        query_body,
        (rows16, flat, flat),
        (q, qf, kf, v, dnum, carried, sc),
        9 * unit,
        "query",
    )
    dk, dv = call(
        functools.partial(key_body, dims, len(cparts)),
        (rows16, rows16),
        (pos, bases, lay, *cparts, k, kf, v, dkp, dvp),
        2 * unit,
        "key",
    )
    if paired:
        parity = z % 2
        order = jnp.stack([1 - parity, parity])
        give_at = 2 * order + (1 - core)
        keep_at = 2 * order + core
        neighbours = [(0, 1), (1, 0), (2, 3), (3, 2)]
        sums = []
        for block in (attn, attn_other):
            got = swap(weight_part(give_at, block, og), "dp")
            give, keep = weight_part(keep_at, block, og, got)
            got = lax.ppermute(give, "seq", neighbours)
            sums.append(call(pair_body, (sds(keep.shape, BF16),), (keep, got), 0, "pair")[0])
        mine, cross = sums
        to_line, to_side, to_both = [], [], []
        for s in range(4):
            for h in range(2):
                if s // 2 == h:
                    to_side.append((s * 2 + h, s * 2 + 1 - h))
                else:
                    to_line.append((s * 2 + h, (s ^ 2) * 2 + h))
                    to_both.append((s * 2 + h, (s ^ 2) * 2 + 1 - h))
        axes = ("seq", "head")
        arrived = (
            lax.ppermute(mine, axes, to_line),
            lax.ppermute(cross, axes, to_both),
            lax.ppermute(cross, axes, to_side),
        )
        (weight_grad,) = call(
            final_body, (sds(mine.shape[::-1], F32),), (pos, mine, *arrived), 0, "final"
        )
    else:
        weight_grad = lax.psum_scatter(
            lax.dot_general(og, attn, TN, preferred_element_type=F32).astype(BF16),
            ("seq", "dp"),
            scatter_dimension=0,
            tiled=True,
        ).astype(F32)
    return attn[None], dq[None], dk[None], dv[None], weight_grad


def solution(mesh):
    rows = P(("groups", "dp"), "seq", "head")
    return jax.shard_map(
        per_device,
        mesh=mesh,
        in_specs=(rows, rows, rows, P("head", None, None), P(None, "head"), rows),
        out_specs=(rows, rows, rows, rows, P(("groups", "seq", "dp"), "head")),
        check_vma=False,
    )
```

```python
import functools

import jax
import jax.numpy as jnp
from jax import lax
from jax.experimental import pallas as pl
from jax.experimental.pallas import tpu as pltpu
from jax.sharding import PartitionSpec as P

DH = 128
BLK = 256
EPS = 1e-06
LIMIT = 16 << 20
SHORT = pl.CostEstimate(flops=1, bytes_accessed=1, transcendentals=0)
LONG = pl.CostEstimate(flops=10**11, bytes_accessed=1, transcendentals=0)
F32 = jnp.float32
BF16 = jnp.bfloat16
VM = pl.BlockSpec(memory_space=pltpu.VMEM)
SM = pl.BlockSpec(memory_space=pltpu.SMEM)
TN = (((0,), (0,)), ((), ()))
NT = (((1,), (1,)), ((), ()))
NN = (((1,), (0,)), ((), ()))


def sds(shape, dtype):
    return jax.ShapeDtypeStruct(shape, dtype)


def mm(a, b, dims):
    return lax.dot_general(a, b, dims, preferred_element_type=F32)


def feature(x):
    return jnp.where(x > 0, x + 1.0, jnp.exp(jnp.minimum(x, 0.0)))


def slope(x):
    return jnp.where(x > 0, 1.0, jnp.exp(jnp.minimum(x, 0.0)))


def call(body, outs, ins, flops, name):
    read = sum(a.size * a.dtype.itemsize for a in ins)
    wrote = sum(s.size * s.dtype.itemsize for s in outs)
    return pl.pallas_call(
        body,
        out_shape=outs,
        in_specs=[SM if a.dtype == jnp.int32 else VM for a in ins],
        out_specs=[VM] * len(outs),
        name=name,
        compiler_params=pltpu.CompilerParams(vmem_limit_bytes=LIMIT),
        cost_estimate=LONG if name in ("key", "numer") else SHORT,
    )(*ins)


def tiles(tokens, heads):
    for n in range(tokens // BLK):
        for h in range(heads):
            yield n * heads + h, slice(n * BLK, (n + 1) * BLK), slice(h * DH, (h + 1) * DH)


def mat(i):
    return slice(i * DH, (i + 1) * DH)


def states_body(k_ref, v_ref, kf_ref, st_ref):
    for i, r, c in tiles(k_ref.shape[0], k_ref.shape[1] // DH):
        kf = feature(k_ref[r, c].astype(F32)).astype(BF16)
        kf_ref[r, c] = kf
        st_ref[mat(i), :] = mm(kf, v_ref[r, c], TN).astype(BF16)


def causal():
    rows = lax.broadcasted_iota(jnp.int32, (BLK, BLK), 0)
    cols = lax.broadcasted_iota(jnp.int32, (BLK, BLK), 1)
    return rows >= cols


def scores_body(q_ref, kf_ref, v_ref, qf_ref, sc_ref, intra_ref):
    keep = causal()
    for i, r, c in tiles(q_ref.shape[0], q_ref.shape[1] // DH):
        qf = feature(q_ref[r, c].astype(F32)).astype(BF16)
        qf_ref[r, c] = qf
        sc = jnp.where(keep, mm(qf, kf_ref[r, c], NT), 0.0).astype(BF16)
        sc_ref[i * BLK : (i + 1) * BLK, :] = sc
        intra_ref[r, c] = mm(sc, v_ref[r, c], NN)


def count(lay_ref, h, i, b):
    total = jnp.int32(0)
    for j in range(lay_ref.shape[2]):
        total = total + jnp.where(lay_ref[h, i, j] == b, 1, 0)
    return total.astype(F32)


def numer_body(dims, np_, *refs):
    nb, heads = dims
    pos_ref, base_ref, lay_ref = refs[:3]
    parts = refs[3 : 3 + np_]
    qf_ref, intra_ref, carried_ref, num_ref, attn_ref = refs[3 + np_ :]
    for i, r, c in tiles(qf_ref.shape[0], heads):
        n, h = divmod(i, heads)
        query_block = pos_ref[0] * nb + n
        total = jnp.zeros((DH, DH), F32)
        for s, part in enumerate(parts):
            for b in range(part.shape[0] // (heads * DH)):
                times = count(lay_ref, h, query_block, base_ref[s] + b)
                total = total + times * part[mat(b * heads + h), :].astype(F32)
        carried = total.astype(BF16)
        carried_ref[mat(i), :] = carried
        num = mm(qf_ref[r, c], carried, NN) + intra_ref[r, c]
        num_ref[r, c] = num
        rinv = lax.rsqrt(jnp.mean(num * num, axis=-1, keepdims=True) + EPS)
        attn_ref[r, c] = (num * rinv).astype(BF16)


def dnum_body(n_d, pos_ref, *refs):
    d_refs = refs[:n_d]
    num_ref, qf_ref, dnum_ref, cg_ref = refs[n_d:]
    heads = num_ref.shape[1] // DH
    for i, r, c in tiles(num_ref.shape[0], num_ref.shape[1] // DH):
        num = num_ref[r, c]
        grad = d_refs[0][r, c].astype(F32)
        if n_d == 3:
            same, sib = d_refs[1][r, :].astype(F32), d_refs[2][r, :].astype(F32)
            grad = grad + jnp.where(pos_ref[3] == i % heads, same, sib)
        grad = grad.astype(BF16).astype(F32)
        rinv = lax.rsqrt(jnp.mean(num * num, axis=-1, keepdims=True) + EPS)
        lean = jnp.mean(grad * num, axis=-1, keepdims=True)
        dnum = (rinv * grad - num * (rinv * rinv * rinv * lean)).astype(BF16)
        dnum_ref[r, c] = dnum
        cg_ref[mat(i), :] = mm(qf_ref[r, c], dnum, TN).astype(BF16)


def query_body(q_ref, qf_ref, kf_ref, v_ref, dnum_ref, carried_ref, sc_ref, dq_ref, dk_ref, dv_ref):
    keep = causal()
    for i, r, c in tiles(q_ref.shape[0], q_ref.shape[1] // DH):
        dnum = dnum_ref[r, c]
        pg = jnp.where(keep, mm(dnum, v_ref[r, c], NT), 0.0).astype(BF16)
        dq = mm(dnum, carried_ref[mat(i), :], NT) + mm(pg, kf_ref[r, c], NN)
        dq_ref[r, c] = (dq * slope(q_ref[r, c].astype(F32))).astype(BF16)
        dk_ref[r, c] = mm(pg, qf_ref[r, c], TN)
        dv_ref[r, c] = mm(sc_ref[i * BLK : (i + 1) * BLK, :], dnum, TN)


def key_body(dims, np_, *refs):
    nb, heads = dims
    pos_ref, base_ref, lay_ref = refs[:3]
    parts = refs[3 : 3 + np_]
    k_ref, kf_ref, v_ref, dkp_ref, dvp_ref, dk_ref, dv_ref = refs[3 + np_ :]
    for i, r, c in tiles(k_ref.shape[0], heads):
        n, h = divmod(i, heads)
        key_block = pos_ref[0] * nb + n
        total = jnp.zeros((DH, DH), F32)
        for s, part in enumerate(parts):
            for b in range(part.shape[0] // (heads * DH)):
                times = count(lay_ref, h, base_ref[s] + b, key_block)
                total = total + times * part[mat(b * heads + h), :].astype(F32)
        sg = total.astype(BF16)
        dk = mm(v_ref[r, c], sg, NT) + dkp_ref[r, c]
        dk_ref[r, c] = (dk * slope(k_ref[r, c].astype(F32))).astype(BF16)
        dv_ref[r, c] = (mm(kf_ref[r, c], sg, NN) + dvp_ref[r, c]).astype(BF16)


def own_body(at_ref, og_ref, w_ref, out_ref):
    part = mm(og_ref[...], w_ref[...], NN)

    @pl.when(pl.program_id(0) == 0)
    def _():
        out_ref[...] = part

    @pl.when(pl.program_id(0) > 0)
    def _():
        out_ref[...] += part


def own_partial(at, og, w, steps=4):
    tokens, width = og.shape
    cols = w.shape[1]
    bk = width // steps
    return pl.pallas_call(
        own_body,
        out_shape=sds((tokens, cols), F32),
        grid_spec=pltpu.PrefetchScalarGridSpec(
            num_scalar_prefetch=1,
            grid=(steps,),
            in_specs=[
                pl.BlockSpec((tokens, bk), lambda g, at: (0, g)),
                pl.BlockSpec((bk, cols), lambda g, at: (at[0] * steps + g, 0)),
            ],
            out_specs=pl.BlockSpec((tokens, cols), lambda g, at: (0, 0)),
        ),
        name="own_partial",
        compiler_params=pltpu.CompilerParams(vmem_limit_bytes=LIMIT),
        cost_estimate=SHORT,
    )(at, og, w)


def other_body(og_ref, og_sib_ref, w_ref, same_ref, sib_ref):
    same_ref[...] = mm(og_ref[...], w_ref[...], NN).astype(BF16)
    sib_ref[...] = mm(og_sib_ref[...], w_ref[...], NN).astype(BF16)


def weight_body(pos_ref, attn_ref, attn_sib_ref, og_ref, og_sib_ref, give_ref, keep_ref):
    rows = give_ref.shape[1]
    parity, core = pos_ref[2], pos_ref[3]

    def part(pair):
        at = pl.ds(pl.multiple_of((2 * pair + core) * rows, rows), rows)
        return mm(attn_ref[...], og_ref[:, at], TN) + mm(attn_sib_ref[...], og_sib_ref[:, at], TN)

    give_ref[...] = part(1 - parity).astype(BF16)
    keep_ref[...] = part(parity)


def pair_body(keep_ref, got_ref, out_ref):
    out_ref[...] = (keep_ref[...] + got_ref[...].astype(F32)).astype(BF16)


def final_body(pos_ref, mine_ref, a_ref, b_ref, c_ref, out_ref):
    mine = jnp.where(pos_ref[1] > 0, mine_ref[...].astype(F32), 0.0)
    total = mine + a_ref[...].astype(F32) + b_ref[...].astype(F32) + c_ref[...].astype(F32)
    out_ref[...] = total.T


def after(x, *deps):
    return lax.optimization_barrier((x, *deps))[0]


def swap(x, axis):
    return lax.ppermute(x, axis, [(0, 1), (1, 0)])


def gather_parts(x, size):
    if size > 4:
        return [lax.all_gather(x, "seq", axis=0, tiled=True)]
    parts = [x]
    for shift in range(1, size):
        pairs = [(i, (i + shift) % size) for i in range(size)]
        parts.append(lax.ppermute(x, "seq", pairs))
    return parts


def per_device(queries, key_rows, value_rows, layout, out_weight, out_grad):
    seq_size = lax.axis_size("seq")
    head_size = lax.axis_size("head")
    dp_size = lax.axis_size("dp")
    z = lax.axis_index("seq").astype(jnp.int32)
    x = lax.axis_index("head").astype(jnp.int32)
    core = lax.axis_index("dp").astype(jnp.int32)
    heads = layout.shape[0]
    q, k, v, og = queries[0], key_rows[0], value_rows[0], out_grad[0]
    tokens, cols = q.shape
    nb = tokens // BLK
    dims = (nb, heads)
    paired = seq_size == 4 and head_size == 2 and dp_size == 2
    home = (z // 2 == x).astype(jnp.int32)
    pos = jnp.stack([z, home, z % 2, core])
    if seq_size > 4:
        bases = jnp.zeros((1,), jnp.int32)
    else:
        bases = ((z - jnp.arange(seq_size, dtype=jnp.int32)) % seq_size) * nb
    flat = sds((tokens, cols), F32)
    rows16 = sds((tokens, cols), BF16)
    mats = sds((nb * heads * DH, DH), BF16)
    unit = 2 * tokens * cols * DH

    kf, st = call(states_body, (rows16, mats), (k, v), unit, "states")
    parts = gather_parts(st, seq_size)
    if paired:
        width = og.shape[1]
        og_sib = swap(og, "dp")
        far = lax.dynamic_slice(after(out_weight, st), ((1 - x) * width, core * DH), (width, DH))
        w_other = swap(far, "head")
    qf, sc, intra = call(
        scores_body,
        (rows16, sds((nb * heads * BLK, BLK), BF16), flat),
        (q, kf, v),
        4 * unit,
        "scores",
    )
    if not paired:
        og = lax.all_gather(og, "head", axis=1, tiled=True)
        d_own = jnp.dot(og, out_weight, preferred_element_type=F32)
    carried, num, attn = call(
        functools.partial(numer_body, dims, len(parts)),
        (mats, flat, rows16),
        (pos, bases, layout, *parts, qf, intra),
        unit,
        "numer",
    )
    if paired:
        attn_other = swap(attn, "head")
        og_late, sib_late = lax.optimization_barrier((og, og_sib, attn))[:2]
        d_own = own_partial(x[None], og_late, out_weight)
        column = sds((tokens, DH), BF16)
        d_same, d_sib = call(other_body, (column, column), (og_late, sib_late, w_other), 0, "other")
        across = [(h * 2 + c, (1 - h) * 2 + 1 - c) for h in range(2) for c in range(2)]
        d_same = swap(d_same, "head")
        d_sib = lax.ppermute(d_sib, ("head", "dp"), across)
        block = (cols, width // 4)
        outs = (sds(block, BF16), sds(block, F32))
        neighbours = [(0, 1), (1, 0), (2, 3), (3, 2)]
        give_a, keep_a = call(weight_body, outs, (pos, attn, swap(attn, "dp"), og, og_sib), 0, "weight")
        got_a = lax.ppermute(give_a, "seq", neighbours)
        d_parts = (d_own, after(d_same, give_a), d_sib)
    else:
        d_parts = (d_own,)
    dnum, cg = call(
        functools.partial(dnum_body, len(d_parts)),
        (rows16, mats),
        (pos, *d_parts, num, qf),
        unit,
        "dnum",
    )
    cparts = gather_parts(cg, seq_size)
    dq, dkp, dvp = call(
        query_body,
        (rows16, flat, flat),
        (q, qf, kf, v, dnum, carried, sc),
        9 * unit,
        "query",
    )
    dk, dv = call(
        functools.partial(key_body, dims, len(cparts)),
        (rows16, rows16),
        (pos, bases, layout, *cparts, k, kf, v, dkp, dvp),
        2 * unit,
        "key",
    )
    if paired:
        attn_other = after(attn_other, cg)
        give_b, keep_b = call(
            weight_body, outs, (pos, attn_other, swap(attn_other, "dp"), og, og_sib), 0, "weight"
        )
        got_b = lax.ppermute(give_b, "seq", neighbours)
        (mine,) = call(pair_body, (sds(keep_a.shape, BF16),), (keep_a, got_a), 0, "pair")
        (cross,) = call(pair_body, (sds(keep_b.shape, BF16),), (keep_b, got_b), 0, "pair")
        to_line, to_side, to_both = [], [], []
        for s in range(4):
            for h in range(2):
                if s // 2 == h:
                    to_side.append((s * 2 + h, s * 2 + 1 - h))
                else:
                    to_line.append((s * 2 + h, (s ^ 2) * 2 + h))
                    to_both.append((s * 2 + h, (s ^ 2) * 2 + 1 - h))
        axes = ("seq", "head")
        arrived = (
            lax.ppermute(mine, axes, to_line),
            lax.ppermute(cross, axes, to_both),
            lax.ppermute(cross, axes, to_side),
        )
        (weight_grad,) = call(
            final_body, (sds(mine.shape[::-1], F32),), (pos, mine, *arrived), 0, "final"
        )
    else:
        weight_grad = lax.psum_scatter(
            lax.dot_general(og, attn, TN, preferred_element_type=F32).astype(BF16),
            ("seq", "dp"),
            scatter_dimension=0,
            tiled=True,
        ).astype(F32)
    return attn[None], dq[None], dk[None], dv[None], weight_grad


def solution(mesh):
    rows = P(("groups", "dp"), "seq", "head")
    return jax.shard_map(
        per_device,
        mesh=mesh,
        in_specs=(rows, rows, rows, P("head", None, None), P(None, "head"), rows),
        out_specs=(rows, rows, rows, rows, P(("groups", "seq", "dp"), "head")),
        check_vma=False,
    )
```

```python
import functools

import jax
import jax.numpy as jnp
from jax import lax
from jax.experimental import pallas as pl
from jax.experimental.pallas import tpu as pltpu
from jax.sharding import PartitionSpec as P

DH = 128
BLK = 256
EPS = 1e-06
LIMIT = 16 << 20
SHORT = pl.CostEstimate(flops=1, bytes_accessed=1, transcendentals=0)
LONG = pl.CostEstimate(flops=10**11, bytes_accessed=1, transcendentals=0)
F32 = jnp.float32
BF16 = jnp.bfloat16
VM = pl.BlockSpec(memory_space=pltpu.VMEM)
SM = pl.BlockSpec(memory_space=pltpu.SMEM)
TN = (((0,), (0,)), ((), ()))
NT = (((1,), (1,)), ((), ()))
NN = (((1,), (0,)), ((), ()))


def sds(shape, dtype):
    return jax.ShapeDtypeStruct(shape, dtype)


def mm(a, b, dims):
    return lax.dot_general(a, b, dims, preferred_element_type=F32)


def feature(x):
    return jnp.where(x > 0, x + 1.0, jnp.exp(jnp.minimum(x, 0.0)))


def slope(x):
    return jnp.where(x > 0, 1.0, jnp.exp(jnp.minimum(x, 0.0)))


def call(body, outs, ins, flops, name):
    read = sum(a.size * a.dtype.itemsize for a in ins)
    wrote = sum(s.size * s.dtype.itemsize for s in outs)
    return pl.pallas_call(
        body,
        out_shape=outs,
        in_specs=[SM if a.dtype == jnp.int32 else VM for a in ins],
        out_specs=[VM] * len(outs),
        name=name,
        compiler_params=pltpu.CompilerParams(vmem_limit_bytes=LIMIT),
        cost_estimate=LONG if name in ("query", "dnum", "numer") else SHORT,
    )(*ins)


def tiles(tokens, heads):
    for n in range(tokens // BLK):
        for h in range(heads):
            yield n * heads + h, slice(n * BLK, (n + 1) * BLK), slice(h * DH, (h + 1) * DH)


def mat(i):
    return slice(i * DH, (i + 1) * DH)


def states_body(k_ref, v_ref, kf_ref, st_ref):
    for i, r, c in tiles(k_ref.shape[0], k_ref.shape[1] // DH):
        kf = feature(k_ref[r, c].astype(F32)).astype(BF16)
        kf_ref[r, c] = kf
        st_ref[mat(i), :] = mm(kf, v_ref[r, c], TN).astype(BF16)


def begin_body(at_ref, k_ref, v_ref, w_ref, kf_ref, st_ref, far_ref):
    far_ref[...] = w_ref[...]
    states_body(k_ref, v_ref, kf_ref, st_ref)


def begin(at, k, v, w, width):
    tokens, cols = k.shape
    count = tokens // BLK * (cols // DH)
    whole = pl.BlockSpec((tokens, cols), lambda g, at: (0, 0))
    return pl.pallas_call(
        begin_body,
        out_shape=(
            sds((tokens, cols), BF16),
            sds((count * DH, DH), BF16),
            sds((width, DH), BF16),
        ),
        grid_spec=pltpu.PrefetchScalarGridSpec(
            num_scalar_prefetch=1,
            grid=(1,),
            in_specs=[whole, whole, pl.BlockSpec((width, DH), lambda g, at: (at[0], at[1]))],
            out_specs=[
                whole,
                pl.BlockSpec((count * DH, DH), lambda g, at: (0, 0)),
                pl.BlockSpec((width, DH), lambda g, at: (0, 0)),
            ],
        ),
        name="begin",
        compiler_params=pltpu.CompilerParams(vmem_limit_bytes=56 << 20),
        cost_estimate=SHORT,
    )(at, k, v, w)


def split_body(x_ref, *outs):
    rows = outs[0].shape[0]
    for i, out in enumerate(outs):
        out[...] = x_ref[i * rows : (i + 1) * rows, :]


def causal():
    rows = lax.broadcasted_iota(jnp.int32, (BLK, BLK), 0)
    cols = lax.broadcasted_iota(jnp.int32, (BLK, BLK), 1)
    return rows >= cols


def scores_body(q_ref, kf_ref, v_ref, qf_ref, sc_ref, intra_ref):
    keep = causal()
    for i, r, c in tiles(q_ref.shape[0], q_ref.shape[1] // DH):
        qf = feature(q_ref[r, c].astype(F32)).astype(BF16)
        qf_ref[r, c] = qf
        sc = jnp.where(keep, mm(qf, kf_ref[r, c], NT), 0.0).astype(BF16)
        sc_ref[i * BLK : (i + 1) * BLK, :] = sc
        intra_ref[r, c] = mm(sc, v_ref[r, c], NN)


def count(lay_ref, h, i, b):
    total = jnp.int32(0)
    for j in range(lay_ref.shape[2]):
        total = total + jnp.where(lay_ref[h, i, j] == b, 1, 0)
    return total.astype(F32)


def numer_body(dims, np_, *refs):
    nb, heads = dims
    pos_ref, base_ref, lay_ref = refs[:3]
    parts = refs[3 : 3 + np_]
    qf_ref, intra_ref, carried_ref, num_ref, attn_ref = refs[3 + np_ :]
    for i, r, c in tiles(qf_ref.shape[0], heads):
        n, h = divmod(i, heads)
        query_block = pos_ref[0] * nb + n
        total = jnp.zeros((DH, DH), F32)
        for s, part in enumerate(parts):
            for b in range(part.shape[0] // (heads * DH)):
                times = count(lay_ref, h, query_block, base_ref[s] + b)
                total = total + times * part[mat(b * heads + h), :].astype(F32)
        carried = total.astype(BF16)
        carried_ref[mat(i), :] = carried
        num = mm(qf_ref[r, c], carried, NN) + intra_ref[r, c]
        num_ref[r, c] = num
        rinv = lax.rsqrt(jnp.mean(num * num, axis=-1, keepdims=True) + EPS)
        attn_ref[r, c] = (num * rinv).astype(BF16)


def dnum_body(n_d, pos_ref, *refs):
    d_refs = refs[:n_d]
    num_ref, qf_ref, dnum_ref, cg_ref = refs[n_d:]
    heads = num_ref.shape[1] // DH
    for i, r, c in tiles(num_ref.shape[0], num_ref.shape[1] // DH):
        num = num_ref[r, c]
        grad = d_refs[0][r, c].astype(F32)
        if n_d == 3:
            same, sib = d_refs[1][r, :].astype(F32), d_refs[2][r, :].astype(F32)
            grad = grad + jnp.where(pos_ref[3] == i % heads, same, sib)
        grad = grad.astype(BF16).astype(F32)
        rinv = lax.rsqrt(jnp.mean(num * num, axis=-1, keepdims=True) + EPS)
        lean = jnp.mean(grad * num, axis=-1, keepdims=True)
        dnum = (rinv * grad - num * (rinv * rinv * rinv * lean)).astype(BF16)
        dnum_ref[r, c] = dnum
        cg_ref[mat(i), :] = mm(qf_ref[r, c], dnum, TN).astype(BF16)


def query_body(q_ref, qf_ref, kf_ref, v_ref, dnum_ref, carried_ref, sc_ref, dq_ref, dk_ref, dv_ref):
    keep = causal()
    for i, r, c in tiles(q_ref.shape[0], q_ref.shape[1] // DH):
        dnum = dnum_ref[r, c]
        pg = jnp.where(keep, mm(dnum, v_ref[r, c], NT), 0.0).astype(BF16)
        dq = mm(dnum, carried_ref[mat(i), :], NT) + mm(pg, kf_ref[r, c], NN)
        dq_ref[r, c] = (dq * slope(q_ref[r, c].astype(F32))).astype(BF16)
        dk_ref[r, c] = mm(pg, qf_ref[r, c], TN)
        dv_ref[r, c] = mm(sc_ref[i * BLK : (i + 1) * BLK, :], dnum, TN)


def key_body(dims, np_, *refs):
    nb, heads = dims
    pos_ref, base_ref, lay_ref = refs[:3]
    parts = refs[3 : 3 + np_]
    k_ref, kf_ref, v_ref, dkp_ref, dvp_ref, dk_ref, dv_ref = refs[3 + np_ :]
    for i, r, c in tiles(k_ref.shape[0], heads):
        n, h = divmod(i, heads)
        key_block = pos_ref[0] * nb + n
        total = jnp.zeros((DH, DH), F32)
        for s, part in enumerate(parts):
            for b in range(part.shape[0] // (heads * DH)):
                times = count(lay_ref, h, base_ref[s] + b, key_block)
                total = total + times * part[mat(b * heads + h), :].astype(F32)
        sg = total.astype(BF16)
        dk = mm(v_ref[r, c], sg, NT) + dkp_ref[r, c]
        dk_ref[r, c] = (dk * slope(k_ref[r, c].astype(F32))).astype(BF16)
        dv_ref[r, c] = (mm(kf_ref[r, c], sg, NN) + dvp_ref[r, c]).astype(BF16)


def own_body(at_ref, og_ref, w_ref, out_ref):
    part = mm(og_ref[...], w_ref[...], NN)

    @pl.when(pl.program_id(0) == 0)
    def _():
        out_ref[...] = part

    @pl.when(pl.program_id(0) > 0)
    def _():
        out_ref[...] += part


def own_partial(at, og, w, steps=4):
    tokens, width = og.shape
    cols = w.shape[1]
    bk = width // steps
    return pl.pallas_call(
        own_body,
        out_shape=sds((tokens, cols), F32),
        grid_spec=pltpu.PrefetchScalarGridSpec(
            num_scalar_prefetch=1,
            grid=(steps,),
            in_specs=[
                pl.BlockSpec((tokens, bk), lambda g, at: (0, g)),
                pl.BlockSpec((bk, cols), lambda g, at: (at[0] * steps + g, 0)),
            ],
            out_specs=pl.BlockSpec((tokens, cols), lambda g, at: (0, 0)),
        ),
        name="own_partial",
        compiler_params=pltpu.CompilerParams(vmem_limit_bytes=LIMIT),
        cost_estimate=SHORT,
    )(at, og, w)


def other_body(og_ref, og_sib_ref, w_ref, same_ref, sib_ref):
    same_ref[...] = mm(og_ref[...], w_ref[...], NN).astype(BF16)
    sib_ref[...] = mm(og_sib_ref[...], w_ref[...], NN).astype(BF16)


def weight_body(pos_ref, attn_ref, og_ref, og_sib_ref, *refs):
    *sib_refs, give_ref, keep_ref = refs
    step = sib_refs[0].shape[0]
    rows = give_ref.shape[1]
    parity, core = pos_ref[2], pos_ref[3]

    def part(pair):
        at = pl.ds(pl.multiple_of((2 * pair + core) * rows, rows), rows)
        total = mm(attn_ref[...], og_ref[:, at], TN)
        for i, sib in enumerate(sib_refs):
            total = total + mm(sib[...], og_sib_ref[i * step : (i + 1) * step, at], TN)
        return total

    give_ref[...] = part(1 - parity).astype(BF16)
    keep_ref[...] = part(parity)


def pair_body(keep_ref, got_ref, out_ref):
    out_ref[...] = (keep_ref[...] + got_ref[...].astype(F32)).astype(BF16)


def final_body(pos_ref, mine_ref, a_ref, b_ref, c_ref, out_ref):
    mine = jnp.where(pos_ref[1] > 0, mine_ref[...].astype(F32), 0.0)
    total = mine + a_ref[...].astype(F32) + b_ref[...].astype(F32) + c_ref[...].astype(F32)
    out_ref[...] = total.T


def after(x, *deps):
    return lax.optimization_barrier((x, *deps))[0]


def swap(x, axis):
    return lax.ppermute(x, axis, [(0, 1), (1, 0)])


def gather_parts(x, size):
    if size > 4:
        return [lax.all_gather(x, "seq", axis=0, tiled=True)]
    parts = [x]
    for shift in range(1, size):
        pairs = [(i, (i + shift) % size) for i in range(size)]
        parts.append(lax.ppermute(x, "seq", pairs))
    return parts


def per_device(queries, key_rows, value_rows, layout, out_weight, out_grad):
    seq_size = lax.axis_size("seq")
    head_size = lax.axis_size("head")
    dp_size = lax.axis_size("dp")
    z = lax.axis_index("seq").astype(jnp.int32)
    x = lax.axis_index("head").astype(jnp.int32)
    core = lax.axis_index("dp").astype(jnp.int32)
    heads = layout.shape[0]
    q, k, v, og = queries[0], key_rows[0], value_rows[0], out_grad[0]
    tokens, cols = q.shape
    nb = tokens // BLK
    dims = (nb, heads)
    paired = seq_size == 4 and head_size == 2 and dp_size == 2
    home = (z // 2 == x).astype(jnp.int32)
    pos = jnp.stack([z, home, z % 2, core])
    if seq_size > 4:
        bases = jnp.zeros((1,), jnp.int32)
    else:
        bases = ((z - jnp.arange(seq_size, dtype=jnp.int32)) % seq_size) * nb
    flat = sds((tokens, cols), F32)
    rows16 = sds((tokens, cols), BF16)
    mats = sds((nb * heads * DH, DH), BF16)
    unit = 2 * tokens * cols * DH

    if paired:
        width = og.shape[1]
        kf, st, far = begin(jnp.stack([1 - x, core]), k, v, out_weight, width)
        w_other = swap(far, "head")
        og_sib = swap(og, "dp")
    else:
        kf, st = call(states_body, (rows16, mats), (k, v), unit, "states")
    parts = gather_parts(st, seq_size)
    qf, sc, intra = call(
        scores_body,
        (rows16, sds((nb * heads * BLK, BLK), BF16), flat),
        (q, kf, v),
        4 * unit,
        "scores",
    )
    if not paired:
        og = lax.all_gather(og, "head", axis=1, tiled=True)
        d_own = jnp.dot(og, out_weight, preferred_element_type=F32)
    carried, num, attn = call(
        functools.partial(numer_body, dims, len(parts)),
        (mats, flat, rows16),
        (pos, bases, layout, *parts, qf, intra),
        unit,
        "numer",
    )
    if paired:
        attn_other = swap(attn, "head")
        column = sds((tokens, DH), BF16)
        sib_late = after(og_sib, attn)
        d_same, d_sib = call(other_body, (column, column), (og, sib_late, w_other), 0, "other")
        across = [(h * 2 + c, (1 - h) * 2 + 1 - c) for h in range(2) for c in range(2)]
        d_sib_sent = d_sib
        d_same = swap(d_same, "head")
        d_sib = lax.ppermute(d_sib, ("head", "dp"), across)
        block = (cols, width // 4)
        outs = (sds(block, BF16), sds(block, F32))
        neighbours = [(0, 1), (1, 0), (2, 3), (3, 2)]
        give_a, keep_a = call(weight_body, outs, (pos, attn, og, og_sib, swap(attn, "dp")), 0, "weight")
        got_a = lax.ppermute(give_a, "seq", neighbours)
        attn_other = after(attn_other, give_a, d_sib_sent)
        quarter = sds((tokens // 4, cols), BF16)
        pieces = call(split_body, (quarter,) * 4, (attn_other,), 0, "split")
        pieces = [swap(piece, "dp") for piece in pieces]
        give_b, keep_b = call(
            weight_body, outs, (pos, attn_other, og, og_sib, *pieces), 0, "weight"
        )
        got_b = lax.ppermute(give_b, "seq", neighbours)
        d_own = own_partial(x[None], after(og, give_b), out_weight)
        (mine,) = call(pair_body, (sds(keep_a.shape, BF16),), (keep_a, got_a), 0, "pair")
        d_parts = (d_own, after(d_same, give_b, mine), d_sib)
    else:
        d_parts = (d_own,)
    dnum, cg = call(
        functools.partial(dnum_body, len(d_parts)),
        (rows16, mats),
        (pos, *d_parts, num, qf),
        unit,
        "dnum",
    )
    if paired:
        two = lax.ppermute(cg, "seq", [(i, i ^ 2) for i in range(4)])
        one = lax.ppermute(cg, "seq", neighbours)
        cparts = [cg, one, two, lax.ppermute(after(two, one), "seq", neighbours)]
        cbases = (z ^ jnp.arange(4, dtype=jnp.int32)) * nb
    else:
        cparts, cbases = gather_parts(cg, seq_size), bases
    dq, dkp, dvp = call(
        query_body,
        (rows16, flat, flat),
        (q, qf, kf, v, dnum, carried, sc),
        9 * unit,
        "query",
    )
    dk, dv = call(
        functools.partial(key_body, dims, len(cparts)),
        (rows16, rows16),
        (pos, cbases, layout, *cparts, k, kf, v, dkp, dvp),
        2 * unit,
        "key",
    )
    if paired:
        (cross,) = call(pair_body, (sds(keep_b.shape, BF16),), (keep_b, got_b), 0, "pair")
        to_line, to_side, to_both = [], [], []
        for s in range(4):
            for h in range(2):
                if s // 2 == h:
                    to_side.append((s * 2 + h, s * 2 + 1 - h))
                else:
                    to_line.append((s * 2 + h, (s ^ 2) * 2 + h))
                    to_both.append((s * 2 + h, (s ^ 2) * 2 + 1 - h))
        axes = ("seq", "head")
        arrived = (
            lax.ppermute(mine, axes, to_line),
            lax.ppermute(cross, axes, to_both),
            lax.ppermute(cross, axes, to_side),
        )
        (weight_grad,) = call(
            final_body, (sds(mine.shape[::-1], F32),), (pos, mine, *arrived), 0, "final"
        )
    else:
        weight_grad = lax.psum_scatter(
            lax.dot_general(og, attn, TN, preferred_element_type=F32).astype(BF16),
            ("seq", "dp"),
            scatter_dimension=0,
            tiled=True,
        ).astype(F32)
    return attn[None], dq[None], dk[None], dv[None], weight_grad


def solution(mesh):
    rows = P(("groups", "dp"), "seq", "head")
    return jax.shard_map(
        per_device,
        mesh=mesh,
        in_specs=(rows, rows, rows, P("head", None, None), P(None, "head"), rows),
        out_specs=(rows, rows, rows, rows, P(("groups", "seq", "dp"), "head")),
        check_vma=False,
    )
```

```python
import functools

import jax
import jax.numpy as jnp
from jax import lax
from jax.experimental import pallas as pl
from jax.experimental.pallas import tpu as pltpu
from jax.sharding import PartitionSpec as P

DH = 128
BLK = 256
EPS = 1e-06
LIMIT = 16 << 20
BEGIN = 56 << 20
SHORT = pl.CostEstimate(flops=1, bytes_accessed=1, transcendentals=0)
LONG = pl.CostEstimate(flops=10**11, bytes_accessed=1, transcendentals=0)
F32 = jnp.float32
BF16 = jnp.bfloat16
VM = pl.BlockSpec(memory_space=pltpu.VMEM)
SM = pl.BlockSpec(memory_space=pltpu.SMEM)
TN = (((0,), (0,)), ((), ()))
NT = (((1,), (1,)), ((), ()))
NN = (((1,), (0,)), ((), ()))


def sds(shape, dtype):
    return jax.ShapeDtypeStruct(shape, dtype)


def mm(a, b, dims):
    return lax.dot_general(a, b, dims, preferred_element_type=F32)


def feature(x):
    return jnp.where(x > 0, x + 1.0, jnp.exp(jnp.minimum(x, 0.0)))


def slope(x):
    return jnp.where(x > 0, 1.0, jnp.exp(jnp.minimum(x, 0.0)))


def call(body, outs, ins, flops, name):
    read = sum(a.size * a.dtype.itemsize for a in ins)
    wrote = sum(s.size * s.dtype.itemsize for s in outs)
    return pl.pallas_call(
        body,
        out_shape=outs,
        in_specs=[SM if a.dtype == jnp.int32 else VM for a in ins],
        out_specs=[VM] * len(outs),
        name=name,
        compiler_params=pltpu.CompilerParams(vmem_limit_bytes=LIMIT),
        cost_estimate=LONG if name in ("query", "dnum", "numer") else SHORT,
    )(*ins)


def tiles(tokens, heads):
    for n in range(tokens // BLK):
        for h in range(heads):
            yield n * heads + h, slice(n * BLK, (n + 1) * BLK), slice(h * DH, (h + 1) * DH)


def mat(i):
    return slice(i * DH, (i + 1) * DH)


def states_body(k_ref, v_ref, kf_ref, st_ref):
    for i, r, c in tiles(k_ref.shape[0], k_ref.shape[1] // DH):
        kf = feature(k_ref[r, c].astype(F32)).astype(BF16)
        kf_ref[r, c] = kf
        st_ref[mat(i), :] = mm(kf, v_ref[r, c], TN).astype(BF16)


def begin_body(k_ref, v_ref, w_ref, kf_ref, st_ref, far_ref, k_in, v_in, far_in, sems):
    width, cols = far_ref.shape
    rows = pl.ds(pl.multiple_of((1 - lax.axis_index("head")) * width, width), width)
    lanes = pl.ds(pl.multiple_of(lax.axis_index("dp") * cols, cols), cols)
    far_copy = pltpu.make_async_copy(w_ref.at[rows, lanes], far_in, sems.at[0])
    k_copy = pltpu.make_async_copy(k_ref, k_in, sems.at[1])
    v_copy = pltpu.make_async_copy(v_ref, v_in, sems.at[2])
    k_copy.start()
    v_copy.start()
    far_copy.start()
    k_copy.wait()
    v_copy.wait()
    states_body(k_in, v_in, kf_ref, st_ref)
    far_copy.wait()
    out_copy = pltpu.make_async_copy(far_in, far_ref, sems.at[3])
    out_copy.start()
    out_copy.wait()


def begin(k, v, w, width):
    tokens, cols = k.shape
    count = tokens // BLK * (cols // DH)
    hbm = pl.BlockSpec(memory_space=pl.ANY)
    return pl.pallas_call(
        begin_body,
        out_shape=(
            sds((tokens, cols), BF16),
            sds((count * DH, DH), BF16),
            sds((width, DH), BF16),
        ),
        in_specs=[hbm, hbm, hbm],
        out_specs=[VM, VM, hbm],
        scratch_shapes=[
            pltpu.VMEM((tokens, cols), BF16),
            pltpu.VMEM((tokens, cols), BF16),
            pltpu.VMEM((width, DH), BF16),
            pltpu.SemaphoreType.DMA((4,)),
        ],
        name="begin",
        compiler_params=pltpu.CompilerParams(vmem_limit_bytes=BEGIN),
        cost_estimate=SHORT,
    )(k, v, w)


def split_body(x_ref, *outs):
    rows = outs[0].shape[0]
    for i, out in enumerate(outs):
        out[...] = x_ref[i * rows : (i + 1) * rows, :]


def causal():
    rows = lax.broadcasted_iota(jnp.int32, (BLK, BLK), 0)
    cols = lax.broadcasted_iota(jnp.int32, (BLK, BLK), 1)
    return rows >= cols


def scores_body(q_ref, kf_ref, v_ref, qf_ref, sc_ref, intra_ref):
    keep = causal()
    for i, r, c in tiles(q_ref.shape[0], q_ref.shape[1] // DH):
        qf = feature(q_ref[r, c].astype(F32)).astype(BF16)
        qf_ref[r, c] = qf
        sc = jnp.where(keep, mm(qf, kf_ref[r, c], NT), 0.0).astype(BF16)
        sc_ref[i * BLK : (i + 1) * BLK, :] = sc
        intra_ref[r, c] = mm(sc, v_ref[r, c], NN)


def count(lay_ref, h, i, b):
    total = jnp.int32(0)
    for j in range(lay_ref.shape[1]):
        total = total + jnp.where(lay_ref[h, j, i] == b, 1, 0)
    return total.astype(F32)


def in_order(z, s):
    return 0


def by_shift(z, s):
    size = lax.axis_size("seq")
    return lax.rem(z + size - s, size)


def by_flip(z, s):
    return lax.bitwise_xor(z, jnp.int32(s))


def numer_body(dims, np_, *refs):
    nb, heads, owner_of = dims
    lay_ref, *parts = refs[: 1 + np_]
    qf_ref, intra_ref, carried_ref, num_ref, attn_ref = refs[1 + np_ :]
    z = lax.axis_index("seq")
    for i, r, c in tiles(qf_ref.shape[0], heads):
        n, h = divmod(i, heads)
        query_block = z * nb + n
        total = jnp.zeros((DH, DH), F32)
        for s, part in enumerate(parts):
            for b in range(part.shape[0] // (heads * DH)):
                times = count(lay_ref, h, query_block, owner_of(z, s) * nb + b)
                total = total + times * part[mat(b * heads + h), :].astype(F32)
        carried = total.astype(BF16)
        carried_ref[mat(i), :] = carried
        num = mm(qf_ref[r, c], carried, NN) + intra_ref[r, c]
        num_ref[r, c] = num
        rinv = lax.rsqrt(jnp.mean(num * num, axis=-1, keepdims=True) + EPS)
        attn_ref[r, c] = (num * rinv).astype(BF16)


def dnum_body(n_d, *refs):
    d_refs = refs[:n_d]
    num_ref, qf_ref, dnum_ref, cg_ref = refs[n_d:]
    heads = num_ref.shape[1] // DH
    for i, r, c in tiles(num_ref.shape[0], num_ref.shape[1] // DH):
        num = num_ref[r, c]
        grad = d_refs[0][r, c].astype(F32)
        if n_d == 3:
            same, sib = d_refs[1][r, :].astype(F32), d_refs[2][r, :].astype(F32)
            grad = grad + jnp.where(lax.axis_index("dp") == i % heads, same, sib)
        grad = grad.astype(BF16).astype(F32)
        rinv = lax.rsqrt(jnp.mean(num * num, axis=-1, keepdims=True) + EPS)
        lean = jnp.mean(grad * num, axis=-1, keepdims=True)
        dnum = (rinv * grad - num * (rinv * rinv * rinv * lean)).astype(BF16)
        dnum_ref[r, c] = dnum
        cg_ref[mat(i), :] = mm(qf_ref[r, c], dnum, TN).astype(BF16)


def query_body(q_ref, qf_ref, kf_ref, v_ref, dnum_ref, carried_ref, sc_ref, dq_ref, dk_ref, dv_ref):
    keep = causal()
    for i, r, c in tiles(q_ref.shape[0], q_ref.shape[1] // DH):
        dnum = dnum_ref[r, c]
        pg = jnp.where(keep, mm(dnum, v_ref[r, c], NT), 0.0).astype(BF16)
        dq = mm(dnum, carried_ref[mat(i), :], NT) + mm(pg, kf_ref[r, c], NN)
        dq_ref[r, c] = (dq * slope(q_ref[r, c].astype(F32))).astype(BF16)
        dk_ref[r, c] = mm(pg, qf_ref[r, c], TN)
        dv_ref[r, c] = mm(sc_ref[i * BLK : (i + 1) * BLK, :], dnum, TN)


def key_body(dims, np_, *refs):
    nb, heads, owner_of = dims
    lay_ref, *parts = refs[: 1 + np_]
    k_ref, kf_ref, v_ref, dkp_ref, dvp_ref, dk_ref, dv_ref = refs[1 + np_ :]
    z = lax.axis_index("seq")
    for i, r, c in tiles(k_ref.shape[0], heads):
        n, h = divmod(i, heads)
        key_block = z * nb + n
        total = jnp.zeros((DH, DH), F32)
        for s, part in enumerate(parts):
            for b in range(part.shape[0] // (heads * DH)):
                times = count(lay_ref, h, owner_of(z, s) * nb + b, key_block)
                total = total + times * part[mat(b * heads + h), :].astype(F32)
        sg = total.astype(BF16)
        dk = mm(v_ref[r, c], sg, NT) + dkp_ref[r, c]
        dk_ref[r, c] = (dk * slope(k_ref[r, c].astype(F32))).astype(BF16)
        dv_ref[r, c] = (mm(kf_ref[r, c], sg, NN) + dvp_ref[r, c]).astype(BF16)


def own_body(og_ref, w_ref, out_ref, w_in, sem):
    width = w_in.shape[0]
    rows = pl.ds(pl.multiple_of(lax.axis_index("head") * width, width), width)
    copy = pltpu.make_async_copy(w_ref.at[rows, :], w_in, sem)
    copy.start()
    copy.wait()
    out_ref[...] = mm(og_ref[...], w_in[...], NN)


def own_partial(og, w):
    tokens, width = og.shape
    cols = w.shape[1]
    return pl.pallas_call(
        own_body,
        out_shape=sds((tokens, cols), F32),
        in_specs=[VM, pl.BlockSpec(memory_space=pl.ANY)],
        out_specs=VM,
        scratch_shapes=[pltpu.VMEM((width, cols), BF16), pltpu.SemaphoreType.DMA],
        name="own_partial",
        compiler_params=pltpu.CompilerParams(vmem_limit_bytes=LIMIT),
        cost_estimate=SHORT,
    )(og, w)


def other_body(og_ref, og_sib_ref, w_ref, same_ref, sib_ref):
    same_ref[...] = mm(og_ref[...], w_ref[...], NN).astype(BF16)
    sib_ref[...] = mm(og_sib_ref[...], w_ref[...], NN).astype(BF16)


def weight_body(attn_ref, og_ref, og_sib_ref, *refs):
    *sib_refs, give_ref, keep_ref = refs
    step = sib_refs[0].shape[0]
    rows = give_ref.shape[1]
    parity, core = lax.rem(lax.axis_index("seq"), 2), lax.axis_index("dp")

    def part(pair):
        at = pl.ds(pl.multiple_of((2 * pair + core) * rows, rows), rows)
        total = mm(attn_ref[...], og_ref[:, at], TN)
        for i, sib in enumerate(sib_refs):
            total = total + mm(sib[...], og_sib_ref[i * step : (i + 1) * step, at], TN)
        return total

    give_ref[...] = part(1 - parity).astype(BF16)
    keep_ref[...] = part(parity)


def pair_body(keep_ref, got_ref, out_ref):
    out_ref[...] = (keep_ref[...] + got_ref[...].astype(F32)).astype(BF16)


def final_body(mine_ref, a_ref, b_ref, c_ref, out_ref):
    home = lax.axis_index("seq") // 2 == lax.axis_index("head")
    mine = jnp.where(home, mine_ref[...].astype(F32), 0.0)
    total = mine + a_ref[...].astype(F32) + b_ref[...].astype(F32) + c_ref[...].astype(F32)
    out_ref[...] = total.T


def after(x, *deps):
    return lax.optimization_barrier((x, *deps))[0]


def swap(x, axis):
    return lax.ppermute(x, axis, [(0, 1), (1, 0)])


def gather_parts(x, size):
    if size > 4:
        return [lax.all_gather(x, "seq", axis=0, tiled=True)]
    parts = [x]
    for shift in range(1, size):
        pairs = [(i, (i + shift) % size) for i in range(size)]
        parts.append(lax.ppermute(x, "seq", pairs))
    return parts


def per_device(queries, key_rows, value_rows, layout, out_weight, out_grad):
    seq_size = lax.axis_size("seq")
    head_size = lax.axis_size("head")
    dp_size = lax.axis_size("dp")
    heads = layout.shape[0]
    q, k, v, og = queries[0], key_rows[0], value_rows[0], out_grad[0]
    tokens, cols = q.shape
    nb = tokens // BLK
    paired = seq_size == 4 and head_size == 2 and dp_size == 2
    lay = layout.transpose(0, 2, 1)
    first_owner = in_order if seq_size > 4 else by_shift
    flat = sds((tokens, cols), F32)
    rows16 = sds((tokens, cols), BF16)
    mats = sds((nb * heads * DH, DH), BF16)
    unit = 2 * tokens * cols * DH

    if paired:
        width = og.shape[1]
        kf, st, far = begin(k, v, out_weight, width)
        w_other = swap(far, "head")
        og_sib = swap(og, "dp")
    else:
        kf, st = call(states_body, (rows16, mats), (k, v), unit, "states")
    parts = gather_parts(st, seq_size)
    qf, sc, intra = call(
        scores_body,
        (rows16, sds((nb * heads * BLK, BLK), BF16), flat),
        (q, kf, v),
        4 * unit,
        "scores",
    )
    if not paired:
        og = lax.all_gather(og, "head", axis=1, tiled=True)
        d_own = jnp.dot(og, out_weight, preferred_element_type=F32)
    carried, num, attn = call(
        functools.partial(numer_body, (nb, heads, first_owner), len(parts)),
        (mats, flat, rows16),
        (lay, *parts, qf, intra),
        unit,
        "numer",
    )
    if paired:
        attn_other = swap(attn, "head")
        column = sds((tokens, DH), BF16)
        sib_late = after(og_sib, attn)
        d_same, d_sib = call(other_body, (column, column), (og, sib_late, w_other), 0, "other")
        across = [(h * 2 + c, (1 - h) * 2 + 1 - c) for h in range(2) for c in range(2)]
        d_sib_sent = d_sib
        d_same = swap(d_same, "head")
        d_sib = lax.ppermute(d_sib, ("head", "dp"), across)
        block = (cols, width // 4)
        outs = (sds(block, BF16), sds(block, F32))
        neighbours = [(0, 1), (1, 0), (2, 3), (3, 2)]
        give_a, keep_a = call(weight_body, outs, (attn, og, og_sib, swap(attn, "dp")), 0, "weight")
        got_a = lax.ppermute(give_a, "seq", neighbours)
        attn_other = after(attn_other, give_a, d_sib_sent)
        quarter = sds((tokens // 4, cols), BF16)
        pieces = call(split_body, (quarter,) * 4, (attn_other,), 0, "split")
        pieces = [swap(piece, "dp") for piece in pieces]
        give_b, keep_b = call(
            weight_body, outs, (attn_other, og, og_sib, *pieces), 0, "weight"
        )
        got_b = lax.ppermute(give_b, "seq", neighbours)
        d_own = own_partial(after(og, give_b), out_weight)
        (mine,) = call(pair_body, (sds(keep_a.shape, BF16),), (keep_a, got_a), 0, "pair")
        d_parts = (d_own, after(d_same, give_b, mine), d_sib)
    else:
        d_parts = (d_own,)
    dnum, cg = call(
        functools.partial(dnum_body, len(d_parts)),
        (rows16, mats),
        (*d_parts, num, qf),
        unit,
        "dnum",
    )
    if paired:
        two = lax.ppermute(cg, "seq", [(i, i ^ 2) for i in range(4)])
        one = lax.ppermute(cg, "seq", neighbours)
        cparts = [cg, one, two, lax.ppermute(after(two, one), "seq", neighbours)]
        second_owner = by_flip
    else:
        cparts, second_owner = gather_parts(cg, seq_size), first_owner
    dq, dkp, dvp = call(
        query_body,
        (rows16, flat, flat),
        (q, qf, kf, v, dnum, carried, sc),
        9 * unit,
        "query",
    )
    dk, dv = call(
        functools.partial(key_body, (nb, heads, second_owner), len(cparts)),
        (rows16, rows16),
        (lay, *cparts, k, kf, v, dkp, dvp),
        2 * unit,
        "key",
    )
    if paired:
        (cross,) = call(pair_body, (sds(keep_b.shape, BF16),), (keep_b, got_b), 0, "pair")
        to_line, to_side, to_both = [], [], []
        for s in range(4):
            for h in range(2):
                if s // 2 == h:
                    to_side.append((s * 2 + h, s * 2 + 1 - h))
                else:
                    to_line.append((s * 2 + h, (s ^ 2) * 2 + h))
                    to_both.append((s * 2 + h, (s ^ 2) * 2 + 1 - h))
        axes = ("seq", "head")
        arrived = (
            lax.ppermute(mine, axes, to_line),
            lax.ppermute(cross, axes, to_both),
            lax.ppermute(cross, axes, to_side),
        )
        (weight_grad,) = call(
            final_body, (sds(mine.shape[::-1], F32),), (mine, *arrived), 0, "final"
        )
    else:
        weight_grad = lax.psum_scatter(
            lax.dot_general(og, attn, TN, preferred_element_type=F32).astype(BF16),
            ("seq", "dp"),
            scatter_dimension=0,
            tiled=True,
        ).astype(F32)
    return attn[None], dq[None], dk[None], dv[None], weight_grad


def solution(mesh):
    rows = P(("groups", "dp"), "seq", "head")
    return jax.shard_map(
        per_device,
        mesh=mesh,
        in_specs=(rows, rows, rows, P("head", None, None), P(None, "head"), rows),
        out_specs=(rows, rows, rows, rows, P(("groups", "seq", "dp"), "head")),
        check_vma=False,
    )
```

```python
import functools

import jax
import jax.numpy as jnp
from jax import lax
from jax.experimental import pallas as pl
from jax.experimental.pallas import tpu as pltpu
from jax.sharding import PartitionSpec as P

DH = 128
BLK = 256
EPS = 1e-06
LIMIT = 16 << 20
BEGIN = 56 << 20
SHORT = pl.CostEstimate(flops=1, bytes_accessed=1, transcendentals=0)
LONG = pl.CostEstimate(flops=10**11, bytes_accessed=1, transcendentals=0)
F32 = jnp.float32
BF16 = jnp.bfloat16
VM = pl.BlockSpec(memory_space=pltpu.VMEM)
SM = pl.BlockSpec(memory_space=pltpu.SMEM)
TN = (((0,), (0,)), ((), ()))
NT = (((1,), (1,)), ((), ()))
NN = (((1,), (0,)), ((), ()))


def sds(shape, dtype):
    return jax.ShapeDtypeStruct(shape, dtype)


def mm(a, b, dims):
    return lax.dot_general(a, b, dims, preferred_element_type=F32)


def feature(x):
    return jnp.where(x > 0, x + 1.0, jnp.exp(jnp.minimum(x, 0.0)))


def slope(x):
    return jnp.where(x > 0, 1.0, jnp.exp(jnp.minimum(x, 0.0)))


def call(body, outs, ins, flops, name):
    read = sum(a.size * a.dtype.itemsize for a in ins)
    wrote = sum(s.size * s.dtype.itemsize for s in outs)
    return pl.pallas_call(
        body,
        out_shape=outs,
        in_specs=[SM if a.dtype == jnp.int32 else VM for a in ins],
        out_specs=[VM] * len(outs),
        name=name,
        compiler_params=pltpu.CompilerParams(vmem_limit_bytes=LIMIT),
        cost_estimate=LONG if name in ("query", "dnum", "numer") else SHORT,
    )(*ins)


def tiles(tokens, heads):
    for n in range(tokens // BLK):
        for h in range(heads):
            yield n * heads + h, slice(n * BLK, (n + 1) * BLK), slice(h * DH, (h + 1) * DH)


def mat(i):
    return slice(i * DH, (i + 1) * DH)


def states_body(k_ref, v_ref, kf_ref, st_ref):
    for i, r, c in tiles(k_ref.shape[0], k_ref.shape[1] // DH):
        kf = feature(k_ref[r, c].astype(F32)).astype(BF16)
        kf_ref[r, c] = kf
        st_ref[mat(i), :] = mm(kf, v_ref[r, c], TN).astype(BF16)


def begin_body(k_ref, v_ref, w_ref, kf_ref, st_ref, far_ref, k_in, v_in, far_in, sems):
    width, cols = far_ref.shape
    rows = pl.ds(pl.multiple_of((1 - lax.axis_index("head")) * width, width), width)
    lanes = pl.ds(pl.multiple_of(lax.axis_index("dp") * cols, cols), cols)
    far_copy = pltpu.make_async_copy(w_ref.at[rows, lanes], far_in, sems.at[0])
    k_copy = pltpu.make_async_copy(k_ref, k_in, sems.at[1])
    v_copy = pltpu.make_async_copy(v_ref, v_in, sems.at[2])
    k_copy.start()
    v_copy.start()
    far_copy.start()
    k_copy.wait()
    v_copy.wait()
    states_body(k_in, v_in, kf_ref, st_ref)
    far_copy.wait()
    out_copy = pltpu.make_async_copy(far_in, far_ref, sems.at[3])
    out_copy.start()
    out_copy.wait()


def begin(k, v, w, width):
    tokens, cols = k.shape
    count = tokens // BLK * (cols // DH)
    hbm = pl.BlockSpec(memory_space=pl.ANY)
    return pl.pallas_call(
        begin_body,
        out_shape=(
            sds((tokens, cols), BF16),
            sds((count * DH, DH), BF16),
            sds((width, DH), BF16),
        ),
        in_specs=[hbm, hbm, hbm],
        out_specs=[VM, VM, hbm],
        scratch_shapes=[
            pltpu.VMEM((tokens, cols), BF16),
            pltpu.VMEM((tokens, cols), BF16),
            pltpu.VMEM((width, DH), BF16),
            pltpu.SemaphoreType.DMA((4,)),
        ],
        name="begin",
        compiler_params=pltpu.CompilerParams(vmem_limit_bytes=BEGIN),
        cost_estimate=SHORT,
    )(k, v, w)


def split_body(x_ref, *outs):
    at = 0
    for out in outs:
        out[...] = x_ref[at : at + out.shape[0], :]
        at += out.shape[0]


def join_body(*refs):
    *parts, out_ref = refs
    rows = parts[0].shape[0]
    for i, part in enumerate(parts):
        out_ref[i * rows : (i + 1) * rows, :] = part[...]


def causal():
    rows = lax.broadcasted_iota(jnp.int32, (BLK, BLK), 0)
    cols = lax.broadcasted_iota(jnp.int32, (BLK, BLK), 1)
    return rows >= cols


def scores_body(q_ref, kf_ref, v_ref, qf_ref, sc_ref, intra_ref):
    keep = causal()
    for i, r, c in tiles(q_ref.shape[0], q_ref.shape[1] // DH):
        qf = feature(q_ref[r, c].astype(F32)).astype(BF16)
        qf_ref[r, c] = qf
        sc = jnp.where(keep, mm(qf, kf_ref[r, c], NT), 0.0).astype(BF16)
        sc_ref[i * BLK : (i + 1) * BLK, :] = sc
        intra_ref[r, c] = mm(sc, v_ref[r, c], NN)


def count(lay_ref, h, i, b):
    total = jnp.int32(0)
    for j in range(lay_ref.shape[1]):
        total = total + jnp.where(lay_ref[h, j, i] == b, 1, 0)
    return total.astype(F32)


def in_order(z, s):
    return s


def by_shift(z, s):
    size = lax.axis_size("seq")
    return lax.rem(z + size - s, size)


def by_flip(z, s):
    return lax.bitwise_xor(z, jnp.int32((0, 2, 1, 3)[s]))


def views(parts, rows):
    return [p.at[i * rows : (i + 1) * rows] for p in parts for i in range(p.shape[0] // rows)]


def numer_body(dims, np_, *refs):
    nb, heads, owner_of = dims
    lay_ref, *parts = refs[: 1 + np_]
    qf_ref, intra_ref, carried_ref, num_ref, attn_ref = refs[1 + np_ :]
    z = lax.axis_index("seq")
    for i, r, c in tiles(qf_ref.shape[0], heads):
        n, h = divmod(i, heads)
        query_block = z * nb + n
        total = jnp.zeros((DH, DH), F32)
        for s, part in enumerate(views(parts, nb * heads * DH)):
            for b in range(nb):
                times = count(lay_ref, h, query_block, owner_of(z, s) * nb + b)
                total = total + times * part[mat(b * heads + h), :].astype(F32)
        carried = total.astype(BF16)
        carried_ref[mat(i), :] = carried
        num = mm(qf_ref[r, c], carried, NN) + intra_ref[r, c]
        num_ref[r, c] = num
        rinv = lax.rsqrt(jnp.mean(num * num, axis=-1, keepdims=True) + EPS)
        attn_ref[r, c] = (num * rinv).astype(BF16)


def dnum_body(n_d, *refs):
    d_refs = refs[:n_d]
    num_ref, qf_ref, dnum_ref, cg_ref = refs[n_d:]
    heads = num_ref.shape[1] // DH
    for i, r, c in tiles(num_ref.shape[0], num_ref.shape[1] // DH):
        num = num_ref[r, c]
        grad = d_refs[0][r, c].astype(F32)
        if n_d == 3:
            same, sib = d_refs[1][r, :].astype(F32), d_refs[2][r, :].astype(F32)
            grad = grad + jnp.where(lax.axis_index("dp") == i % heads, same, sib)
        grad = grad.astype(BF16).astype(F32)
        rinv = lax.rsqrt(jnp.mean(num * num, axis=-1, keepdims=True) + EPS)
        lean = jnp.mean(grad * num, axis=-1, keepdims=True)
        dnum = (rinv * grad - num * (rinv * rinv * rinv * lean)).astype(BF16)
        dnum_ref[r, c] = dnum
        cg_ref[mat(i), :] = mm(qf_ref[r, c], dnum, TN).astype(BF16)


def query_body(q_ref, qf_ref, kf_ref, v_ref, dnum_ref, carried_ref, sc_ref, dq_ref, dk_ref, dv_ref):
    keep = causal()
    for i, r, c in tiles(q_ref.shape[0], q_ref.shape[1] // DH):
        dnum = dnum_ref[r, c]
        pg = jnp.where(keep, mm(dnum, v_ref[r, c], NT), 0.0).astype(BF16)
        dq = mm(dnum, carried_ref[mat(i), :], NT) + mm(pg, kf_ref[r, c], NN)
        dq_ref[r, c] = (dq * slope(q_ref[r, c].astype(F32))).astype(BF16)
        dk_ref[r, c] = mm(pg, qf_ref[r, c], TN)
        dv_ref[r, c] = mm(sc_ref[i * BLK : (i + 1) * BLK, :], dnum, TN)


def key_body(dims, np_, *refs):
    nb, heads, owner_of = dims
    lay_ref, *parts = refs[: 1 + np_]
    k_ref, kf_ref, v_ref, dkp_ref, dvp_ref, dk_ref, dv_ref = refs[1 + np_ :]
    z = lax.axis_index("seq")
    for i, r, c in tiles(k_ref.shape[0], heads):
        n, h = divmod(i, heads)
        key_block = z * nb + n
        total = jnp.zeros((DH, DH), F32)
        for s, part in enumerate(views(parts, nb * heads * DH)):
            for b in range(nb):
                times = count(lay_ref, h, owner_of(z, s) * nb + b, key_block)
                total = total + times * part[mat(b * heads + h), :].astype(F32)
        sg = total.astype(BF16)
        dk = mm(v_ref[r, c], sg, NT) + dkp_ref[r, c]
        dk_ref[r, c] = (dk * slope(k_ref[r, c].astype(F32))).astype(BF16)
        dv_ref[r, c] = (mm(kf_ref[r, c], sg, NN) + dvp_ref[r, c]).astype(BF16)


def own_body(og_ref, w_ref, out_ref, w_in, sem):
    width = w_in.shape[0]
    rows = pl.ds(pl.multiple_of(lax.axis_index("head") * width, width), width)
    copy = pltpu.make_async_copy(w_ref.at[rows, :], w_in, sem)
    copy.start()
    copy.wait()
    out_ref[...] = mm(og_ref[...], w_in[...], NN)


def own_partial(og, w):
    tokens, width = og.shape
    cols = w.shape[1]
    return pl.pallas_call(
        own_body,
        out_shape=sds((tokens, cols), F32),
        in_specs=[VM, pl.BlockSpec(memory_space=pl.ANY)],
        out_specs=VM,
        scratch_shapes=[pltpu.VMEM((width, cols), BF16), pltpu.SemaphoreType.DMA],
        name="own_partial",
        compiler_params=pltpu.CompilerParams(vmem_limit_bytes=LIMIT),
        cost_estimate=SHORT,
    )(og, w)


def other_body(og_ref, og_sib_ref, w_ref, same_ref, sib_ref):
    same_ref[...] = mm(og_ref[...], w_ref[...], NN).astype(BF16)
    sib_ref[...] = mm(og_sib_ref[...], w_ref[...], NN).astype(BF16)


def weight_body(n_out, attn_ref, og_ref, og_sib_ref, *refs):
    sibs, outs = refs[:-n_out], refs[-n_out:]
    rows = outs[0].shape[1]
    pieces = len(outs) // 2
    parity, core = lax.rem(lax.axis_index("seq"), 2), lax.axis_index("dp")
    for which, pair in enumerate((1 - parity, parity)):
        at = pl.ds(pl.multiple_of((2 * pair + core) * rows, rows), rows)
        total = mm(attn_ref[...], og_ref[:, at], TN)
        row = 0
        for sib in sibs:
            total = total + mm(sib[...], og_sib_ref[row : row + sib.shape[0], at], TN)
            row += sib.shape[0]
        for i in range(pieces):
            out = outs[which * pieces + i]
            size = out.shape[0]
            out[...] = total[i * size : (i + 1) * size, :].astype(out.dtype)


def pair_body(keep_ref, got_ref, out_ref):
    out_ref[...] = (keep_ref[...] + got_ref[...].astype(F32)).astype(BF16)


def cross_body(i, keep_ref, got_ref, mine_ref, send_ref, stay_ref):
    home = lax.axis_index("seq") // 2 == lax.axis_index("head")
    cross = (keep_ref[...].astype(F32) + got_ref[...].astype(F32)).astype(BF16)
    mine = mine_ref[mat(i), :]
    send_ref[...] = jnp.where(home, cross, mine)
    stay_ref[...] = jnp.where(home, mine, cross)


def final_body(*refs):
    *got, out_ref = refs
    for i in range(len(got) // 2):
        total = got[2 * i][...].astype(F32) + got[2 * i + 1][...].astype(F32)
        out_ref[:, mat(i)] = total.T


def after(x, *deps):
    return lax.optimization_barrier((x, *deps))[0]


def swap(x, axis):
    return lax.ppermute(x, axis, [(0, 1), (1, 0)])


def gather_parts(x, size):
    if size > 4:
        return [lax.all_gather(x, "seq", axis=0, tiled=True)]
    parts = [x]
    for shift in range(1, size):
        pairs = [(i, (i + shift) % size) for i in range(size)]
        parts.append(lax.ppermute(x, "seq", pairs))
    return parts


def per_device(queries, key_rows, value_rows, layout, out_weight, out_grad):
    seq_size = lax.axis_size("seq")
    head_size = lax.axis_size("head")
    dp_size = lax.axis_size("dp")
    heads = layout.shape[0]
    q, k, v, og = queries[0], key_rows[0], value_rows[0], out_grad[0]
    tokens, cols = q.shape
    nb = tokens // BLK
    paired = seq_size == 4 and head_size == 2 and dp_size == 2
    lay = layout.transpose(0, 2, 1)
    first_owner = in_order if seq_size > 4 else by_shift
    flat = sds((tokens, cols), F32)
    rows16 = sds((tokens, cols), BF16)
    mats = sds((nb * heads * DH, DH), BF16)
    unit = 2 * tokens * cols * DH

    if paired:
        width = og.shape[1]
        kf, st, far = begin(k, v, out_weight, width)
        w_other = swap(far, "head")
        og_sib = swap(og, "dp")
    else:
        kf, st = call(states_body, (rows16, mats), (k, v), unit, "states")
    parts = gather_parts(st, seq_size)
    qf, sc, intra = call(
        scores_body,
        (rows16, sds((nb * heads * BLK, BLK), BF16), flat),
        (q, kf, v),
        4 * unit,
        "scores",
    )
    if not paired:
        og = lax.all_gather(og, "head", axis=1, tiled=True)
        d_own = jnp.dot(og, out_weight, preferred_element_type=F32)
    if paired:
        column = sds((tokens, DH), BF16)
        d_same, d_sib = call(other_body, (column, column), (after(og, qf), og_sib, w_other), 0, "other")
        across = [(h * 2 + c, (1 - h) * 2 + 1 - c) for h in range(2) for c in range(2)]
        intra = after(intra, d_sib)
        d_same = swap(d_same, "head")
        d_sib = lax.ppermute(d_sib, ("head", "dp"), across)
    carried, num, attn = call(
        functools.partial(numer_body, (nb, heads, first_owner), len(parts)),
        (mats, flat, rows16),
        (lay, *parts, qf, intra),
        unit,
        "numer",
    )
    if paired:
        attn_other = swap(attn, "head")
        attn_sib = swap(attn, "dp")
        d_own = own_partial(after(og, attn), out_weight)
        d_parts = (d_own, d_same, d_sib)
    else:
        d_parts = (d_own,)
    dnum, cg = call(
        functools.partial(dnum_body, len(d_parts)),
        (rows16, mats),
        (*d_parts, num, qf),
        unit,
        "dnum",
    )
    if paired:
        neighbours = [(0, 1), (1, 0), (2, 3), (3, 2)]
        two = lax.ppermute(cg, "seq", [(i, i ^ 2) for i in range(4)])
        block, half = (cols, width // 4), sds((DH, width // 4), BF16)
        give, keep = call(
            functools.partial(weight_body, 2),
            (sds(block, BF16), sds(block, F32)),
            (after(attn, cg), og, og_sib, attn_sib),
            0,
            "weight",
        )
        got = lax.ppermute(give, "seq", neighbours)
        attn_other = after(attn_other, give)
        third = tokens // 48 * 16
        sizes = (third, third, tokens - 2 * third)
        cuts = call(split_body, tuple(sds((n, cols), BF16) for n in sizes), (attn_other,), 0, "split")
        pieces = call(
            functools.partial(weight_body, 2 * heads),
            (half,) * (2 * heads),
            (attn_other, og, og_sib, *[swap(cut, "dp") for cut in cuts]),
            0,
            "weight",
        )
        give_b, keep_b = pieces[:heads], pieces[heads:]
        beside = [((s ^ 1) * 2 + 1 - h, s * 2 + h) for s in range(4) for h in range(2)]
        crossed = [
            (swap(k, "head"), lax.ppermute(g, ("seq", "head"), beside)) for k, g in zip(keep_b, give_b)
        ]
        (joined,) = call(
            join_body, (sds((2 * cg.shape[0], DH), BF16),), (cg, after(two, give_b[0])), 0, "join"
        )
        cparts = [cg, two, lax.ppermute(joined, "seq", neighbours)]
        second_owner = by_flip
        (mine,) = call(pair_body, (sds(block, BF16),), (keep, got), 0, "pair")
    else:
        cparts, second_owner = gather_parts(cg, seq_size), first_owner
    dq, dkp, dvp = call(
        query_body,
        (rows16, flat, flat),
        (q, qf, kf, v, dnum, carried, sc),
        9 * unit,
        "query",
    )
    dk, dv = call(
        functools.partial(key_body, (nb, heads, second_owner), len(cparts)),
        (rows16, rows16),
        (lay, *cparts, k, kf, v, dkp, dvp),
        2 * unit,
        "key",
    )
    if paired:
        sums = []
        for i, (k, g) in enumerate(crossed):
            send, stay = call(functools.partial(cross_body, i), (half, half), (k, g, mine), 0, "cross")
            sums += [stay, lax.ppermute(send, "seq", [(s, s ^ 2) for s in range(4)])]
        (weight_grad,) = call(final_body, (sds(block[::-1], F32),), tuple(sums), 0, "final")
    else:
        weight_grad = lax.psum_scatter(
            lax.dot_general(og, attn, TN, preferred_element_type=F32).astype(BF16),
            ("seq", "dp"),
            scatter_dimension=0,
            tiled=True,
        ).astype(F32)
    return attn[None], dq[None], dk[None], dv[None], weight_grad


def solution(mesh):
    rows = P(("groups", "dp"), "seq", "head")
    return jax.shard_map(
        per_device,
        mesh=mesh,
        in_specs=(rows, rows, rows, P("head", None, None), P(None, "head"), rows),
        out_specs=(rows, rows, rows, rows, P(("groups", "seq", "dp"), "head")),
        check_vma=False,
    )
```

```python
import functools

import jax
import jax.numpy as jnp
from jax import lax
from jax.experimental import pallas as pl
from jax.experimental.pallas import tpu as pltpu
from jax.sharding import PartitionSpec as P

DH = 128
BLK = 256
EPS = 1e-06
LIMIT = 16 << 20
BEGIN = 56 << 20
SHORT = pl.CostEstimate(flops=1, bytes_accessed=1, transcendentals=0)
LONG = pl.CostEstimate(flops=10**11, bytes_accessed=1, transcendentals=0)
F32 = jnp.float32
BF16 = jnp.bfloat16
VM = pl.BlockSpec(memory_space=pltpu.VMEM)
SM = pl.BlockSpec(memory_space=pltpu.SMEM)
TN = (((0,), (0,)), ((), ()))
NT = (((1,), (1,)), ((), ()))
NN = (((1,), (0,)), ((), ()))


def sds(shape, dtype):
    return jax.ShapeDtypeStruct(shape, dtype)


def mm(a, b, dims):
    return lax.dot_general(a, b, dims, preferred_element_type=F32)


def feature(x):
    return jnp.where(x > 0, x + 1.0, jnp.exp(jnp.minimum(x, 0.0)))


def slope(x):
    return jnp.where(x > 0, 1.0, jnp.exp(jnp.minimum(x, 0.0)))


def call(body, outs, ins, flops, name):
    read = sum(a.size * a.dtype.itemsize for a in ins)
    wrote = sum(s.size * s.dtype.itemsize for s in outs)
    return pl.pallas_call(
        body,
        out_shape=outs,
        in_specs=[SM if a.dtype == jnp.int32 else VM for a in ins],
        out_specs=[VM] * len(outs),
        name=name,
        compiler_params=pltpu.CompilerParams(vmem_limit_bytes=LIMIT),
        cost_estimate=LONG if name in ("query", "dnum", "numer") else SHORT,
    )(*ins)


def tiles(tokens, heads):
    for n in range(tokens // BLK):
        for h in range(heads):
            yield n * heads + h, slice(n * BLK, (n + 1) * BLK), slice(h * DH, (h + 1) * DH)


def mat(i):
    return slice(i * DH, (i + 1) * DH)


def states_body(k_ref, v_ref, kf_ref, st_ref):
    for i, r, c in tiles(k_ref.shape[0], k_ref.shape[1] // DH):
        kf = feature(k_ref[r, c].astype(F32)).astype(BF16)
        kf_ref[r, c] = kf
        st_ref[mat(i), :] = mm(kf, v_ref[r, c], TN).astype(BF16)


def far_body(w_ref, far_ref, sem):
    width, cols = far_ref.shape
    rows = pl.ds(pl.multiple_of((1 - lax.axis_index("head")) * width, width), width)
    lanes = pl.ds(pl.multiple_of(lax.axis_index("dp") * cols, cols), cols)
    copy = pltpu.make_async_copy(w_ref.at[rows, lanes], far_ref, sem)
    copy.start()
    copy.wait()


def far_rows(w, width):
    return pl.pallas_call(
        far_body,
        out_shape=sds((width, DH), BF16),
        in_specs=[pl.BlockSpec(memory_space=pl.ANY)],
        out_specs=VM,
        scratch_shapes=[pltpu.SemaphoreType.DMA],
        name="far",
        compiler_params=pltpu.CompilerParams(vmem_limit_bytes=BEGIN),
        cost_estimate=SHORT,
    )(w)


def begin_body(k_ref, v_ref, kf_ref, st_ref, k_in, v_in, sems):
    k_copy = pltpu.make_async_copy(k_ref, k_in, sems.at[0])
    v_copy = pltpu.make_async_copy(v_ref, v_in, sems.at[1])
    k_copy.start()
    v_copy.start()
    k_copy.wait()
    v_copy.wait()
    states_body(k_in, v_in, kf_ref, st_ref)


def begin(k, v):
    tokens, cols = k.shape
    count = tokens // BLK * (cols // DH)
    hbm = pl.BlockSpec(memory_space=pl.ANY)
    return pl.pallas_call(
        begin_body,
        out_shape=(sds((tokens, cols), BF16), sds((count * DH, DH), BF16)),
        in_specs=[hbm, hbm],
        out_specs=[VM, VM],
        scratch_shapes=[
            pltpu.VMEM((tokens, cols), BF16),
            pltpu.VMEM((tokens, cols), BF16),
            pltpu.SemaphoreType.DMA((2,)),
        ],
        name="begin",
        compiler_params=pltpu.CompilerParams(vmem_limit_bytes=BEGIN),
        cost_estimate=SHORT,
    )(k, v)


def split_body(x_ref, *outs):
    at = 0
    for out in outs:
        out[...] = x_ref[at : at + out.shape[0], :]
        at += out.shape[0]


def causal():
    rows = lax.broadcasted_iota(jnp.int32, (BLK, BLK), 0)
    cols = lax.broadcasted_iota(jnp.int32, (BLK, BLK), 1)
    return rows >= cols


def scores_body(q_ref, kf_ref, v_ref, qf_ref, sc_ref, intra_ref):
    keep = causal()
    for i, r, c in tiles(q_ref.shape[0], q_ref.shape[1] // DH):
        qf = feature(q_ref[r, c].astype(F32)).astype(BF16)
        qf_ref[r, c] = qf
        sc = jnp.where(keep, mm(qf, kf_ref[r, c], NT), 0.0).astype(BF16)
        sc_ref[i * BLK : (i + 1) * BLK, :] = sc
        intra_ref[r, c] = mm(sc, v_ref[r, c], NN)


def count(lay_ref, h, i, b):
    total = jnp.int32(0)
    for j in range(lay_ref.shape[1]):
        total = total + jnp.where(lay_ref[h, j, i] == b, 1, 0)
    return total.astype(F32)


def in_order(z, s):
    return s


def by_shift(z, s):
    size = lax.axis_size("seq")
    return lax.rem(z + size - s, size)


def by_flip(z, s):
    return lax.bitwise_xor(z, jnp.int32((0, 2, 1, 3)[s]))


def views(parts, rows):
    return [p.at[i * rows : (i + 1) * rows] for p in parts for i in range(p.shape[0] // rows)]


def numer_body(dims, np_, *refs):
    nb, heads, owner_of = dims
    lay_ref, *parts = refs[: 1 + np_]
    qf_ref, intra_ref, carried_ref, num_ref, attn_ref = refs[1 + np_ :]
    z = lax.axis_index("seq")
    for i, r, c in tiles(qf_ref.shape[0], heads):
        n, h = divmod(i, heads)
        query_block = z * nb + n
        total = jnp.zeros((DH, DH), F32)
        for s, part in enumerate(views(parts, nb * heads * DH)):
            for b in range(nb):
                times = count(lay_ref, h, query_block, owner_of(z, s) * nb + b)
                total = total + times * part[mat(b * heads + h), :].astype(F32)
        carried = total.astype(BF16)
        carried_ref[mat(i), :] = carried
        num = mm(qf_ref[r, c], carried, NN) + intra_ref[r, c]
        num_ref[r, c] = num
        rinv = lax.rsqrt(jnp.mean(num * num, axis=-1, keepdims=True) + EPS)
        attn_ref[r, c] = (num * rinv).astype(BF16)


def dnum_body(n_d, *refs):
    d_refs = refs[:n_d]
    num_ref, qf_ref, dnum_ref, cg_ref = refs[n_d:]
    heads = num_ref.shape[1] // DH
    for i, r, c in tiles(num_ref.shape[0], num_ref.shape[1] // DH):
        num = num_ref[r, c]
        grad = d_refs[0][r, c].astype(F32)
        if n_d == 3:
            same, sib = d_refs[1][r, :].astype(F32), d_refs[2][r, :].astype(F32)
            grad = grad + jnp.where(lax.axis_index("dp") == i % heads, same, sib)
        grad = grad.astype(BF16).astype(F32)
        rinv = lax.rsqrt(jnp.mean(num * num, axis=-1, keepdims=True) + EPS)
        lean = jnp.mean(grad * num, axis=-1, keepdims=True)
        dnum = (rinv * grad - num * (rinv * rinv * rinv * lean)).astype(BF16)
        dnum_ref[r, c] = dnum
        cg_ref[mat(i), :] = mm(qf_ref[r, c], dnum, TN).astype(BF16)


def query_body(q_ref, qf_ref, kf_ref, v_ref, dnum_ref, carried_ref, sc_ref, dq_ref, dk_ref, dv_ref):
    keep = causal()
    for i, r, c in tiles(q_ref.shape[0], q_ref.shape[1] // DH):
        dnum = dnum_ref[r, c]
        pg = jnp.where(keep, mm(dnum, v_ref[r, c], NT), 0.0).astype(BF16)
        dq = mm(dnum, carried_ref[mat(i), :], NT) + mm(pg, kf_ref[r, c], NN)
        dq_ref[r, c] = (dq * slope(q_ref[r, c].astype(F32))).astype(BF16)
        dk_ref[r, c] = mm(pg, qf_ref[r, c], TN)
        dv_ref[r, c] = mm(sc_ref[i * BLK : (i + 1) * BLK, :], dnum, TN)


def key_body(dims, np_, *refs):
    nb, heads, owner_of = dims
    lay_ref, *parts = refs[: 1 + np_]
    k_ref, kf_ref, v_ref, dkp_ref, dvp_ref, dk_ref, dv_ref = refs[1 + np_ :]
    z = lax.axis_index("seq")
    for i, r, c in tiles(k_ref.shape[0], heads):
        n, h = divmod(i, heads)
        key_block = z * nb + n
        total = jnp.zeros((DH, DH), F32)
        for s, part in enumerate(views(parts, nb * heads * DH)):
            for b in range(nb):
                times = count(lay_ref, h, owner_of(z, s) * nb + b, key_block)
                total = total + times * part[mat(b * heads + h), :].astype(F32)
        sg = total.astype(BF16)
        dk = mm(v_ref[r, c], sg, NT) + dkp_ref[r, c]
        dk_ref[r, c] = (dk * slope(k_ref[r, c].astype(F32))).astype(BF16)
        dv_ref[r, c] = (mm(kf_ref[r, c], sg, NN) + dvp_ref[r, c]).astype(BF16)


def own_body(og_ref, w_ref, out_ref, w_in, sem):
    width = w_in.shape[0]
    rows = pl.ds(pl.multiple_of(lax.axis_index("head") * width, width), width)
    copy = pltpu.make_async_copy(w_ref.at[rows, :], w_in, sem)
    copy.start()
    copy.wait()
    out_ref[...] = mm(og_ref[...], w_in[...], NN)


def own_partial(og, w):
    tokens, width = og.shape
    cols = w.shape[1]
    return pl.pallas_call(
        own_body,
        out_shape=sds((tokens, cols), F32),
        in_specs=[VM, pl.BlockSpec(memory_space=pl.ANY)],
        out_specs=VM,
        scratch_shapes=[pltpu.VMEM((width, cols), BF16), pltpu.SemaphoreType.DMA],
        name="own_partial",
        compiler_params=pltpu.CompilerParams(vmem_limit_bytes=LIMIT),
        cost_estimate=SHORT,
    )(og, w)


def other_body(og_ref, og_sib_ref, w_ref, same_ref, sib_ref):
    same_ref[...] = mm(og_ref[...], w_ref[...], NN).astype(BF16)
    sib_ref[...] = mm(og_sib_ref[...], w_ref[...], NN).astype(BF16)


def weight_body(cols, attn_ref, og_ref, og_sib_ref, *refs):
    sibs, outs = refs[:-2], refs[-2:]
    rows = outs[0].shape[1]
    parity, core = lax.rem(lax.axis_index("seq"), 2), lax.axis_index("dp")
    for which, pair in enumerate((1 - parity, parity)):
        at = pl.ds(pl.multiple_of((2 * pair + core) * rows, rows), rows)
        total = mm(attn_ref[:, cols], og_ref[:, at], TN)
        row = 0
        for sib in sibs:
            total = total + mm(sib[:, cols], og_sib_ref[row : row + sib.shape[0], at], TN)
            row += sib.shape[0]
        outs[which][...] = total.astype(outs[which].dtype)


def pair_body(keep_ref, got_ref, cg_ref, two_ref, out_ref, joined_ref):
    out_ref[...] = (keep_ref[...] + got_ref[...].astype(F32)).astype(BF16)
    rows = cg_ref.shape[0]
    joined_ref[:rows, :] = cg_ref[...]
    joined_ref[rows:, :] = two_ref[...]


def cross_body(i, keep_ref, got_ref, mine_ref, send_ref, stay_ref):
    home = lax.axis_index("seq") // 2 == lax.axis_index("head")
    cross = (keep_ref[...].astype(F32) + got_ref[...].astype(F32)).astype(BF16)
    mine = mine_ref[mat(i), :]
    send_ref[...] = jnp.where(home, cross, mine)
    stay_ref[...] = jnp.where(home, mine, cross)


def final_body(*refs):
    *got, out_ref = refs
    for i in range(len(got) // 2):
        total = got[2 * i][...].astype(F32) + got[2 * i + 1][...].astype(F32)
        out_ref[:, mat(i)] = total.T


def after(x, *deps):
    return lax.optimization_barrier((x, *deps))[0]


def swap(x, axis):
    return lax.ppermute(x, axis, [(0, 1), (1, 0)])


def gather_parts(x, size):
    if size > 4:
        return [lax.all_gather(x, "seq", axis=0, tiled=True)]
    parts = [x]
    for shift in range(1, size):
        pairs = [(i, (i + shift) % size) for i in range(size)]
        parts.append(lax.ppermute(x, "seq", pairs))
    return parts


def per_device(queries, key_rows, value_rows, layout, out_weight, out_grad):
    seq_size = lax.axis_size("seq")
    head_size = lax.axis_size("head")
    dp_size = lax.axis_size("dp")
    heads = layout.shape[0]
    q, k, v, og = queries[0], key_rows[0], value_rows[0], out_grad[0]
    tokens, cols = q.shape
    nb = tokens // BLK
    paired = seq_size == 4 and head_size == 2 and dp_size == 2
    lay = layout.transpose(0, 2, 1)
    first_owner = in_order if seq_size > 4 else by_shift
    flat = sds((tokens, cols), F32)
    rows16 = sds((tokens, cols), BF16)
    mats = sds((nb * heads * DH, DH), BF16)
    unit = 2 * tokens * cols * DH

    if paired:
        width = og.shape[1]
        far = far_rows(out_weight, width)
        w_other = swap(far, "head")
        kf, st = begin(after(k, far), v)
        og_sib = swap(og, "dp")
    else:
        kf, st = call(states_body, (rows16, mats), (k, v), unit, "states")
    parts = gather_parts(st, seq_size)
    qf, sc, intra = call(
        scores_body,
        (rows16, sds((nb * heads * BLK, BLK), BF16), flat),
        (q, kf, v),
        4 * unit,
        "scores",
    )
    if not paired:
        og = lax.all_gather(og, "head", axis=1, tiled=True)
        d_own = jnp.dot(og, out_weight, preferred_element_type=F32)
    if paired:
        column = sds((tokens, DH), BF16)
        d_same, d_sib = call(other_body, (column, column), (after(og, qf), og_sib, w_other), 0, "other")
        across = [(h * 2 + c, (1 - h) * 2 + 1 - c) for h in range(2) for c in range(2)]
        intra = after(intra, d_sib)
        d_same = swap(d_same, "head")
        d_sib = lax.ppermute(d_sib, ("head", "dp"), across)
    carried, num, attn = call(
        functools.partial(numer_body, (nb, heads, first_owner), len(parts)),
        (mats, flat, rows16),
        (lay, *parts, qf, intra),
        unit,
        "numer",
    )
    if paired:
        attn_other = swap(attn, "head")
        attn_sib = swap(attn, "dp")
        d_own = own_partial(after(og, attn), out_weight)
        d_parts = (d_own, d_same, d_sib)
    else:
        d_parts = (d_own,)
    dnum, cg = call(
        functools.partial(dnum_body, len(d_parts)),
        (rows16, mats),
        (*d_parts, num, qf),
        unit,
        "dnum",
    )
    if paired:
        neighbours = [(0, 1), (1, 0), (2, 3), (3, 2)]
        two = lax.ppermute(cg, "seq", [(i, i ^ 2) for i in range(4)])
        block, half = (cols, width // 4), sds((DH, width // 4), BF16)
        give, keep = call(
            functools.partial(weight_body, slice(None)),
            (sds(block, BF16), sds(block, F32)),
            (after(attn, cg), og, og_sib, attn_sib),
            0,
            "weight",
        )
        got = lax.ppermute(give, "seq", neighbours)
        attn_other = after(attn_other, give)
        third = tokens // 48 * 16
        sizes = (third, third, tokens - 2 * third)
        cuts = call(split_body, tuple(sds((n, cols), BF16) for n in sizes), (attn_other,), 0, "split")
        cuts = [swap(cut, "dp") for cut in cuts]
        beside = [((s ^ 1) * 2 + 1 - h, s * 2 + h) for s in range(4) for h in range(2)]

        def cross_piece(i, *deps):
            give, keep = call(
                functools.partial(weight_body, mat(i)),
                (half, half),
                (after(attn_other, *deps), og, og_sib, *cuts),
                0,
                "weight",
            )
            return give, (swap(keep, "head"), lax.ppermute(give, ("seq", "head"), beside))

        give_b, first_crossed = cross_piece(0)
        mine, joined = call(
            pair_body,
            (sds(block, BF16), sds((2 * cg.shape[0], DH), BF16)),
            (keep, got, cg, two),
            0,
            "pair",
        )
        crossed = [first_crossed]
        for i in range(1, heads):
            give_b, piece = cross_piece(i, mine)
            crossed.append(piece)
        cparts = [cg, two, lax.ppermute(joined, "seq", neighbours)]
        second_owner = by_flip
    else:
        cparts, second_owner = gather_parts(cg, seq_size), first_owner
    dq, dkp, dvp = call(
        query_body,
        (rows16, flat, flat),
        (q, qf, kf, v, dnum, carried, sc),
        9 * unit,
        "query",
    )
    dk, dv = call(
        functools.partial(key_body, (nb, heads, second_owner), len(cparts)),
        (rows16, rows16),
        (lay, *cparts, k, kf, v, dkp, dvp),
        2 * unit,
        "key",
    )
    if paired:
        sums = []
        for i, (k, g) in enumerate(crossed):
            send, stay = call(functools.partial(cross_body, i), (half, half), (k, g, mine), 0, "cross")
            sums += [stay, lax.ppermute(send, "seq", [(s, s ^ 2) for s in range(4)])]
        (weight_grad,) = call(final_body, (sds(block[::-1], F32),), tuple(sums), 0, "final")
    else:
        weight_grad = lax.psum_scatter(
            lax.dot_general(og, attn, TN, preferred_element_type=F32).astype(BF16),
            ("seq", "dp"),
            scatter_dimension=0,
            tiled=True,
        ).astype(F32)
    return attn[None], dq[None], dk[None], dv[None], weight_grad


def solution(mesh):
    rows = P(("groups", "dp"), "seq", "head")
    return jax.shard_map(
        per_device,
        mesh=mesh,
        in_specs=(rows, rows, rows, P("head", None, None), P(None, "head"), rows),
        out_specs=(rows, rows, rows, rows, P(("groups", "seq", "dp"), "head")),
        check_vma=False,
    )
```

```python
import functools

import jax
import jax.numpy as jnp
from jax import lax
from jax.experimental import pallas as pl
from jax.experimental.pallas import tpu as pltpu
from jax.sharding import PartitionSpec as P

DH = 128
BLK = 256
EPS = 1e-06
LIMIT = 16 << 20
BEGIN = 56 << 20
SHORT = pl.CostEstimate(flops=1, bytes_accessed=1, transcendentals=0)
LONG = pl.CostEstimate(flops=10**11, bytes_accessed=1, transcendentals=0)
F32 = jnp.float32
BF16 = jnp.bfloat16
VM = pl.BlockSpec(memory_space=pltpu.VMEM)
SM = pl.BlockSpec(memory_space=pltpu.SMEM)
TN = (((0,), (0,)), ((), ()))
NT = (((1,), (1,)), ((), ()))
NN = (((1,), (0,)), ((), ()))


def sds(shape, dtype):
    return jax.ShapeDtypeStruct(shape, dtype)


def mm(a, b, dims):
    return lax.dot_general(a, b, dims, preferred_element_type=F32)


def feature(x):
    return jnp.where(x > 0, x + 1.0, jnp.exp(jnp.minimum(x, 0.0)))


def slope(x):
    return jnp.where(x > 0, 1.0, jnp.exp(jnp.minimum(x, 0.0)))


def call(body, outs, ins, flops, name):
    read = sum(a.size * a.dtype.itemsize for a in ins)
    wrote = sum(s.size * s.dtype.itemsize for s in outs)
    return pl.pallas_call(
        body,
        out_shape=outs,
        in_specs=[SM if a.dtype == jnp.int32 else VM for a in ins],
        out_specs=[VM] * len(outs),
        name=name,
        compiler_params=pltpu.CompilerParams(vmem_limit_bytes=LIMIT),
        cost_estimate=LONG if name in ("query", "dnum", "numer") else SHORT,
    )(*ins)


def tiles(tokens, heads):
    for n in range(tokens // BLK):
        for h in range(heads):
            yield n * heads + h, slice(n * BLK, (n + 1) * BLK), slice(h * DH, (h + 1) * DH)


def mat(i):
    return slice(i * DH, (i + 1) * DH)


def states_body(k_ref, v_ref, kf_ref, st_ref):
    for i, r, c in tiles(k_ref.shape[0], k_ref.shape[1] // DH):
        kf = feature(k_ref[r, c].astype(F32)).astype(BF16)
        kf_ref[r, c] = kf
        st_ref[mat(i), :] = mm(kf, v_ref[r, c], TN).astype(BF16)


def far_body(w_ref, far_ref, sem):
    width, cols = far_ref.shape
    rows = pl.ds(pl.multiple_of((1 - lax.axis_index("head")) * width, width), width)
    lanes = pl.ds(pl.multiple_of(lax.axis_index("dp") * cols, cols), cols)
    copy = pltpu.make_async_copy(w_ref.at[rows, lanes], far_ref, sem)
    copy.start()
    copy.wait()


def far_rows(w, width):
    return pl.pallas_call(
        far_body,
        out_shape=sds((width, DH), BF16),
        in_specs=[pl.BlockSpec(memory_space=pl.ANY)],
        out_specs=VM,
        scratch_shapes=[pltpu.SemaphoreType.DMA],
        name="far",
        compiler_params=pltpu.CompilerParams(vmem_limit_bytes=BEGIN),
        cost_estimate=SHORT,
    )(w)


def begin_body(k_ref, v_ref, kf_ref, st_ref, k_in, v_in, sems):
    k_copy = pltpu.make_async_copy(k_ref, k_in, sems.at[0])
    v_copy = pltpu.make_async_copy(v_ref, v_in, sems.at[1])
    k_copy.start()
    v_copy.start()
    k_copy.wait()
    v_copy.wait()
    states_body(k_in, v_in, kf_ref, st_ref)


def begin(k, v):
    tokens, cols = k.shape
    count = tokens // BLK * (cols // DH)
    hbm = pl.BlockSpec(memory_space=pl.ANY)
    return pl.pallas_call(
        begin_body,
        out_shape=(sds((tokens, cols), BF16), sds((count * DH, DH), BF16)),
        in_specs=[hbm, hbm],
        out_specs=[VM, VM],
        scratch_shapes=[
            pltpu.VMEM((tokens, cols), BF16),
            pltpu.VMEM((tokens, cols), BF16),
            pltpu.SemaphoreType.DMA((2,)),
        ],
        name="begin",
        compiler_params=pltpu.CompilerParams(vmem_limit_bytes=BEGIN),
        cost_estimate=SHORT,
    )(k, v)


def split_body(x_ref, *outs):
    at = 0
    for out in outs:
        out[...] = x_ref[at : at + out.shape[0], :]
        at += out.shape[0]


def causal():
    rows = lax.broadcasted_iota(jnp.int32, (BLK, BLK), 0)
    cols = lax.broadcasted_iota(jnp.int32, (BLK, BLK), 1)
    return rows >= cols


def scores_body(q_ref, kf_ref, v_ref, qf_ref, sc_ref, intra_ref):
    keep = causal()
    for i, r, c in tiles(q_ref.shape[0], q_ref.shape[1] // DH):
        qf = feature(q_ref[r, c].astype(F32)).astype(BF16)
        qf_ref[r, c] = qf
        sc = jnp.where(keep, mm(qf, kf_ref[r, c], NT), 0.0).astype(BF16)
        sc_ref[i * BLK : (i + 1) * BLK, :] = sc
        intra_ref[r, c] = mm(sc, v_ref[r, c], NN)


def count(lay_ref, h, i, b):
    total = jnp.int32(0)
    for j in range(lay_ref.shape[1]):
        total = total + jnp.where(lay_ref[h, j, i] == b, 1, 0)
    return total.astype(F32)


def in_order(z, s):
    return s


def by_shift(z, s):
    size = lax.axis_size("seq")
    return lax.rem(z + size - s, size)


def by_flip(z, s):
    return lax.bitwise_xor(z, jnp.int32((0, 2, 1, 3)[s]))


def views(parts, rows):
    return [p.at[i * rows : (i + 1) * rows] for p in parts for i in range(p.shape[0] // rows)]


def numer_body(dims, np_, *refs):
    nb, heads, owner_of = dims
    lay_ref, *parts = refs[: 1 + np_]
    qf_ref, intra_ref, carried_ref, num_ref, attn_ref = refs[1 + np_ :]
    z = lax.axis_index("seq")
    for i, r, c in tiles(qf_ref.shape[0], heads):
        n, h = divmod(i, heads)
        query_block = z * nb + n
        total = jnp.zeros((DH, DH), F32)
        for s, part in enumerate(views(parts, nb * heads * DH)):
            for b in range(nb):
                times = count(lay_ref, h, query_block, owner_of(z, s) * nb + b)
                total = total + times * part[mat(b * heads + h), :].astype(F32)
        carried = total.astype(BF16)
        carried_ref[mat(i), :] = carried
        num = mm(qf_ref[r, c], carried, NN) + intra_ref[r, c]
        num_ref[r, c] = num
        rinv = lax.rsqrt(jnp.mean(num * num, axis=-1, keepdims=True) + EPS)
        attn_ref[r, c] = (num * rinv).astype(BF16)


def dnum_body(n_d, *refs):
    d_refs = refs[:n_d]
    num_ref, qf_ref, dnum_ref, cg_ref = refs[n_d:]
    heads = num_ref.shape[1] // DH
    for i, r, c in tiles(num_ref.shape[0], num_ref.shape[1] // DH):
        num = num_ref[r, c]
        grad = d_refs[0][r, c].astype(F32)
        if n_d == 3:
            same, sib = d_refs[1][r, :].astype(F32), d_refs[2][r, :].astype(F32)
            grad = grad + jnp.where(lax.axis_index("dp") == i % heads, same, sib)
        grad = grad.astype(BF16).astype(F32)
        rinv = lax.rsqrt(jnp.mean(num * num, axis=-1, keepdims=True) + EPS)
        lean = jnp.mean(grad * num, axis=-1, keepdims=True)
        dnum = (rinv * grad - num * (rinv * rinv * rinv * lean)).astype(BF16)
        dnum_ref[r, c] = dnum
        cg_ref[mat(i), :] = mm(qf_ref[r, c], dnum, TN).astype(BF16)


def query_body(q_ref, qf_ref, kf_ref, v_ref, dnum_ref, carried_ref, sc_ref, attn_ref, *outs):
    dq_ref, dk_ref, dv_ref, attn_out_ref = outs
    attn_out_ref[...] = attn_ref[...]
    keep = causal()
    for i, r, c in tiles(q_ref.shape[0], q_ref.shape[1] // DH):
        dnum = dnum_ref[r, c]
        pg = jnp.where(keep, mm(dnum, v_ref[r, c], NT), 0.0).astype(BF16)
        dq = mm(dnum, carried_ref[mat(i), :], NT) + mm(pg, kf_ref[r, c], NN)
        dq_ref[r, c] = (dq * slope(q_ref[r, c].astype(F32))).astype(BF16)
        dk_ref[r, c] = mm(pg, qf_ref[r, c], TN)
        dv_ref[r, c] = mm(sc_ref[i * BLK : (i + 1) * BLK, :], dnum, TN)


def key_body(dims, np_, *refs):
    nb, heads, owner_of = dims
    lay_ref, *parts = refs[: 1 + np_]
    k_ref, kf_ref, v_ref, dkp_ref, dvp_ref, dk_ref, dv_ref = refs[1 + np_ :]
    z = lax.axis_index("seq")
    for i, r, c in tiles(k_ref.shape[0], heads):
        n, h = divmod(i, heads)
        key_block = z * nb + n
        total = jnp.zeros((DH, DH), F32)
        for s, part in enumerate(views(parts, nb * heads * DH)):
            for b in range(nb):
                times = count(lay_ref, h, owner_of(z, s) * nb + b, key_block)
                total = total + times * part[mat(b * heads + h), :].astype(F32)
        sg = total.astype(BF16)
        dk = mm(v_ref[r, c], sg, NT) + dkp_ref[r, c]
        dk_ref[r, c] = (dk * slope(k_ref[r, c].astype(F32))).astype(BF16)
        dv_ref[r, c] = (mm(kf_ref[r, c], sg, NN) + dvp_ref[r, c]).astype(BF16)


def own_body(og_ref, w_ref, out_ref, w_in, sem):
    width = w_in.shape[0]
    rows = pl.ds(pl.multiple_of(lax.axis_index("head") * width, width), width)
    copy = pltpu.make_async_copy(w_ref.at[rows, :], w_in, sem)
    copy.start()
    copy.wait()
    out_ref[...] = mm(og_ref[...], w_in[...], NN)


def own_partial(og, w):
    tokens, width = og.shape
    cols = w.shape[1]
    return pl.pallas_call(
        own_body,
        out_shape=sds((tokens, cols), F32),
        in_specs=[VM, pl.BlockSpec(memory_space=pl.ANY)],
        out_specs=VM,
        scratch_shapes=[pltpu.VMEM((width, cols), BF16), pltpu.SemaphoreType.DMA],
        name="own_partial",
        compiler_params=pltpu.CompilerParams(vmem_limit_bytes=LIMIT),
        cost_estimate=SHORT,
    )(og, w)


def other_body(og_ref, og_sib_ref, w_ref, same_ref, sib_ref):
    same_ref[...] = mm(og_ref[...], w_ref[...], NN).astype(BF16)
    sib_ref[...] = mm(og_sib_ref[...], w_ref[...], NN).astype(BF16)


def weight_body(cols, attn_ref, og_ref, og_sib_ref, *refs):
    sibs, outs = refs[:-2], refs[-2:]
    rows = outs[0].shape[1]
    parity, core = lax.rem(lax.axis_index("seq"), 2), lax.axis_index("dp")
    for which, pair in enumerate((1 - parity, parity)):
        at = pl.ds(pl.multiple_of((2 * pair + core) * rows, rows), rows)
        total = mm(attn_ref[:, cols], og_ref[:, at], TN)
        row = 0
        for sib in sibs:
            total = total + mm(sib[:, cols], og_sib_ref[row : row + sib.shape[0], at], TN)
            row += sib.shape[0]
        outs[which][...] = total.astype(outs[which].dtype)


def pair_body(keep_ref, got_ref, cg_ref, two_ref, out_ref, joined_ref):
    out_ref[...] = (keep_ref[...] + got_ref[...].astype(F32)).astype(BF16)
    rows = cg_ref.shape[0]
    joined_ref[:rows, :] = cg_ref[...]
    joined_ref[rows:, :] = two_ref[...]


def cross_body(i, keep_ref, got_ref, mine_ref, send_ref, stay_ref):
    home = lax.axis_index("seq") // 2 == lax.axis_index("head")
    cross = (keep_ref[...].astype(F32) + got_ref[...].astype(F32)).astype(BF16)
    mine = mine_ref[mat(i), :]
    send_ref[...] = jnp.where(home, cross, mine)
    stay_ref[...] = jnp.where(home, mine, cross)


def final_body(*refs):
    *got, out_ref = refs
    for i in range(len(got) // 2):
        total = got[2 * i][...].astype(F32) + got[2 * i + 1][...].astype(F32)
        out_ref[:, mat(i)] = total.T


def after(x, *deps):
    return lax.optimization_barrier((x, *deps))[0]


def swap(x, axis):
    return lax.ppermute(x, axis, [(0, 1), (1, 0)])


def gather_parts(x, size):
    if size > 4:
        return [lax.all_gather(x, "seq", axis=0, tiled=True)]
    parts = [x]
    for shift in range(1, size):
        pairs = [(i, (i + shift) % size) for i in range(size)]
        parts.append(lax.ppermute(x, "seq", pairs))
    return parts


def per_device(queries, key_rows, value_rows, layout, out_weight, out_grad):
    seq_size = lax.axis_size("seq")
    head_size = lax.axis_size("head")
    dp_size = lax.axis_size("dp")
    heads = layout.shape[0]
    q, k, v, og = queries[0], key_rows[0], value_rows[0], out_grad[0]
    tokens, cols = q.shape
    nb = tokens // BLK
    paired = seq_size == 4 and head_size == 2 and dp_size == 2
    lay = layout.transpose(0, 2, 1)
    first_owner = in_order if seq_size > 4 else by_shift
    flat = sds((tokens, cols), F32)
    rows16 = sds((tokens, cols), BF16)
    mats = sds((nb * heads * DH, DH), BF16)
    unit = 2 * tokens * cols * DH

    if paired:
        width = og.shape[1]
        far = far_rows(out_weight, width)
        w_other = swap(far, "head")
        kf, st = begin(after(k, far), v)
        og_sib = swap(og, "dp")
    else:
        kf, st = call(states_body, (rows16, mats), (k, v), unit, "states")
    parts = gather_parts(st, seq_size)
    qf, sc, intra = call(
        scores_body,
        (rows16, sds((nb * heads * BLK, BLK), BF16), flat),
        (q, kf, v),
        4 * unit,
        "scores",
    )
    if not paired:
        og = lax.all_gather(og, "head", axis=1, tiled=True)
        d_own = jnp.dot(og, out_weight, preferred_element_type=F32)
    if paired:
        column = sds((tokens, DH), BF16)
        d_same, d_sib = call(other_body, (column, column), (after(og, qf), og_sib, w_other), 0, "other")
        across = [(h * 2 + c, (1 - h) * 2 + 1 - c) for h in range(2) for c in range(2)]
        intra = after(intra, d_sib)
        d_same = swap(d_same, "head")
        d_sib = lax.ppermute(d_sib, ("head", "dp"), across)
    carried, num, attn = call(
        functools.partial(numer_body, (nb, heads, first_owner), len(parts)),
        (mats, flat, rows16),
        (lay, *parts, qf, intra),
        unit,
        "numer",
    )
    if paired:
        attn_other = swap(attn, "head")
        attn_sib = swap(attn, "dp")
        d_own = own_partial(after(og, attn), out_weight)
        d_parts = (d_own, d_same, d_sib)
    else:
        d_parts = (d_own,)
    dnum, cg = call(
        functools.partial(dnum_body, len(d_parts)),
        (rows16, mats),
        (*d_parts, num, qf),
        unit,
        "dnum",
    )
    if paired:
        neighbours = [(0, 1), (1, 0), (2, 3), (3, 2)]
        two = lax.ppermute(cg, "seq", [(i, i ^ 2) for i in range(4)])
        block, half = (cols, width // 4), sds((DH, width // 4), BF16)
        give, keep = call(
            functools.partial(weight_body, slice(None)),
            (sds(block, BF16), sds(block, F32)),
            (after(attn, cg), og, og_sib, attn_sib),
            0,
            "weight",
        )
        got = lax.ppermute(give, "seq", neighbours)
        attn_other = after(attn_other, give)
        third = tokens // 48 * 16
        sizes = (third, third, tokens - 2 * third)
        cuts = call(split_body, tuple(sds((n, cols), BF16) for n in sizes), (attn_other,), 0, "split")
        cuts = [swap(cut, "dp") for cut in cuts]
        beside = [((s ^ 1) * 2 + 1 - h, s * 2 + h) for s in range(4) for h in range(2)]

        def cross_piece(i, *deps):
            give, keep = call(
                functools.partial(weight_body, mat(i)),
                (half, half),
                (after(attn_other, *deps), og, og_sib, *cuts),
                0,
                "weight",
            )
            return give, (swap(keep, "head"), lax.ppermute(give, ("seq", "head"), beside))

        give_b, first_crossed = cross_piece(0)
        mine, joined = call(
            pair_body,
            (sds(block, BF16), sds((2 * cg.shape[0], DH), BF16)),
            (keep, got, cg, two),
            0,
            "pair",
        )
        crossed = [first_crossed]
        for i in range(1, heads):
            give_b, piece = cross_piece(i, mine)
            crossed.append(piece)
        cparts = [cg, two, lax.ppermute(joined, "seq", neighbours)]
        second_owner = by_flip
    else:
        cparts, second_owner = gather_parts(cg, seq_size), first_owner
    dq, dkp, dvp, attn_out = call(
        query_body,
        (rows16, flat, flat, rows16),
        (q, qf, kf, v, dnum, carried, sc, attn),
        9 * unit,
        "query",
    )
    if paired:
        sums = []
        for i, (straight, diagonal) in enumerate(crossed):
            send, stay = call(functools.partial(cross_body, i), (half, half), (straight, diagonal, mine), 0, "cross")
            mine = after(mine, send)
            sums += [stay, lax.ppermute(send, "seq", [(s, s ^ 2) for s in range(4)])]
        (weight_grad,) = call(final_body, (sds(block[::-1], F32),), tuple(sums), 0, "final")
    else:
        weight_grad = lax.psum_scatter(
            lax.dot_general(og, attn, TN, preferred_element_type=F32).astype(BF16),
            ("seq", "dp"),
            scatter_dimension=0,
            tiled=True,
        ).astype(F32)
    if paired:
        dkp = after(dkp, weight_grad)
    dk, dv = call(
        functools.partial(key_body, (nb, heads, second_owner), len(cparts)),
        (rows16, rows16),
        (lay, *cparts, k, kf, v, dkp, dvp),
        2 * unit,
        "key",
    )
    return attn_out[None], dq[None], dk[None], dv[None], weight_grad


def solution(mesh):
    rows = P(("groups", "dp"), "seq", "head")
    return jax.shard_map(
        per_device,
        mesh=mesh,
        in_specs=(rows, rows, rows, P("head", None, None), P(None, "head"), rows),
        out_specs=(rows, rows, rows, rows, P(("groups", "seq", "dp"), "head")),
        check_vma=False,
    )
```

```python
import functools

import jax
import jax.numpy as jnp
from jax import lax
from jax.experimental import pallas as pl
from jax.experimental.pallas import tpu as pltpu
from jax.sharding import PartitionSpec as P

DH = 128
BLK = 256
EPS = 1e-06
LIMIT = 16 << 20
BEGIN = 52 << 20
FAR = 4
SHORT = pl.CostEstimate(flops=1, bytes_accessed=1, transcendentals=0)
LONG = pl.CostEstimate(flops=10**11, bytes_accessed=1, transcendentals=0)
F32 = jnp.float32
BF16 = jnp.bfloat16
VM = pl.BlockSpec(memory_space=pltpu.VMEM)
SM = pl.BlockSpec(memory_space=pltpu.SMEM)
TN = (((0,), (0,)), ((), ()))
NT = (((1,), (1,)), ((), ()))
NN = (((1,), (0,)), ((), ()))


def sds(shape, dtype):
    return jax.ShapeDtypeStruct(shape, dtype)


def mm(a, b, dims):
    return lax.dot_general(a, b, dims, preferred_element_type=F32)


def feature(x):
    return jnp.where(x > 0, x + 1.0, jnp.exp(jnp.minimum(x, 0.0)))


def slope(x):
    return jnp.where(x > 0, 1.0, jnp.exp(jnp.minimum(x, 0.0)))


def streamed(outs, streams):
    if not streams:
        return []
    return [pltpu.VMEM(o.shape, o.dtype) for o in outs] + [pltpu.SemaphoreType.DMA((streams,))]


def call(body, outs, ins, flops, name, streams=0):
    read = sum(a.size * a.dtype.itemsize for a in ins)
    wrote = sum(s.size * s.dtype.itemsize for s in outs)
    return pl.pallas_call(
        body,
        out_shape=outs,
        in_specs=[SM if a.dtype == jnp.int32 else VM for a in ins],
        out_specs=[pl.BlockSpec(memory_space=pl.ANY) if streams else VM] * len(outs),
        scratch_shapes=streamed(outs, streams),
        name=name,
        compiler_params=pltpu.CompilerParams(vmem_limit_bytes=LIMIT),
        cost_estimate=LONG if name in ("query", "dnum", "numer") else SHORT,
    )(*ins)


def tiles(tokens, heads):
    for n in range(tokens // BLK):
        for h in range(heads):
            yield n * heads + h, slice(n * BLK, (n + 1) * BLK), slice(h * DH, (h + 1) * DH)


def mat(i):
    return slice(i * DH, (i + 1) * DH)


def states_body(k_ref, v_ref, kf_ref, st_ref):
    for i, r, c in tiles(k_ref.shape[0], k_ref.shape[1] // DH):
        kf = feature(k_ref[r, c].astype(F32)).astype(BF16)
        kf_ref[r, c] = kf
        st_ref[mat(i), :] = mm(kf, v_ref[r, c], TN).astype(BF16)


def far_body(w_ref, far_ref, sems):
    width, cols = far_ref.shape
    first = (1 - lax.axis_index("head")) * width
    lanes = pl.ds(pl.multiple_of(lax.axis_index("dp") * cols, cols), cols)
    copies = []
    for i in range(FAR):
        size = width // FAR
        rows = pl.ds(pl.multiple_of(first + i * size, size), size)
        into = far_ref.at[i * size : (i + 1) * size]
        copies.append(pltpu.make_async_copy(w_ref.at[rows, lanes], into, sems.at[i]))
    for copy in copies:
        copy.start()
    for copy in copies:
        copy.wait()


def far_rows(w, width):
    return pl.pallas_call(
        far_body,
        out_shape=sds((width, DH), BF16),
        in_specs=[pl.BlockSpec(memory_space=pl.ANY)],
        out_specs=VM,
        scratch_shapes=[pltpu.SemaphoreType.DMA((FAR,))],
        name="far",
        compiler_params=pltpu.CompilerParams(vmem_limit_bytes=BEGIN),
        cost_estimate=SHORT,
    )(w)


def begin_body(k_ref, v_ref, kf_ref, st_ref, k_in, v_in, sems):
    k_copy = pltpu.make_async_copy(k_ref, k_in, sems.at[0])
    v_copy = pltpu.make_async_copy(v_ref, v_in, sems.at[1])
    k_copy.start()
    v_copy.start()
    k_copy.wait()
    v_copy.wait()
    states_body(k_in, v_in, kf_ref, st_ref)


def begin(k, v):
    tokens, cols = k.shape
    count = tokens // BLK * (cols // DH)
    hbm = pl.BlockSpec(memory_space=pl.ANY)
    return pl.pallas_call(
        begin_body,
        out_shape=(sds((tokens, cols), BF16), sds((count * DH, DH), BF16)),
        in_specs=[hbm, hbm],
        out_specs=[VM, VM],
        scratch_shapes=[
            pltpu.VMEM((tokens, cols), BF16),
            pltpu.VMEM((tokens, cols), BF16),
            pltpu.SemaphoreType.DMA((2,)),
        ],
        name="begin",
        compiler_params=pltpu.CompilerParams(vmem_limit_bytes=BEGIN),
        cost_estimate=SHORT,
    )(k, v)


def split_body(x_ref, *outs):
    at = 0
    for out in outs:
        out[...] = x_ref[at : at + out.shape[0], :]
        at += out.shape[0]


def causal():
    rows = lax.broadcasted_iota(jnp.int32, (BLK, BLK), 0)
    cols = lax.broadcasted_iota(jnp.int32, (BLK, BLK), 1)
    return rows >= cols


def scores_body(q_ref, kf_ref, v_ref, qf_ref, sc_ref, intra_ref):
    keep = causal()
    for i, r, c in tiles(q_ref.shape[0], q_ref.shape[1] // DH):
        qf = feature(q_ref[r, c].astype(F32)).astype(BF16)
        qf_ref[r, c] = qf
        sc = jnp.where(keep, mm(qf, kf_ref[r, c], NT), 0.0).astype(BF16)
        sc_ref[i * BLK : (i + 1) * BLK, :] = sc
        intra_ref[r, c] = mm(sc, v_ref[r, c], NN)


def count(lay_ref, h, i, b):
    total = jnp.int32(0)
    for j in range(lay_ref.shape[1]):
        total = total + jnp.where(lay_ref[h, j, i] == b, 1, 0)
    return total.astype(F32)


def in_order(z, s):
    return s


def by_shift(z, s):
    size = lax.axis_size("seq")
    return lax.rem(z + size - s, size)


def by_flip(z, s):
    return lax.bitwise_xor(z, jnp.int32((0, 2, 1, 3)[s]))


def views(parts, rows):
    return [p.at[i * rows : (i + 1) * rows] for p in parts for i in range(p.shape[0] // rows)]


def numer_body(dims, np_, *refs):
    nb, heads, owner_of = dims
    lay_ref, *parts = refs[: 1 + np_]
    qf_ref, intra_ref, carried_ref, num_ref, attn_ref = refs[1 + np_ :]
    z = lax.axis_index("seq")
    for i, r, c in tiles(qf_ref.shape[0], heads):
        n, h = divmod(i, heads)
        query_block = z * nb + n
        total = jnp.zeros((DH, DH), F32)
        for s, part in enumerate(views(parts, nb * heads * DH)):
            for b in range(nb):
                times = count(lay_ref, h, query_block, owner_of(z, s) * nb + b)
                total = total + times * part[mat(b * heads + h), :].astype(F32)
        carried = total.astype(BF16)
        carried_ref[mat(i), :] = carried
        num = mm(qf_ref[r, c], carried, NN) + intra_ref[r, c]
        num_ref[r, c] = num
        rinv = lax.rsqrt(jnp.mean(num * num, axis=-1, keepdims=True) + EPS)
        attn_ref[r, c] = (num * rinv).astype(BF16)


def dnum_body(n_d, *refs):
    d_refs = refs[:n_d]
    num_ref, qf_ref, dnum_ref, cg_ref = refs[n_d:]
    heads = num_ref.shape[1] // DH
    for i, r, c in tiles(num_ref.shape[0], num_ref.shape[1] // DH):
        num = num_ref[r, c]
        grad = d_refs[0][r, c].astype(F32)
        if n_d == 3:
            same, sib = d_refs[1][r, :].astype(F32), d_refs[2][r, :].astype(F32)
            grad = grad + jnp.where(lax.axis_index("dp") == i % heads, same, sib)
        grad = grad.astype(BF16).astype(F32)
        rinv = lax.rsqrt(jnp.mean(num * num, axis=-1, keepdims=True) + EPS)
        lean = jnp.mean(grad * num, axis=-1, keepdims=True)
        dnum = (rinv * grad - num * (rinv * rinv * rinv * lean)).astype(BF16)
        dnum_ref[r, c] = dnum
        cg_ref[mat(i), :] = mm(qf_ref[r, c], dnum, TN).astype(BF16)


def query_body(q_ref, qf_ref, kf_ref, v_ref, dnum_ref, carried_ref, sc_ref, attn_ref, *outs):
    dq_ref, dk_ref, dv_ref, attn_out_ref = outs
    attn_out_ref[...] = attn_ref[...]
    keep = causal()
    for i, r, c in tiles(q_ref.shape[0], q_ref.shape[1] // DH):
        dnum = dnum_ref[r, c]
        pg = jnp.where(keep, mm(dnum, v_ref[r, c], NT), 0.0).astype(BF16)
        dq = mm(dnum, carried_ref[mat(i), :], NT) + mm(pg, kf_ref[r, c], NN)
        dq_ref[r, c] = (dq * slope(q_ref[r, c].astype(F32))).astype(BF16)
        dk_ref[r, c] = mm(pg, qf_ref[r, c], TN)
        dv_ref[r, c] = mm(sc_ref[i * BLK : (i + 1) * BLK, :], dnum, TN)


def key_body(dims, np_, *refs):
    nb, heads, owner_of = dims
    lay_ref, *parts = refs[: 1 + np_]
    k_ref, kf_ref, v_ref, dkp_ref, dvp_ref, dk_out, dv_out, dk_ref, dv_ref, sems = refs[1 + np_ :]
    copies = []
    z = lax.axis_index("seq")
    for i, r, c in tiles(k_ref.shape[0], heads):
        n, h = divmod(i, heads)
        key_block = z * nb + n
        total = jnp.zeros((DH, DH), F32)
        for s, part in enumerate(views(parts, nb * heads * DH)):
            for b in range(nb):
                times = count(lay_ref, h, owner_of(z, s) * nb + b, key_block)
                total = total + times * part[mat(b * heads + h), :].astype(F32)
        sg = total.astype(BF16)
        dk = mm(v_ref[r, c], sg, NT) + dkp_ref[r, c]
        dk_ref[r, c] = (dk * slope(k_ref[r, c].astype(F32))).astype(BF16)
        dv_ref[r, c] = (mm(kf_ref[r, c], sg, NN) + dvp_ref[r, c]).astype(BF16)
        if h == heads - 1:
            for at, (ref, out) in enumerate(((dk_ref, dk_out), (dv_ref, dv_out))):
                copies.append(pltpu.make_async_copy(ref.at[r, :], out.at[r, :], sems.at[2 * n + at]))
                copies[-1].start()
    for copy in copies:
        copy.wait()


def own_body(og_ref, w_ref, out_ref, w_in, sem):
    width = w_in.shape[0]
    rows = pl.ds(pl.multiple_of(lax.axis_index("head") * width, width), width)
    copy = pltpu.make_async_copy(w_ref.at[rows, :], w_in, sem)
    copy.start()
    copy.wait()
    out_ref[...] = mm(og_ref[...], w_in[...], NN)


def own_partial(og, w):
    tokens, width = og.shape
    cols = w.shape[1]
    return pl.pallas_call(
        own_body,
        out_shape=sds((tokens, cols), F32),
        in_specs=[VM, pl.BlockSpec(memory_space=pl.ANY)],
        out_specs=VM,
        scratch_shapes=[pltpu.VMEM((width, cols), BF16), pltpu.SemaphoreType.DMA],
        name="own_partial",
        compiler_params=pltpu.CompilerParams(vmem_limit_bytes=LIMIT),
        cost_estimate=SHORT,
    )(og, w)


def other_body(og_ref, og_sib_ref, w_ref, same_ref, sib_ref):
    same_ref[...] = mm(og_ref[...], w_ref[...], NN).astype(BF16)
    sib_ref[...] = mm(og_sib_ref[...], w_ref[...], NN).astype(BF16)


def weight_body(cols, attn_ref, og_ref, og_sib_ref, *refs):
    sibs, outs = refs[:-2], refs[-2:]
    rows = outs[0].shape[1]
    parity, core = lax.rem(lax.axis_index("seq"), 2), lax.axis_index("dp")
    for which, pair in enumerate((1 - parity, parity)):
        at = pl.ds(pl.multiple_of((2 * pair + core) * rows, rows), rows)
        total = mm(attn_ref[:, cols], og_ref[:, at], TN)
        row = 0
        for sib in sibs:
            total = total + mm(sib[:, cols], og_sib_ref[row : row + sib.shape[0], at], TN)
            row += sib.shape[0]
        outs[which][...] = total.astype(outs[which].dtype)


def pair_body(keep_ref, got_ref, cg_ref, two_ref, out_ref, joined_ref):
    out_ref[...] = (keep_ref[...] + got_ref[...].astype(F32)).astype(BF16)
    rows = cg_ref.shape[0]
    joined_ref[:rows, :] = cg_ref[...]
    joined_ref[rows:, :] = two_ref[...]


def cross_body(i, keep_ref, got_ref, mine_ref, send_ref, stay_ref):
    home = lax.axis_index("seq") // 2 == lax.axis_index("head")
    cross = (keep_ref[...].astype(F32) + got_ref[...].astype(F32)).astype(BF16)
    mine = mine_ref[mat(i), :]
    send_ref[...] = jnp.where(home, cross, mine)
    stay_ref[...] = jnp.where(home, mine, cross)


def final_body(*refs):
    *got, out_ref, total_ref, sems = refs
    copies = []
    for j in range(total_ref.shape[0] // DH):
        for i in range(len(got) // 2):
            total = got[2 * i][:, mat(j)].astype(F32) + got[2 * i + 1][:, mat(j)].astype(F32)
            total_ref[mat(j), mat(i)] = total.T
        copies.append(pltpu.make_async_copy(total_ref.at[mat(j), :], out_ref.at[mat(j), :], sems.at[j]))
        copies[-1].start()
    for copy in copies:
        copy.wait()


def after(x, *deps):
    return lax.optimization_barrier((x, *deps))[0]


def swap(x, axis):
    return lax.ppermute(x, axis, [(0, 1), (1, 0)])


def gather_parts(x, size):
    if size > 4:
        return [lax.all_gather(x, "seq", axis=0, tiled=True)]
    parts = [x]
    for shift in range(1, size):
        pairs = [(i, (i + shift) % size) for i in range(size)]
        parts.append(lax.ppermute(x, "seq", pairs))
    return parts


def per_device(queries, key_rows, value_rows, layout, out_weight, out_grad):
    seq_size = lax.axis_size("seq")
    head_size = lax.axis_size("head")
    dp_size = lax.axis_size("dp")
    heads = layout.shape[0]
    q, k, v, og = queries[0], key_rows[0], value_rows[0], out_grad[0]
    tokens, cols = q.shape
    nb = tokens // BLK
    paired = seq_size == 4 and head_size == 2 and dp_size == 2
    lay = layout.transpose(0, 2, 1)
    first_owner = in_order if seq_size > 4 else by_shift
    flat = sds((tokens, cols), F32)
    rows16 = sds((tokens, cols), BF16)
    mats = sds((nb * heads * DH, DH), BF16)
    unit = 2 * tokens * cols * DH

    if paired:
        width = og.shape[1]
        far = far_rows(out_weight, width)
        w_other = swap(far, "head")
        kf, st = begin(after(k, far), v)
        og_sib = swap(og, "dp")
    else:
        kf, st = call(states_body, (rows16, mats), (k, v), unit, "states")
    parts = gather_parts(st, seq_size)
    qf, sc, intra = call(
        scores_body,
        (rows16, sds((nb * heads * BLK, BLK), BF16), flat),
        (q, kf, v),
        4 * unit,
        "scores",
    )
    if not paired:
        og = lax.all_gather(og, "head", axis=1, tiled=True)
        d_own = jnp.dot(og, out_weight, preferred_element_type=F32)
    if paired:
        column = sds((tokens, DH), BF16)
        d_same, d_sib = call(other_body, (column, column), (after(og, qf), og_sib, w_other), 0, "other")
        across = [(h * 2 + c, (1 - h) * 2 + 1 - c) for h in range(2) for c in range(2)]
        intra = after(intra, d_sib)
        d_same = swap(d_same, "head")
        d_sib = lax.ppermute(d_sib, ("head", "dp"), across)
    carried, num, attn = call(
        functools.partial(numer_body, (nb, heads, first_owner), len(parts)),
        (mats, flat, rows16),
        (lay, *parts, qf, intra),
        unit,
        "numer",
    )
    if paired:
        attn_other = swap(attn, "head")
        attn_sib = swap(attn, "dp")
        d_own = own_partial(after(og, attn), out_weight)
        d_parts = (d_own, d_same, d_sib)
    else:
        d_parts = (d_own,)
    dnum, cg = call(
        functools.partial(dnum_body, len(d_parts)),
        (rows16, mats),
        (*d_parts, num, qf),
        unit,
        "dnum",
    )
    if paired:
        neighbours = [(0, 1), (1, 0), (2, 3), (3, 2)]
        two = lax.ppermute(cg, "seq", [(i, i ^ 2) for i in range(4)])
        block, half = (cols, width // 4), sds((DH, width // 4), BF16)
        give, keep = call(
            functools.partial(weight_body, slice(None)),
            (sds(block, BF16), sds(block, F32)),
            (after(attn, cg), og, og_sib, attn_sib),
            0,
            "weight",
        )
        got = lax.ppermute(give, "seq", neighbours)
        attn_other = after(attn_other, give)
        third = tokens // 48 * 16
        sizes = (third, third, tokens - 2 * third)
        cuts = call(split_body, tuple(sds((n, cols), BF16) for n in sizes), (attn_other,), 0, "split")
        cuts = [swap(cut, "dp") for cut in cuts]
        beside = [((s ^ 1) * 2 + 1 - h, s * 2 + h) for s in range(4) for h in range(2)]

        def cross_piece(i, *deps):
            give, keep = call(
                functools.partial(weight_body, mat(i)),
                (half, half),
                (after(attn_other, *deps), og, og_sib, *cuts),
                0,
                "weight",
            )
            return give, (swap(keep, "head"), lax.ppermute(give, ("seq", "head"), beside))

        give_b, first_crossed = cross_piece(0)
        mine, joined = call(
            pair_body,
            (sds(block, BF16), sds((2 * cg.shape[0], DH), BF16)),
            (keep, got, cg, two),
            0,
            "pair",
        )
        crossed = [first_crossed]
        for i in range(1, heads):
            give_b, piece = cross_piece(i, mine)
            crossed.append(piece)
        cparts = [cg, two, lax.ppermute(joined, "seq", neighbours)]
        second_owner = by_flip
    else:
        cparts, second_owner = gather_parts(cg, seq_size), first_owner
    dq, dkp, dvp, attn_out = call(
        query_body,
        (rows16, flat, flat, rows16),
        (q, qf, kf, v, dnum, carried, sc, attn),
        9 * unit,
        "query",
    )
    if paired:
        sums = []
        for i, (straight, diagonal) in enumerate(crossed):
            send, stay = call(functools.partial(cross_body, i), (half, half), (straight, diagonal, mine), 0, "cross")
            mine = after(mine, send)
            sums += [stay, lax.ppermute(send, "seq", [(s, s ^ 2) for s in range(4)])]
        (weight_grad,) = call(final_body, (sds(block[::-1], F32),), tuple(sums), 0, "final", block[1] // DH)
    else:
        weight_grad = lax.psum_scatter(
            lax.dot_general(og, attn, TN, preferred_element_type=F32).astype(BF16),
            ("seq", "dp"),
            scatter_dimension=0,
            tiled=True,
        ).astype(F32)
    if paired:
        dkp = after(dkp, weight_grad)
    dk, dv = call(
        functools.partial(key_body, (nb, heads, second_owner), len(cparts)),
        (rows16, rows16),
        (lay, *cparts, k, kf, v, dkp, dvp),
        2 * unit,
        "key",
        2 * nb,
    )
    return attn_out[None], dq[None], dk[None], dv[None], weight_grad


def solution(mesh):
    rows = P(("groups", "dp"), "seq", "head")
    return jax.shard_map(
        per_device,
        mesh=mesh,
        in_specs=(rows, rows, rows, P("head", None, None), P(None, "head"), rows),
        out_specs=(rows, rows, rows, rows, P(("groups", "seq", "dp"), "head")),
        check_vma=False,
    )
```

```python
import functools

import jax
import jax.numpy as jnp
from jax import lax
from jax.experimental import pallas as pl
from jax.experimental.pallas import tpu as pltpu
from jax.sharding import PartitionSpec as P

DH = 128
BLK = 256
EPS = 1e-06
LIMIT = 16 << 20
BEGIN = 52 << 20
FAR = 4
SHORT = pl.CostEstimate(flops=1, bytes_accessed=1, transcendentals=0)
LONG = pl.CostEstimate(flops=10**11, bytes_accessed=1, transcendentals=0)
F32 = jnp.float32
BF16 = jnp.bfloat16
VM = pl.BlockSpec(memory_space=pltpu.VMEM)
SM = pl.BlockSpec(memory_space=pltpu.SMEM)
TN = (((0,), (0,)), ((), ()))
NT = (((1,), (1,)), ((), ()))
NN = (((1,), (0,)), ((), ()))


def sds(shape, dtype):
    return jax.ShapeDtypeStruct(shape, dtype)


def mm(a, b, dims):
    return lax.dot_general(a, b, dims, preferred_element_type=F32)


def feature(x):
    return jnp.where(x > 0, x + 1.0, jnp.exp(jnp.minimum(x, 0.0)))


def slope(x):
    return jnp.where(x > 0, 1.0, jnp.exp(jnp.minimum(x, 0.0)))


def streamed(outs, streams):
    if not streams:
        return []
    return [pltpu.VMEM(o.shape, o.dtype) for o in outs] + [pltpu.SemaphoreType.DMA((streams,))]


def call(body, outs, ins, flops, name, streams=0):
    read = sum(a.size * a.dtype.itemsize for a in ins)
    wrote = sum(s.size * s.dtype.itemsize for s in outs)
    return pl.pallas_call(
        body,
        out_shape=outs,
        in_specs=[SM if a.dtype == jnp.int32 else VM for a in ins],
        out_specs=[pl.BlockSpec(memory_space=pl.ANY) if streams else VM] * len(outs),
        scratch_shapes=streamed(outs, streams),
        name=name,
        compiler_params=pltpu.CompilerParams(vmem_limit_bytes=LIMIT),
        cost_estimate=LONG if name in ("query", "dnum") else SHORT,
    )(*ins)


def tiles(tokens, heads):
    for n in range(tokens // BLK):
        for h in range(heads):
            yield n * heads + h, slice(n * BLK, (n + 1) * BLK), slice(h * DH, (h + 1) * DH)


def mat(i):
    return slice(i * DH, (i + 1) * DH)


def states_body(k_ref, v_ref, kf_ref, st_ref):
    for i, r, c in tiles(k_ref.shape[0], k_ref.shape[1] // DH):
        kf = feature(k_ref[r, c].astype(F32)).astype(BF16)
        kf_ref[r, c] = kf
        st_ref[mat(i), :] = mm(kf, v_ref[r, c], TN).astype(BF16)


def far_body(w_ref, far_ref, sems):
    width, cols = far_ref.shape
    first = (1 - lax.axis_index("head")) * width
    lanes = pl.ds(pl.multiple_of(lax.axis_index("dp") * cols, cols), cols)
    copies = []
    for i in range(FAR):
        size = width // FAR
        rows = pl.ds(pl.multiple_of(first + i * size, size), size)
        into = far_ref.at[i * size : (i + 1) * size]
        copies.append(pltpu.make_async_copy(w_ref.at[rows, lanes], into, sems.at[i]))
    for copy in copies:
        copy.start()
    for copy in copies:
        copy.wait()


def far_rows(w, width):
    return pl.pallas_call(
        far_body,
        out_shape=sds((width, DH), BF16),
        in_specs=[pl.BlockSpec(memory_space=pl.ANY)],
        out_specs=VM,
        scratch_shapes=[pltpu.SemaphoreType.DMA((FAR,))],
        name="far",
        compiler_params=pltpu.CompilerParams(vmem_limit_bytes=BEGIN),
        cost_estimate=SHORT,
    )(w)


def begin_body(k_ref, v_ref, kf_ref, st_ref, k_in, v_in, sems):
    k_copy = pltpu.make_async_copy(k_ref, k_in, sems.at[0])
    v_copy = pltpu.make_async_copy(v_ref, v_in, sems.at[1])
    k_copy.start()
    v_copy.start()
    k_copy.wait()
    v_copy.wait()
    states_body(k_in, v_in, kf_ref, st_ref)


def begin(k, v):
    tokens, cols = k.shape
    count = tokens // BLK * (cols // DH)
    hbm = pl.BlockSpec(memory_space=pl.ANY)
    return pl.pallas_call(
        begin_body,
        out_shape=(sds((tokens, cols), BF16), sds((count * DH, DH), BF16)),
        in_specs=[hbm, hbm],
        out_specs=[VM, VM],
        scratch_shapes=[
            pltpu.VMEM((tokens, cols), BF16),
            pltpu.VMEM((tokens, cols), BF16),
            pltpu.SemaphoreType.DMA((2,)),
        ],
        name="begin",
        compiler_params=pltpu.CompilerParams(vmem_limit_bytes=BEGIN),
        cost_estimate=SHORT,
    )(k, v)


def split_body(x_ref, *outs):
    at = 0
    for out in outs:
        out[...] = x_ref[at : at + out.shape[0], :]
        at += out.shape[0]


def causal():
    rows = lax.broadcasted_iota(jnp.int32, (BLK, BLK), 0)
    cols = lax.broadcasted_iota(jnp.int32, (BLK, BLK), 1)
    return rows >= cols


def scores_body(q_ref, kf_ref, v_ref, qf_ref, sc_ref, intra_ref):
    keep = causal()
    for i, r, c in tiles(q_ref.shape[0], q_ref.shape[1] // DH):
        qf = feature(q_ref[r, c].astype(F32)).astype(BF16)
        qf_ref[r, c] = qf
        sc = jnp.where(keep, mm(qf, kf_ref[r, c], NT), 0.0).astype(BF16)
        sc_ref[i * BLK : (i + 1) * BLK, :] = sc
        intra_ref[r, c] = mm(sc, v_ref[r, c], NN)


def count(lay_ref, h, i, b):
    total = jnp.int32(0)
    for j in range(lay_ref.shape[1]):
        total = total + jnp.where(lay_ref[h, j, i] == b, 1, 0)
    return total.astype(F32)


def in_order(z, s):
    return s


def by_shift(z, s):
    size = lax.axis_size("seq")
    return lax.rem(z + size - s, size)


def by_flip(z, s):
    return lax.bitwise_xor(z, jnp.int32((0, 2, 1, 3)[s]))


def views(parts, rows):
    return [p.at[i * rows : (i + 1) * rows] for p in parts for i in range(p.shape[0] // rows)]


def numer_body(dims, np_, *refs):
    nb, heads, owner_of = dims
    lay_ref, *parts = refs[: 1 + np_]
    qf_ref, intra_ref, carried_ref, num_ref, attn_ref = refs[1 + np_ :]
    z = lax.axis_index("seq")
    for i, r, c in tiles(qf_ref.shape[0], heads):
        n, h = divmod(i, heads)
        query_block = z * nb + n
        total = jnp.zeros((DH, DH), F32)
        for s, part in enumerate(views(parts, nb * heads * DH)):
            for b in range(nb):
                times = count(lay_ref, h, query_block, owner_of(z, s) * nb + b)
                total = total + times * part[mat(b * heads + h), :].astype(F32)
        carried = total.astype(BF16)
        carried_ref[mat(i), :] = carried
        num = mm(qf_ref[r, c], carried, NN) + intra_ref[r, c]
        num_ref[r, c] = num
        rinv = lax.rsqrt(jnp.mean(num * num, axis=-1, keepdims=True) + EPS)
        attn_ref[r, c] = (num * rinv).astype(BF16)


def dnum_body(n_d, *refs):
    d_refs = refs[:n_d]
    num_ref, qf_ref, dnum_ref, cg_ref = refs[n_d:]
    heads = num_ref.shape[1] // DH
    for i, r, c in tiles(num_ref.shape[0], num_ref.shape[1] // DH):
        num = num_ref[r, c]
        grad = d_refs[0][r, c].astype(F32)
        if n_d == 3:
            same, sib = d_refs[1][r, :].astype(F32), d_refs[2][r, :].astype(F32)
            grad = grad + jnp.where(lax.axis_index("dp") == i % heads, same, sib)
        grad = grad.astype(BF16).astype(F32)
        rinv = lax.rsqrt(jnp.mean(num * num, axis=-1, keepdims=True) + EPS)
        lean = jnp.mean(grad * num, axis=-1, keepdims=True)
        dnum = (rinv * grad - num * (rinv * rinv * rinv * lean)).astype(BF16)
        dnum_ref[r, c] = dnum
        cg_ref[mat(i), :] = mm(qf_ref[r, c], dnum, TN).astype(BF16)


def query_body(q_ref, qf_ref, kf_ref, v_ref, dnum_ref, carried_ref, sc_ref, attn_ref, *outs):
    dq_ref, dk_ref, dv_ref, attn_out_ref = outs
    attn_out_ref[...] = attn_ref[...]
    keep = causal()
    for i, r, c in tiles(q_ref.shape[0], q_ref.shape[1] // DH):
        dnum = dnum_ref[r, c]
        pg = jnp.where(keep, mm(dnum, v_ref[r, c], NT), 0.0).astype(BF16)
        dq = mm(dnum, carried_ref[mat(i), :], NT) + mm(pg, kf_ref[r, c], NN)
        dq_ref[r, c] = (dq * slope(q_ref[r, c].astype(F32))).astype(BF16)
        dk_ref[r, c] = mm(pg, qf_ref[r, c], TN)
        dv_ref[r, c] = mm(sc_ref[i * BLK : (i + 1) * BLK, :], dnum, TN)


def key_body(dims, np_, *refs):
    nb, heads, owner_of = dims
    lay_ref, *parts = refs[: 1 + np_]
    k_ref, kf_ref, v_ref, dkp_ref, dvp_ref, dk_out, dv_out, dk_ref, dv_ref, sems = refs[1 + np_ :]
    copies = []
    z = lax.axis_index("seq")
    for i, r, c in tiles(k_ref.shape[0], heads):
        n, h = divmod(i, heads)
        key_block = z * nb + n
        total = jnp.zeros((DH, DH), F32)
        for s, part in enumerate(views(parts, nb * heads * DH)):
            for b in range(nb):
                times = count(lay_ref, h, owner_of(z, s) * nb + b, key_block)
                total = total + times * part[mat(b * heads + h), :].astype(F32)
        sg = total.astype(BF16)
        dk = mm(v_ref[r, c], sg, NT) + dkp_ref[r, c]
        dk_ref[r, c] = (dk * slope(k_ref[r, c].astype(F32))).astype(BF16)
        dv_ref[r, c] = (mm(kf_ref[r, c], sg, NN) + dvp_ref[r, c]).astype(BF16)
        if h == heads - 1:
            for at, (ref, out) in enumerate(((dk_ref, dk_out), (dv_ref, dv_out))):
                copies.append(pltpu.make_async_copy(ref.at[r, :], out.at[r, :], sems.at[2 * n + at]))
                copies[-1].start()
    for copy in copies:
        copy.wait()


def own_body(og_ref, w_ref, out_ref, w_in, sem):
    width = w_in.shape[0]
    rows = pl.ds(pl.multiple_of(lax.axis_index("head") * width, width), width)
    copy = pltpu.make_async_copy(w_ref.at[rows, :], w_in, sem)
    copy.start()
    copy.wait()
    out_ref[...] = mm(og_ref[...], w_in[...], NN)


def own_partial(og, w):
    tokens, width = og.shape
    cols = w.shape[1]
    return pl.pallas_call(
        own_body,
        out_shape=sds((tokens, cols), F32),
        in_specs=[VM, pl.BlockSpec(memory_space=pl.ANY)],
        out_specs=VM,
        scratch_shapes=[pltpu.VMEM((width, cols), BF16), pltpu.SemaphoreType.DMA],
        name="own_partial",
        compiler_params=pltpu.CompilerParams(vmem_limit_bytes=LIMIT),
        cost_estimate=SHORT,
    )(og, w)


def other_body(og_ref, og_sib_ref, w_ref, same_ref, sib_ref):
    same_ref[...] = mm(og_ref[...], w_ref[...], NN).astype(BF16)
    sib_ref[...] = mm(og_sib_ref[...], w_ref[...], NN).astype(BF16)


def weight_body(cols, attn_ref, og_ref, og_sib_ref, *refs):
    sibs, outs = refs[:-2], refs[-2:]
    rows = outs[0].shape[1]
    parity, core = lax.rem(lax.axis_index("seq"), 2), lax.axis_index("dp")
    for which, pair in enumerate((1 - parity, parity)):
        at = pl.ds(pl.multiple_of((2 * pair + core) * rows, rows), rows)
        total = mm(attn_ref[:, cols], og_ref[:, at], TN)
        row = 0
        for sib in sibs:
            total = total + mm(sib[:, cols], og_sib_ref[row : row + sib.shape[0], at], TN)
            row += sib.shape[0]
        outs[which][...] = total.astype(outs[which].dtype)


def pair_body(keep_ref, got_ref, cg_ref, two_ref, out_ref, joined_ref):
    out_ref[...] = (keep_ref[...] + got_ref[...].astype(F32)).astype(BF16)
    rows = cg_ref.shape[0]
    joined_ref[:rows, :] = cg_ref[...]
    joined_ref[rows:, :] = two_ref[...]


def cross_body(i, keep_ref, got_ref, mine_ref, send_ref, stay_ref):
    home = lax.axis_index("seq") // 2 == lax.axis_index("head")
    cross = (keep_ref[...].astype(F32) + got_ref[...].astype(F32)).astype(BF16)
    mine = mine_ref[mat(i), :]
    send_ref[...] = jnp.where(home, cross, mine)
    stay_ref[...] = jnp.where(home, mine, cross)


def final_body(*refs):
    *got, out_ref, total_ref, sems = refs
    copies = []
    for j in range(total_ref.shape[0] // DH):
        for i in range(len(got) // 2):
            total = got[2 * i][:, mat(j)].astype(F32) + got[2 * i + 1][:, mat(j)].astype(F32)
            total_ref[mat(j), mat(i)] = total.T
        copies.append(pltpu.make_async_copy(total_ref.at[mat(j), :], out_ref.at[mat(j), :], sems.at[j]))
        copies[-1].start()
    for copy in copies:
        copy.wait()


def after(x, *deps):
    return lax.optimization_barrier((x, *deps))[0]


def swap(x, axis):
    return lax.ppermute(x, axis, [(0, 1), (1, 0)])


def gather_parts(x, size):
    if size > 4:
        return [lax.all_gather(x, "seq", axis=0, tiled=True)]
    parts = [x]
    for shift in range(1, size):
        pairs = [(i, (i + shift) % size) for i in range(size)]
        parts.append(lax.ppermute(x, "seq", pairs))
    return parts


def per_device(queries, key_rows, value_rows, layout, out_weight, out_grad):
    seq_size = lax.axis_size("seq")
    head_size = lax.axis_size("head")
    dp_size = lax.axis_size("dp")
    heads = layout.shape[0]
    q, k, v, og = queries[0], key_rows[0], value_rows[0], out_grad[0]
    tokens, cols = q.shape
    nb = tokens // BLK
    paired = seq_size == 4 and head_size == 2 and dp_size == 2
    lay = layout.transpose(0, 2, 1)
    first_owner = in_order if seq_size > 4 else by_shift
    flat = sds((tokens, cols), F32)
    rows16 = sds((tokens, cols), BF16)
    mats = sds((nb * heads * DH, DH), BF16)
    unit = 2 * tokens * cols * DH

    if paired:
        width = og.shape[1]
        far = far_rows(out_weight, width)
        w_other = swap(far, "head")
        kf, st = begin(after(k, far), v)
        og_sib = swap(og, "dp")
    else:
        kf, st = call(states_body, (rows16, mats), (k, v), unit, "states")
    parts = gather_parts(st, seq_size)
    qf, sc, intra = call(
        scores_body,
        (rows16, sds((nb * heads * BLK, BLK), BF16), flat),
        (q, kf, v),
        4 * unit,
        "scores",
    )
    if not paired:
        og = lax.all_gather(og, "head", axis=1, tiled=True)
        d_own = jnp.dot(og, out_weight, preferred_element_type=F32)
    if paired:
        column = sds((tokens, DH), BF16)
        d_same, d_sib = call(other_body, (column, column), (after(og, qf), og_sib, w_other), 0, "other")
        across = [(h * 2 + c, (1 - h) * 2 + 1 - c) for h in range(2) for c in range(2)]
        intra = after(intra, d_sib)
        d_same = swap(d_same, "head")
        d_sib = lax.ppermute(d_sib, ("head", "dp"), across)
    carried, num, attn = call(
        functools.partial(numer_body, (nb, heads, first_owner), len(parts)),
        (mats, flat, rows16),
        (lay, *parts, qf, intra),
        unit,
        "numer",
    )
    if paired:
        attn_other = swap(attn, "head")
        attn_sib = swap(attn, "dp")
        d_own = own_partial(after(og, attn), out_weight)
        d_parts = (d_own, d_same, d_sib)
    else:
        d_parts = (d_own,)
    dnum, cg = call(
        functools.partial(dnum_body, len(d_parts)),
        (rows16, mats),
        (*d_parts, num, qf),
        unit,
        "dnum",
    )
    if paired:
        neighbours = [(0, 1), (1, 0), (2, 3), (3, 2)]
        two = lax.ppermute(cg, "seq", [(i, i ^ 2) for i in range(4)])
        block, half = (cols, width // 4), sds((DH, width // 4), BF16)
        give, keep = call(
            functools.partial(weight_body, slice(None)),
            (sds(block, BF16), sds(block, F32)),
            (after(attn, cg), og, og_sib, attn_sib),
            0,
            "weight",
        )
        got = lax.ppermute(give, "seq", neighbours)
        attn_other = after(attn_other, give)
        third = tokens // 48 * 16
        sizes = (third, third, tokens - 2 * third)
        cuts = call(split_body, tuple(sds((n, cols), BF16) for n in sizes), (attn_other,), 0, "split")
        cuts = [swap(cut, "dp") for cut in cuts]
        beside = [((s ^ 1) * 2 + 1 - h, s * 2 + h) for s in range(4) for h in range(2)]

        def cross_piece(i, *deps):
            give, keep = call(
                functools.partial(weight_body, mat(i)),
                (half, half),
                (after(attn_other, *deps), og, og_sib, *cuts),
                0,
                "weight",
            )
            return give, (swap(keep, "head"), lax.ppermute(give, ("seq", "head"), beside))

        give_b, first_crossed = cross_piece(0)
        mine, joined = call(
            pair_body,
            (sds(block, BF16), sds((2 * cg.shape[0], DH), BF16)),
            (keep, got, cg, two),
            0,
            "pair",
        )
        crossed = [first_crossed]
        for i in range(1, heads):
            give_b, piece = cross_piece(i, mine)
            crossed.append(piece)
        cparts = [cg, two, lax.ppermute(joined, "seq", neighbours)]
        second_owner = by_flip
    else:
        cparts, second_owner = gather_parts(cg, seq_size), first_owner
    dq, dkp, dvp, attn_out = call(
        query_body,
        (rows16, flat, flat, rows16),
        (q, qf, kf, v, dnum, carried, sc, attn),
        9 * unit,
        "query",
    )
    if paired:
        sums = []
        for i, (straight, diagonal) in enumerate(crossed):
            send, stay = call(functools.partial(cross_body, i), (half, half), (straight, diagonal, mine), 0, "cross")
            mine = after(mine, send)
            sums += [stay, lax.ppermute(send, "seq", [(s, s ^ 2) for s in range(4)])]
        (weight_grad,) = call(final_body, (sds(block[::-1], F32),), tuple(sums), 0, "final", block[1] // DH)
    else:
        weight_grad = lax.psum_scatter(
            lax.dot_general(og, attn, TN, preferred_element_type=F32).astype(BF16),
            ("seq", "dp"),
            scatter_dimension=0,
            tiled=True,
        ).astype(F32)
    if paired:
        dkp = after(dkp, weight_grad)
    dk, dv = call(
        functools.partial(key_body, (nb, heads, second_owner), len(cparts)),
        (rows16, rows16),
        (lay, *cparts, k, kf, v, dkp, dvp),
        2 * unit,
        "key",
        2 * nb,
    )
    return attn_out[None], dq[None], dk[None], dv[None], weight_grad


def solution(mesh):
    rows = P(("groups", "dp"), "seq", "head")
    return jax.shard_map(
        per_device,
        mesh=mesh,
        in_specs=(rows, rows, rows, P("head", None, None), P(None, "head"), rows),
        out_specs=(rows, rows, rows, rows, P(("groups", "seq", "dp"), "head")),
        check_vma=False,
    )
```

```python
import functools

import jax
import jax.numpy as jnp
from jax import lax
from jax.experimental import pallas as pl
from jax.experimental.pallas import tpu as pltpu
from jax.sharding import PartitionSpec as P

DH = 128
BLK = 256
EPS = 1e-06
LIMIT = 10 << 20
BEGIN = 52 << 20
FAR = 4
SHORT = pl.CostEstimate(flops=1, bytes_accessed=1, transcendentals=0)
LONG = pl.CostEstimate(flops=10**11, bytes_accessed=1, transcendentals=0)
F32 = jnp.float32
BF16 = jnp.bfloat16
VM = pl.BlockSpec(memory_space=pltpu.VMEM)
SM = pl.BlockSpec(memory_space=pltpu.SMEM)
TN = (((0,), (0,)), ((), ()))
NT = (((1,), (1,)), ((), ()))
NN = (((1,), (0,)), ((), ()))


def sds(shape, dtype):
    return jax.ShapeDtypeStruct(shape, dtype)


def mm(a, b, dims):
    return lax.dot_general(a, b, dims, preferred_element_type=F32)


def feature(x):
    return jnp.where(x > 0, x + 1.0, jnp.exp(jnp.minimum(x, 0.0)))


def slope(x):
    return jnp.where(x > 0, 1.0, jnp.exp(jnp.minimum(x, 0.0)))


def streamed(outs, streams):
    if not streams:
        return []
    return [pltpu.VMEM(o.shape, o.dtype) for o in outs] + [pltpu.SemaphoreType.DMA((streams,))]


def call(body, outs, ins, flops, name, streams=0):
    read = sum(a.size * a.dtype.itemsize for a in ins)
    wrote = sum(s.size * s.dtype.itemsize for s in outs)
    return pl.pallas_call(
        body,
        out_shape=outs,
        in_specs=[SM if a.dtype == jnp.int32 else VM for a in ins],
        out_specs=[pl.BlockSpec(memory_space=pl.ANY) if streams else VM] * len(outs),
        scratch_shapes=streamed(outs, streams),
        name=name,
        compiler_params=pltpu.CompilerParams(vmem_limit_bytes=LIMIT),
        cost_estimate=LONG if name in ("query", "dnum") else SHORT,
    )(*ins)


def tiles(tokens, heads):
    for n in range(tokens // BLK):
        for h in range(heads):
            yield n * heads + h, slice(n * BLK, (n + 1) * BLK), slice(h * DH, (h + 1) * DH)


def mat(i):
    return slice(i * DH, (i + 1) * DH)


def states_body(k_ref, v_ref, kf_ref, st_ref):
    for i, r, c in tiles(k_ref.shape[0], k_ref.shape[1] // DH):
        kf = feature(k_ref[r, c].astype(F32)).astype(BF16)
        kf_ref[r, c] = kf
        st_ref[mat(i), :] = mm(kf, v_ref[r, c], TN).astype(BF16)


def far_body(w_ref, far_ref, sems):
    width, cols = far_ref.shape
    first = (1 - lax.axis_index("head")) * width
    lanes = pl.ds(pl.multiple_of(lax.axis_index("dp") * cols, cols), cols)
    copies = []
    for i in range(FAR):
        size = width // FAR
        rows = pl.ds(pl.multiple_of(first + i * size, size), size)
        into = far_ref.at[i * size : (i + 1) * size]
        copies.append(pltpu.make_async_copy(w_ref.at[rows, lanes], into, sems.at[i]))
    for copy in copies:
        copy.start()
    for copy in copies:
        copy.wait()


def far_rows(w, width):
    return pl.pallas_call(
        far_body,
        out_shape=sds((width, DH), BF16),
        in_specs=[pl.BlockSpec(memory_space=pl.ANY)],
        out_specs=VM,
        scratch_shapes=[pltpu.SemaphoreType.DMA((FAR,))],
        name="far",
        compiler_params=pltpu.CompilerParams(vmem_limit_bytes=BEGIN),
        cost_estimate=SHORT,
    )(w)


def begin_body(k_ref, v_ref, kf_ref, st_ref, k_in, v_in, sems):
    k_copy = pltpu.make_async_copy(k_ref, k_in, sems.at[0])
    v_copy = pltpu.make_async_copy(v_ref, v_in, sems.at[1])
    k_copy.start()
    v_copy.start()
    k_copy.wait()
    v_copy.wait()
    states_body(k_in, v_in, kf_ref, st_ref)


def begin(k, v):
    tokens, cols = k.shape
    count = tokens // BLK * (cols // DH)
    hbm = pl.BlockSpec(memory_space=pl.ANY)
    return pl.pallas_call(
        begin_body,
        out_shape=(sds((tokens, cols), BF16), sds((count * DH, DH), BF16)),
        in_specs=[hbm, hbm],
        out_specs=[VM, VM],
        scratch_shapes=[
            pltpu.VMEM((tokens, cols), BF16),
            pltpu.VMEM((tokens, cols), BF16),
            pltpu.SemaphoreType.DMA((2,)),
        ],
        name="begin",
        compiler_params=pltpu.CompilerParams(vmem_limit_bytes=BEGIN),
        cost_estimate=SHORT,
    )(k, v)


def split_body(x_ref, *outs):
    at = 0
    for out in outs:
        out[...] = x_ref[at : at + out.shape[0], :]
        at += out.shape[0]


def causal():
    rows = lax.broadcasted_iota(jnp.int32, (BLK, BLK), 0)
    cols = lax.broadcasted_iota(jnp.int32, (BLK, BLK), 1)
    return rows >= cols


def scores_body(q_ref, kf_ref, v_ref, qf_ref, sc_ref, intra_ref):
    keep = causal()
    for i, r, c in tiles(q_ref.shape[0], q_ref.shape[1] // DH):
        qf = feature(q_ref[r, c].astype(F32)).astype(BF16)
        qf_ref[r, c] = qf
        sc = jnp.where(keep, mm(qf, kf_ref[r, c], NT), 0.0).astype(BF16)
        sc_ref[i * BLK : (i + 1) * BLK, :] = sc
        intra_ref[r, c] = mm(sc, v_ref[r, c], NN)


def count(lay_ref, h, i, b):
    total = jnp.int32(0)
    for j in range(lay_ref.shape[1]):
        total = total + jnp.where(lay_ref[h, j, i] == b, 1, 0)
    return total.astype(F32)


def in_order(z, s):
    return s


def by_shift(z, s):
    size = lax.axis_size("seq")
    return lax.rem(z + size - s, size)


def by_flip(z, s):
    return lax.bitwise_xor(z, jnp.int32((0, 2, 1, 3)[s]))


def views(parts, rows):
    return [p.at[i * rows : (i + 1) * rows] for p in parts for i in range(p.shape[0] // rows)]


def numer_body(dims, np_, *refs):
    nb, heads, owner_of = dims
    lay_ref, *parts = refs[: 1 + np_]
    qf_ref, intra_ref, carried_ref, num_ref, attn_ref = refs[1 + np_ :]
    z = lax.axis_index("seq")
    for i, r, c in tiles(qf_ref.shape[0], heads):
        n, h = divmod(i, heads)
        query_block = z * nb + n
        total = jnp.zeros((DH, DH), F32)
        for s, part in enumerate(views(parts, nb * heads * DH)):
            for b in range(nb):
                times = count(lay_ref, h, query_block, owner_of(z, s) * nb + b)
                total = total + times * part[mat(b * heads + h), :].astype(F32)
        carried = total.astype(BF16)
        carried_ref[mat(i), :] = carried
        num = mm(qf_ref[r, c], carried, NN) + intra_ref[r, c]
        num_ref[r, c] = num
        rinv = lax.rsqrt(jnp.mean(num * num, axis=-1, keepdims=True) + EPS)
        attn_ref[r, c] = (num * rinv).astype(BF16)


def dnum_body(n_d, *refs):
    d_refs = refs[:n_d]
    num_ref, qf_ref, dnum_ref, cg_ref = refs[n_d:]
    heads = num_ref.shape[1] // DH
    for i, r, c in tiles(num_ref.shape[0], num_ref.shape[1] // DH):
        num = num_ref[r, c]
        grad = d_refs[0][r, c].astype(F32)
        if n_d == 3:
            same, sib = d_refs[1][r, :].astype(F32), d_refs[2][r, :].astype(F32)
            grad = grad + jnp.where(lax.axis_index("dp") == i % heads, same, sib)
        grad = grad.astype(BF16).astype(F32)
        rinv = lax.rsqrt(jnp.mean(num * num, axis=-1, keepdims=True) + EPS)
        lean = jnp.mean(grad * num, axis=-1, keepdims=True)
        dnum = (rinv * grad - num * (rinv * rinv * rinv * lean)).astype(BF16)
        dnum_ref[r, c] = dnum
        cg_ref[mat(i), :] = mm(qf_ref[r, c], dnum, TN).astype(BF16)


def query_body(q_ref, qf_ref, kf_ref, v_ref, dnum_ref, carried_ref, sc_ref, attn_ref, *outs):
    dq_ref, dk_ref, dv_ref, attn_out_ref = outs
    attn_out_ref[...] = attn_ref[...]
    keep = causal()
    for i, r, c in tiles(q_ref.shape[0], q_ref.shape[1] // DH):
        dnum = dnum_ref[r, c]
        pg = jnp.where(keep, mm(dnum, v_ref[r, c], NT), 0.0).astype(BF16)
        dq = mm(dnum, carried_ref[mat(i), :], NT) + mm(pg, kf_ref[r, c], NN)
        dq_ref[r, c] = (dq * slope(q_ref[r, c].astype(F32))).astype(BF16)
        dk_ref[r, c] = mm(pg, qf_ref[r, c], TN)
        dv_ref[r, c] = mm(sc_ref[i * BLK : (i + 1) * BLK, :], dnum, TN)


def key_body(dims, np_, *refs):
    nb, heads, owner_of = dims
    lay_ref, *parts = refs[: 1 + np_]
    k_ref, kf_ref, v_ref, dkp_ref, dvp_ref, dk_out, dv_out, dk_ref, dv_ref, sems = refs[1 + np_ :]
    copies = []
    z = lax.axis_index("seq")
    for i, r, c in tiles(k_ref.shape[0], heads):
        n, h = divmod(i, heads)
        key_block = z * nb + n
        total = jnp.zeros((DH, DH), F32)
        for s, part in enumerate(views(parts, nb * heads * DH)):
            for b in range(nb):
                times = count(lay_ref, h, owner_of(z, s) * nb + b, key_block)
                total = total + times * part[mat(b * heads + h), :].astype(F32)
        sg = total.astype(BF16)
        dk = mm(v_ref[r, c], sg, NT) + dkp_ref[r, c]
        dk_ref[r, c] = (dk * slope(k_ref[r, c].astype(F32))).astype(BF16)
        dv_ref[r, c] = (mm(kf_ref[r, c], sg, NN) + dvp_ref[r, c]).astype(BF16)
        if h == heads - 1:
            for at, (ref, out) in enumerate(((dk_ref, dk_out), (dv_ref, dv_out))):
                copies.append(pltpu.make_async_copy(ref.at[r, :], out.at[r, :], sems.at[2 * n + at]))
                copies[-1].start()
    for copy in copies:
        copy.wait()


def own_body(og_ref, w_ref, out_ref, w_in, sem):
    width = w_in.shape[0]
    rows = pl.ds(pl.multiple_of(lax.axis_index("head") * width, width), width)
    copy = pltpu.make_async_copy(w_ref.at[rows, :], w_in, sem)
    copy.start()
    copy.wait()
    out_ref[...] = mm(og_ref[...], w_in[...], NN)


def own_partial(og, w):
    tokens, width = og.shape
    cols = w.shape[1]
    return pl.pallas_call(
        own_body,
        out_shape=sds((tokens, cols), F32),
        in_specs=[VM, pl.BlockSpec(memory_space=pl.ANY)],
        out_specs=VM,
        scratch_shapes=[pltpu.VMEM((width, cols), BF16), pltpu.SemaphoreType.DMA],
        name="own_partial",
        compiler_params=pltpu.CompilerParams(vmem_limit_bytes=LIMIT),
        cost_estimate=SHORT,
    )(og, w)


def other_body(og_ref, og_sib_ref, w_ref, same_ref, sib_ref):
    same_ref[...] = mm(og_ref[...], w_ref[...], NN).astype(BF16)
    sib_ref[...] = mm(og_sib_ref[...], w_ref[...], NN).astype(BF16)


def weight_body(cols, attn_ref, og_ref, og_sib_ref, *refs):
    sibs, outs = refs[:-2], refs[-2:]
    rows = outs[0].shape[1]
    parity, core = lax.rem(lax.axis_index("seq"), 2), lax.axis_index("dp")
    for which, pair in enumerate((1 - parity, parity)):
        at = pl.ds(pl.multiple_of((2 * pair + core) * rows, rows), rows)
        total = mm(attn_ref[:, cols], og_ref[:, at], TN)
        row = 0
        for sib in sibs:
            total = total + mm(sib[:, cols], og_sib_ref[row : row + sib.shape[0], at], TN)
            row += sib.shape[0]
        outs[which][...] = total.astype(outs[which].dtype)


def pair_body(keep_ref, got_ref, cg_ref, two_ref, out_ref, joined_ref):
    out_ref[...] = (keep_ref[...] + got_ref[...].astype(F32)).astype(BF16)
    rows = cg_ref.shape[0]
    joined_ref[:rows, :] = cg_ref[...]
    joined_ref[rows:, :] = two_ref[...]


def cross_body(i, keep_ref, got_ref, mine_ref, send_ref, stay_ref):
    home = lax.axis_index("seq") // 2 == lax.axis_index("head")
    cross = (keep_ref[...].astype(F32) + got_ref[...].astype(F32)).astype(BF16)
    mine = mine_ref[mat(i), :]
    send_ref[...] = jnp.where(home, cross, mine)
    stay_ref[...] = jnp.where(home, mine, cross)


def final_body(*refs):
    *got, out_ref, total_ref, sems = refs
    copies = []
    for j in range(total_ref.shape[0] // DH):
        for i in range(len(got) // 2):
            total = got[2 * i][:, mat(j)].astype(F32) + got[2 * i + 1][:, mat(j)].astype(F32)
            total_ref[mat(j), mat(i)] = total.T
        copies.append(pltpu.make_async_copy(total_ref.at[mat(j), :], out_ref.at[mat(j), :], sems.at[j]))
        copies[-1].start()
    for copy in copies:
        copy.wait()


def after(x, *deps):
    return lax.optimization_barrier((x, *deps))[0]


def swap(x, axis):
    return lax.ppermute(x, axis, [(0, 1), (1, 0)])


def gather_parts(x, size):
    if size > 4:
        return [lax.all_gather(x, "seq", axis=0, tiled=True)]
    parts = [x]
    for shift in range(1, size):
        pairs = [(i, (i + shift) % size) for i in range(size)]
        parts.append(lax.ppermute(x, "seq", pairs))
    return parts


def per_device(queries, key_rows, value_rows, layout, out_weight, out_grad):
    seq_size = lax.axis_size("seq")
    head_size = lax.axis_size("head")
    dp_size = lax.axis_size("dp")
    heads = layout.shape[0]
    q, k, v, og = queries[0], key_rows[0], value_rows[0], out_grad[0]
    tokens, cols = q.shape
    nb = tokens // BLK
    paired = seq_size == 4 and head_size == 2 and dp_size == 2
    lay = layout.transpose(0, 2, 1)
    first_owner = in_order if seq_size > 4 else by_shift
    flat = sds((tokens, cols), F32)
    rows16 = sds((tokens, cols), BF16)
    mats = sds((nb * heads * DH, DH), BF16)
    unit = 2 * tokens * cols * DH

    if paired:
        width = og.shape[1]
        far = far_rows(out_weight, width)
        w_other = swap(far, "head")
        kf, st = begin(after(k, far), v)
        og_sib = swap(og, "dp")
    else:
        kf, st = call(states_body, (rows16, mats), (k, v), unit, "states")
    parts = gather_parts(st, seq_size)
    qf, sc, intra = call(
        scores_body,
        (rows16, sds((nb * heads * BLK, BLK), BF16), flat),
        (q, kf, v),
        4 * unit,
        "scores",
    )
    if not paired:
        og = lax.all_gather(og, "head", axis=1, tiled=True)
        d_own = jnp.dot(og, out_weight, preferred_element_type=F32)
    if paired:
        column = sds((tokens, DH), BF16)
        d_same, d_sib = call(other_body, (column, column), (after(og, qf), og_sib, w_other), 0, "other")
        across = [(h * 2 + c, (1 - h) * 2 + 1 - c) for h in range(2) for c in range(2)]
        intra = after(intra, d_sib)
        d_same = swap(d_same, "head")
        d_sib = lax.ppermute(d_sib, ("head", "dp"), across)
    carried, num, attn = call(
        functools.partial(numer_body, (nb, heads, first_owner), len(parts)),
        (mats, flat, rows16),
        (lay, *parts, qf, intra),
        unit,
        "numer",
    )
    if paired:
        attn_other = swap(attn, "head")
        attn_sib = swap(attn, "dp")
        d_own = own_partial(after(og, attn), out_weight)
        d_parts = (d_own, d_same, d_sib)
    else:
        d_parts = (d_own,)
    dnum, cg = call(
        functools.partial(dnum_body, len(d_parts)),
        (rows16, mats),
        (*d_parts, num, qf),
        unit,
        "dnum",
    )
    if paired:
        neighbours = [(0, 1), (1, 0), (2, 3), (3, 2)]
        two = lax.ppermute(cg, "seq", [(i, i ^ 2) for i in range(4)])
        block, half = (cols, width // 4), sds((DH, width // 4), BF16)
        give, keep = call(
            functools.partial(weight_body, slice(None)),
            (sds(block, BF16), sds(block, F32)),
            (after(attn, cg), og, og_sib, attn_sib),
            0,
            "weight",
        )
        got = lax.ppermute(give, "seq", neighbours)
        attn_other = after(attn_other, give)
        third = tokens // 48 * 16
        sizes = (third, third, tokens - 2 * third)
        cuts = call(split_body, tuple(sds((n, cols), BF16) for n in sizes), (attn_other,), 0, "split")
        cuts = [swap(cut, "dp") for cut in cuts]
        beside = [((s ^ 1) * 2 + 1 - h, s * 2 + h) for s in range(4) for h in range(2)]

        def cross_piece(i, *deps):
            give, keep = call(
                functools.partial(weight_body, mat(i)),
                (half, half),
                (after(attn_other, *deps), og, og_sib, *cuts),
                0,
                "weight",
            )
            return give, (swap(keep, "head"), lax.ppermute(give, ("seq", "head"), beside))

        give_b, first_crossed = cross_piece(0)
        mine, joined = call(
            pair_body,
            (sds(block, BF16), sds((2 * cg.shape[0], DH), BF16)),
            (keep, got, cg, two),
            0,
            "pair",
        )
        crossed = [first_crossed]
        for i in range(1, heads):
            give_b, piece = cross_piece(i, mine)
            crossed.append(piece)
        cparts = [cg, two, lax.ppermute(joined, "seq", neighbours)]
        second_owner = by_flip
    else:
        cparts, second_owner = gather_parts(cg, seq_size), first_owner
    dq, dkp, dvp, attn_out = call(
        query_body,
        (rows16, flat, flat, rows16),
        (q, qf, kf, v, dnum, carried, sc, attn),
        9 * unit,
        "query",
    )
    if paired:
        sums = []
        for i, (straight, diagonal) in enumerate(crossed):
            send, stay = call(functools.partial(cross_body, i), (half, half), (straight, diagonal, mine), 0, "cross")
            mine = after(mine, send)
            sums += [stay, lax.ppermute(send, "seq", [(s, s ^ 2) for s in range(4)])]
        (weight_grad,) = call(final_body, (sds(block[::-1], F32),), tuple(sums), 0, "final", block[1] // DH)
    else:
        weight_grad = lax.psum_scatter(
            lax.dot_general(og, attn, TN, preferred_element_type=F32).astype(BF16),
            ("seq", "dp"),
            scatter_dimension=0,
            tiled=True,
        ).astype(F32)
    if paired:
        dkp = after(dkp, weight_grad)
    dk, dv = call(
        functools.partial(key_body, (nb, heads, second_owner), len(cparts)),
        (rows16, rows16),
        (lay, *cparts, k, kf, v, dkp, dvp),
        2 * unit,
        "key",
        2 * nb,
    )
    return attn_out[None], dq[None], dk[None], dv[None], weight_grad


def solution(mesh):
    rows = P(("groups", "dp"), "seq", "head")
    return jax.shard_map(
        per_device,
        mesh=mesh,
        in_specs=(rows, rows, rows, P("head", None, None), P(None, "head"), rows),
        out_specs=(rows, rows, rows, rows, P(("groups", "seq", "dp"), "head")),
        check_vma=False,
    )
```
